256 devices in a mesh: tm: 16 (over z, x_lo), lon: 4 (over x_hi, core), lat: 4 (over y).
Axes of the slice: x: 4 (x_hi: 2, x_lo: 2; x = x_hi * 2 + x_lo), y: 4, z: 8, core: 2. Of those that a mesh axis runs over, the one named last changes fastest.
Arguments:
- iterate: float32 [16, 64, 64, 512], P('tm', None, 'lat', 'lon'), may hold values from -6 to 6
- heating: float32 [16, 64, 64, 512], P('tm', None, 'lat', 'lon'), may hold values from -6 to 6
- initial: float32 [64, 64, 512], P(None, 'lat', 'lon'), may hold values from -6 to 6
- region: int32 [64, 64, 512], P(None, 'lat', 'lon'), may hold values from 0 to 7
- cond_table: float32 [8], replicated, may hold values from 0.3 to 3
Outputs:
- updated: float32 [16, 64, 64, 512], P('tm', None, 'lat', 'lon')
The draws below stay inside these ranges and needn't reach their ends.
Inputs may be any that keep to these rules, and one draw needn't show every extreme that they name: `region`: class index of each cell.
All inputs are finite; a program needn't handle non-finite values.
Results may differ from the reference program's by a relative error of at most 0.0003.
Values sent between devices are 32-bit elements; how exact they have to be, the bound alone decides.
A program may use at most 128 MiB of HBM per device.

```python
import math
import jax
import jax.numpy as jnp
from jax import lax

LEV = 64
CLASSES = 8
SWEEPS = 4
STEPS = 16
NLAT = 64
NLON = 512


def set_ends(array, own_key, smallest, largest):
    place = [jax.random.randint(jax.random.fold_in(own_key, axis), (), 0, length) for axis, length in enumerate(array.shape)]
    main_axis = array.shape.index(max(array.shape))
    beside = place[:main_axis] + [(place[main_axis] + 1) % array.shape[main_axis]] + place[main_axis + 1:]
    return array.at[tuple(place)].set(smallest).at[tuple(beside)].set(largest)


def block_scale(key, extent, shards, smallest, top_value):
    gain = 1.0
    for position, blocks in shards:
        draws = jax.random.uniform(jax.random.fold_in(jax.random.fold_in(key, 6), position), (blocks,), jnp.float32, smallest / len(shards), top_value / len(shards))
        gain = gain * jnp.repeat(jnp.exp(draws), extent[position] // blocks).reshape((-1,) + (1,) * (len(extent) - 1 - position))
    return gain


def centred(own_key, dims, width, bound, shards=(), kind=jnp.bfloat16):
    array = jax.random.normal(own_key, dims, jnp.float32) * width
    if len(shards) > 0:
        array = block_scale(own_key, dims, shards, -0.22, 0.18) * array
    return jnp.clip(array, min=-bound, max=bound).astype(kind)


def setup_inputs(seed: int = 0) -> dict:
    seeds = jax.random.split(jax.random.key(seed), 6)
    iterate = centred(seeds[0], (STEPS, LEV, NLAT, NLON), 1.0, 6.0, ((0, 16), (2, 4), (3, 4)), jnp.float32)
    heating = centred(seeds[1], (STEPS, LEV, NLAT, NLON), 1.0, 6.0, ((0, 16), (2, 4), (3, 4)), jnp.float32)
    initial = centred(seeds[2], (LEV, NLAT, NLON), 1.0, 6.0, ((1, 4), (2, 4)), jnp.float32)
    region = set_ends(jax.random.randint(seeds[3], (LEV, NLAT, NLON), 0, CLASSES), jax.random.fold_in(seeds[3], 1), 0, CLASSES - 1).astype(jnp.int32)
    cond_table = jnp.clip(jnp.exp(jax.random.uniform(seeds[4], (CLASSES,), jnp.float32, math.log(0.3), math.log(3.0))), 0.3, 3.0)
    return {"iterate": iterate, "heating": heating, "initial": initial, "region": region, "cond_table": cond_table}


corner_weight = 0.1


def harmonic(first, second):
    return 2.0 * first * second / (first + second)


def conductivity(region, cond_table):
    classes = jnp.arange(cond_table.shape[0], dtype=jnp.int32)
    onehot = (region[..., None] == classes).astype(jnp.float32)
    return jnp.sum(onehot * cond_table.astype(jnp.float32), axis=-1)


def extend(field):
    lead = field.ndim - 3
    wrapped = jnp.concatenate([field[..., -1:], field, field[..., :1]], axis=-1)
    pads = [(0, 0)] * lead + [(1, 1), (1, 1), (0, 0)]
    return jnp.pad(wrapped, pads)


def face_weights(kext):
    centre = kext[1:-1, 1:-1, 1:-1]
    return (harmonic(centre, kext[:-2, 1:-1, 1:-1]), harmonic(centre, kext[2:, 1:-1, 1:-1]),
            harmonic(centre, kext[1:-1, :-2, 1:-1]), harmonic(centre, kext[1:-1, 2:, 1:-1]),
            harmonic(centre, kext[1:-1, 1:-1, :-2]), harmonic(centre, kext[1:-1, 1:-1, 2:]))


def neighbours(weights, ext):
    near = weights[0] * ext[..., :-2, 1:-1, 1:-1] + weights[1] * ext[..., 2:, 1:-1, 1:-1]
    near = near + weights[2] * ext[..., 1:-1, :-2, 1:-1] + weights[3] * ext[..., 1:-1, 2:, 1:-1]
    near = near + weights[4] * ext[..., 1:-1, 1:-1, :-2] + weights[5] * ext[..., 1:-1, 1:-1, 2:]
    return near


def reference(iterate, heating, initial, region, cond_table):
    steps = iterate.shape[0]
    weights = face_weights(extend(conductivity(region, cond_table)))
    total = weights[0] + weights[1] + weights[2] + weights[3] + weights[4] + weights[5]
    previous = jnp.concatenate([initial[None], iterate[:-1]], axis=0)
    residual = heating + previous - ((1.0 + total) * iterate - neighbours(weights, extend(iterate)))
    index = jnp.arange(steps, dtype=jnp.int32)
    scales = corner_weight ** (index.astype(jnp.float32) / steps)
    beta = corner_weight ** (1.0 / steps)
    scaled = residual * scales[:, None, None, None]
    angle = (2.0 * jnp.pi / steps) * ((index[:, None] * index[None, :]) % steps).astype(jnp.float32)
    cosine = jnp.cos(angle)
    sine = jnp.sin(angle)
    high = lax.Precision.HIGHEST
    spec_re = jnp.einsum("kn,nabc->kabc", cosine, scaled, precision=high)
    spec_im = -jnp.einsum("kn,nabc->kabc", sine, scaled, precision=high)
    shift_re = 1.0 - beta * cosine[:, 1]
    shift_im = beta * sine[:, 1]
    diag_re = shift_re[:, None, None, None] + total[None]
    diag_im = shift_im[:, None, None, None] + jnp.zeros_like(total)[None]
    denom = diag_re * diag_re + diag_im * diag_im
    inv_re = diag_re / denom
    inv_im = -diag_im / denom
    sol_re = spec_re * inv_re - spec_im * inv_im
    sol_im = spec_re * inv_im + spec_im * inv_re
    for sweep in range(SWEEPS - 1):
        rhs_re = spec_re + neighbours(weights, extend(sol_re))
        rhs_im = spec_im + neighbours(weights, extend(sol_im))
        sol_re = rhs_re * inv_re - rhs_im * inv_im
        sol_im = rhs_re * inv_im + rhs_im * inv_re
    back = (jnp.einsum("kn,kabc->nabc", cosine, sol_re, precision=high)
            - jnp.einsum("kn,kabc->nabc", sine, sol_im, precision=high)) / steps
    return iterate + back / scales[:, None, None, None]
```

```python
import functools
import math

import jax
import jax.numpy as jnp
from jax import lax
from jax.experimental import pallas as pl
from jax.experimental.pallas import tpu as pltpu
from jax.sharding import PartitionSpec as P

MESH = pl.DeviceIdType.MESH
F32 = jnp.float32
CORNER = 0.1
SWEEPS = 3
LP = 8
AP = 8
NA = 16
NX = 128


def harmonic(first, second):
    return 2.0 * first * second / (first + second)


def weighted(pairs):
    total = None
    for coefficient, value in pairs:
        if abs(coefficient) < 1e-12:
            continue
        if abs(coefficient - 1.0) < 1e-12:
            term = value
        elif abs(coefficient + 1.0) < 1e-12:
            total = -value if total is None else total - value
            continue
        else:
            term = value * coefficient
        total = term if total is None else total + term
    return total


def cosine_sums(e, n):
    half, quarter = n // 2, n // 4
    even = [e[m] + e[half - m] for m in range(quarter)]
    odd = [e[m] - e[half - m] for m in range(quarter)]
    out = []
    for k in range(half + 1):
        parts = even if k % 2 == 0 else odd
        pairs = [(math.cos(2 * math.pi * k * m / n), parts[m]) for m in range(quarter)]
        pairs.append((math.cos(2 * math.pi * k * quarter / n), e[quarter]))
        out.append(weighted(pairs))
    return out


def sine_sums(o, n):
    half, quarter = n // 2, n // 4
    plus = [o[m - 1] + o[half - m - 1] for m in range(1, quarter)]
    minus = [o[m - 1] - o[half - m - 1] for m in range(1, quarter)]
    out = []
    for k in range(1, half):
        parts = plus if k % 2 == 1 else minus
        pairs = [(math.sin(2 * math.pi * k * m / n), parts[m - 1]) for m in range(1, quarter)]
        pairs.append((math.sin(2 * math.pi * k * quarter / n), o[quarter - 1]))
        total = weighted(pairs)
        out.append(total if total is not None else jnp.zeros_like(o[0]))
    return out


def pick(index, values):
    chosen = jnp.float32(values[0])
    for i, value in enumerate(values):
        if i > 0:
            chosen = jnp.where(index == i, jnp.float32(value), chosen)
    return chosen


def kernel(
    steps, nlat, nlon,
    u_ref, h_ref, reg_ref, table_ref, init_ref, out_ref,
    kap, wts, pbuf, lat_out, lat_in, lon_out, lon_in,
    rs, rr, spec, coef, xe, xf, edge_out, edge_in, ws, wb,
    init_sem, shift_s, shift_r, side_s, side_r, fwd_s, fwd_r, halo_s, halo_r, back_s, back_r,
):
    levels = u_ref.shape[0] // NA
    zs = steps // 2
    half = steps // 2
    me = lax.axis_index("tm")
    lat = lax.axis_index("lat")
    lon = lax.axis_index("lon")
    z = lax.div(me, 2)
    xl = lax.rem(me, 2)
    q = lax.rem(xl + lat, 2)
    left = lax.rem(lon + nlon - 1, nlon)
    right = lax.rem(lon + 1, nlon)
    sub = lax.broadcasted_iota(jnp.int32, (8, NX), 0)
    lane = lax.broadcasted_iota(jnp.int32, (8, NX), 1)
    zero = jnp.zeros((8, NX), F32)

    def remote(src, dst, send, recv, device):
        return pltpu.make_async_remote_copy(
            src_ref=src, dst_ref=dst, send_sem=send, recv_sem=recv, device_id=device, device_id_type=MESH
        )

    sides = (
        (lat > 0, {"lat": lat - 1}),
        (lat < nlat - 1, {"lat": lat + 1}),
        (None, {"lon": left}),
        (None, {"lon": right}),
    )
    x_low = xl * (1 - q) + (1 - xl) * q
    x_high = xl * q + (1 - xl) * (1 - q)
    homes = (
        (z > 0, {"tm": me - 2}),
        (z < zs - 1, {"tm": me + 2}),
        (q + lat > 0, {"tm": z * 2 + x_low, "lat": lat - (1 - q)}),
        ((1 - q) + (nlat - 1 - lat) > 0, {"tm": z * 2 + x_high, "lat": lat + q}),
        (None, {"lon": left}),
        (None, {"lon": right}),
    )

    def guarded(condition, act):
        if condition is None:
            act()
        else:
            pl.when(condition)(act)

    barrier = pltpu.get_barrier_semaphore()
    for d in range(1, steps):
        pl.semaphore_signal(barrier, inc=1, device_id={"tm": lax.rem(me + d, steps)}, device_id_type=MESH)
    for condition, device in sides:
        guarded(
            condition,
            functools.partial(pl.semaphore_signal, barrier, inc=1, device_id=device, device_id_type=MESH),
        )
    first = pltpu.make_async_copy(init_ref, pbuf, init_sem)

    @pl.when(me == 0)
    def _():
        first.start()

    lat_count = jnp.where(lat > 0, 1, 0) + jnp.where(lat < nlat - 1, 1, 0)
    pl.semaphore_wait(barrier, steps - 1 + 2 + lat_count)

    rows = LP * NA

    def order(i, at):
        odd = lax.rem(i, 2)
        away = zs // 2 + (1 - odd) * lax.div(i, 2) - odd * lax.div(i + 1, 2)
        return lax.rem(at + away, zs)

    def shift_copy(i, at, to):
        part = pl.ds(pl.multiple_of(order(i, at) * rows, 8), rows)
        return remote(u_ref.at[part, :], pbuf.at[part, :], shift_s.at[i], shift_r.at[i], {"tm": to})

    later = lax.rem(me + 1, steps)
    later_z = lax.div(later, 2)

    @pl.when(me < steps - 1)
    def _():
        for i in range(zs):
            shift_copy(i, later_z, later).start()

    kap[pl.ds(0, NA), :] = jnp.zeros((NA, NX), F32)
    kap[pl.ds((levels + 1) * NA, NA), :] = jnp.zeros((NA, NX), F32)
    table = [table_ref[c] for c in range(8)]

    def conduct(g, packs):
        gathered = [zero] * 4
        for j in range(16):
            at = pl.multiple_of(g * 128, 8) + j * 8
            reg = reg_ref[pl.ds(at, 8), :]
            k = jnp.full((8, NX), table[0], F32)
            for c in range(1, 8):
                k = jnp.where(reg == c, table[c], k)
            kap[pl.ds(at + NA, 8), :] = k
            u = u_ref[pl.ds(at, 8), :]
            for f, tile in ((0, u), (1, k)):
                here = lane == j
                low = pltpu.roll(tile, j, 1) if j > 0 else tile
                gathered[f] = jnp.where(here, low, gathered[f])
                gathered[2 + f] = jnp.where(here, pltpu.roll(tile, j + 1, 1), gathered[2 + f])
        mask = lax.div(lane, 16) == g
        return tuple(
            jnp.where(mask, pltpu.roll(gathered[f], g * 16, 1), packs[f]) for f in range(4)
        )

    packs = lax.fori_loop(0, levels // 8, conduct, (zero,) * 4)
    for side in range(2):
        for f in range(2):
            lon_out[side, pl.ds(f * 8, 8), :] = packs[side * 2 + f]
    for g in range(levels // 8):
        for side, row in ((0, 0), (1, NA - 1)):
            lat_out[side, pl.ds(g * 8, 8), :] = u_ref[pl.ds(g * 128 + row, 8, stride=NA), :]
            lat_out[side, pl.ds(levels + g * 8, 8), :] = kap[pl.ds(NA + g * 128 + row, 8, stride=NA), :]

    def side_copy(d):
        if d < 2:
            return remote(lat_out.at[d], lat_in.at[1 - d], side_s.at[d], side_r.at[1 - d], sides[d][1])
        return remote(lon_out.at[d - 2], lon_in.at[3 - d], side_s.at[d], side_r.at[5 - d], sides[d][1])

    def side_arrival(d):
        if d < 2:
            return remote(lat_out.at[d], lat_in.at[d], side_s.at[d], side_r.at[d], sides[d][1])
        return remote(lon_out.at[d - 2], lon_in.at[d - 2], side_s.at[d], side_r.at[d], sides[d][1])

    for d in range(4):
        guarded(sides[d][0], lambda d=d: side_copy(d).start())

    @pl.when(lat == 0)
    def _():
        lat_in[0] = jnp.zeros(lat_in.shape[1:], F32)

    @pl.when(lat == nlat - 1)
    def _():
        lat_in[1] = jnp.zeros(lat_in.shape[1:], F32)

    for b in range(SWEEPS):
        for condition, place in (
            (z == 0, (b, 0, slice(None))),
            (z == zs - 1, (b, LP + 1, slice(None))),
            (q + lat == 0, (b, slice(None), 0)),
            ((1 - q) + (nlat - 1 - lat) == 0, (b, slice(None), AP + 1)),
        ):
            def clear(place=place):
                xe[place] = jnp.zeros((10, 16, NX), F32)

            pl.when(condition)(clear)

    for d in range(4):
        guarded(sides[d][0], lambda d=d: side_arrival(d).wait_recv())

    @pl.when(me == 0)
    def _():
        first.wait()

    gamma = [CORNER ** (n / steps) for n in range(steps)]
    scale = pick(me, gamma)
    u_sides = [lon_in[s, pl.ds(0, 8), :] for s in range(2)]
    k_sides = [lon_in[s, pl.ds(8, 8), :] for s in range(2)]

    def fwd_copy(part, zd, to):
        return remote(
            rs.at[part, pl.ds(pl.multiple_of(zd * 64, 8), 64), :], rr.at[me], fwd_s.at[to], fwd_r.at[me], {"tm": to}
        )

    def chunk(i, carry):
        zd = order(i, z)

        @pl.when(me > 0)
        def _():
            shift_copy(i, z, later).wait_recv()

        def level(l, carry):
            lev = zd * LP + l
            base = pl.multiple_of(lev * NA, 8)
            under = pl.multiple_of(jnp.maximum(lev - 1, 0) * NA, 8)
            over = pl.multiple_of(jnp.minimum(lev + 1, levels - 1) * NA, 8)
            fields = []
            for ref, low, mid, high, off, ends in (
                (u_ref, under, base, over, 0, u_sides),
                (kap, base, base + NA, base + 2 * NA, levels, k_sides),
            ):
                tile = [ref[pl.ds(mid + 8 * t, 8), :] for t in range(2)]
                down = [ref[pl.ds(low + 8 * t, 8), :] for t in range(2)]
                up = [ref[pl.ds(high + 8 * t, 8), :] for t in range(2)]
                row = [
                    jnp.broadcast_to(lat_in[s, pl.ds(off + lev, 1), :], (8, NX)) for s in range(2)
                ]
                one = [pltpu.roll(tile[t], 1, 0) for t in range(2)]
                seven = [pltpu.roll(tile[t], 7, 0) for t in range(2)]
                before = [jnp.where(sub == 0, row[0], one[0]), jnp.where(sub == 0, one[0], one[1])]
                after = [jnp.where(sub == 7, seven[1], seven[0]), jnp.where(sub == 7, row[1], seven[1])]
                west, east = [], []
                for t in range(2):
                    j = lev * 2 + t
                    with_left = jnp.where(lane == NX - 1, pltpu.roll(ends[0], NX - 1 - j, 1), tile[t])
                    west.append(pltpu.roll(with_left, 1, 1))
                    with_right = jnp.where(
                        lane == 0, pltpu.roll(ends[1], lax.rem(NX - j, NX), 1), tile[t]
                    )
                    east.append(pltpu.roll(with_right, NX - 1, 1))
                fields.append((tile, (down, up, before, after, west, east)))
            (u, u_near), (k, k_near) = fields
            for t in range(2):
                at = pl.multiple_of(l * NA, 8) + 8 * t
                total = None
                for f in range(6):
                    w = harmonic(k[t], k_near[f][t])
                    wts[f, pl.ds(at, 8), :] = w
                    term = w * (u_near[f][t] - u[t])
                    total = term if total is None else total + term
                r = (h_ref[pl.ds(base + 8 * t, 8), :] + pbuf[pl.ds(base + 8 * t, 8), :]) - (u[t] - total)
                rs[t, pl.ds(pl.multiple_of(lev * 8, 8), 8), :] = r * scale
            return carry

        def two_levels(m, carry):
            level(m * 2, carry)
            return level(m * 2 + 1, carry)

        lax.fori_loop(0, LP // 2, two_levels, 0)
        for part in range(2):
            to = zd * 2 + lax.rem(part + lat, 2)

            @pl.when(to != me)
            def _():
                fwd_copy(part, zd, to).start()

            @pl.when(to == me)
            def _():
                rr[me] = rs[part, pl.ds(pl.multiple_of(zd * 64, 8), 64), :]

        return carry

    lax.fori_loop(0, zs, chunk, 0)

    beta = CORNER ** (1.0 / steps)
    shift_re = [1.0 - beta * math.cos(2 * math.pi * k / steps) for k in range(half + 1)]
    shift_im = [beta * math.sin(2 * math.pi * k / steps) for k in range(half + 1)]

    def invert(l, carry):
        at = pl.multiple_of(l * NA + q * 8, 8)
        total = wts[0, pl.ds(at, 8), :]
        for f in range(1, 6):
            total = total + wts[f, pl.ds(at, 8), :]
        for k in range(half + 1):
            re = total + shift_re[k]
            if k in (0, half):
                value = 1.0 / re
                row = 0 if k == 0 else 8
                coef[pl.ds(l * 192 + row, 8, stride=24), :] = value
                if k == 0:
                    coef[pl.ds(l * 192 + 16, 8, stride=24), :] = zero
            else:
                share = 1.0 / (re * re + shift_im[k] * shift_im[k])
                real = re * share
                coef[pl.ds(l * 192 + k, 8, stride=24), :] = real
                coef[pl.ds(l * 192 + 8 + k, 8, stride=24), :] = real
                coef[pl.ds(l * 192 + 16 + k, 8, stride=24), :] = share * (-shift_im[k])
        return carry

    lax.fori_loop(0, LP, invert, 0)

    def fwd_arrival(src):
        return remote(rs.at[0, pl.ds(0, 64), :], rr.at[src], fwd_s.at[src], fwd_r.at[src], {"tm": src})

    def await_fwd(d, carry):
        fwd_arrival(lax.rem(me + d, steps)).wait_recv()
        return carry

    lax.fori_loop(1, steps, await_fwd, 0)

    lane64 = lax.rem(lane, 64)

    def pack(l, tiles, packs):
        low, high = zero, zero
        for a in range(AP):
            for f in range(2):
                j = a + 64 * f
                tile = tiles[a][f]
                here = lane == j
                low = jnp.where(here, pltpu.roll(tile, j, 1) if j > 0 else tile, low)
                high = jnp.where(here, pltpu.roll(tile, j + 1, 1), high)
        mask = lax.div(lane64, 8) == l
        return (
            jnp.where(mask, pltpu.roll(low, l * 8, 1), packs[0]),
            jnp.where(mask, pltpu.roll(high, l * 8, 1), packs[1]),
        )

    def divide(l, a, re, im):
        at = pl.multiple_of((l * 8 + a) * 24, 8)
        c_re, c_im, cross = (coef[pl.ds(at + 8 * i, 8), :] for i in range(3))
        return re * c_re - im * cross, im * c_im + re * cross

    def to_spectrum(l, packs):
        at = pl.multiple_of(l * 8, 8)
        r = [rr[n, pl.ds(at, 8), :] for n in range(steps)]
        e = [r[0]] + [r[n] + r[steps - n] for n in range(1, half)] + [r[half]]
        o = [r[n] - r[steps - n] for n in range(1, half)]
        real = cosine_sums(e, steps)
        imag = sine_sums(o, steps)
        for k in range(half):
            spec[pl.ds(l * 128 + k, 8, stride=16), :] = real[k]
        spec[pl.ds(l * 128 + 8, 8, stride=16), :] = real[half]
        for k in range(1, half):
            spec[pl.ds(l * 128 + 8 + k, 8, stride=16), :] = -imag[k - 1]
        tiles = []
        for a in range(AP):
            row = pl.multiple_of((l * 8 + a) * 16, 8)
            x = divide(l, a, spec[pl.ds(row, 8), :], spec[pl.ds(row + 8, 8), :])
            for f in range(2):
                xe[0, l + 1, a + 1, pl.ds(8 * f, 8), :] = x[f]
            tiles.append(x)
        return pack(l, tiles, packs)

    def halo_refs(b, d):
        inner = pl.ds(1, 8)
        if d == 0:
            return xe.at[b, 1, inner], xe.at[b, 0, inner]
        if d == 1:
            return xe.at[b, LP, inner], xe.at[b, LP + 1, inner]
        if d == 2:
            return xe.at[b, inner, 1], xe.at[b, inner, 0]
        if d == 3:
            return xe.at[b, inner, AP], xe.at[b, inner, AP + 1]
        return edge_out.at[b, d - 4], edge_in.at[b, d - 4]

    def halo_copy(b, d):
        other = d + 1 - 2 * (d % 2)
        return remote(
            halo_refs(b, d)[0], halo_refs(b, other)[1], halo_s.at[b, d], halo_r.at[b, other], homes[d][1]
        )

    def halo_arrival(b, d):
        return remote(halo_refs(b, d)[0], halo_refs(b, d)[1], halo_s.at[b, d], halo_r.at[b, d], homes[d][1])

    def exchange(b, packs):
        for s in range(2):
            edge_out[b, s] = packs[s]
        for d in range(6):
            guarded(homes[d][0], lambda d=d: halo_copy(b, d).start())
        for d in range(6):
            guarded(homes[d][0], lambda d=d: halo_arrival(b, d).wait_recv())

    exchange(0, lax.fori_loop(0, LP, to_spectrum, (zero, zero)))

    def sweep(b, last):
        ends = [edge_in[b, s] for s in range(2)]

        def level(l, packs):
            near_ends = [pltpu.roll(ends[s], NX - 8 * l, 1) for s in range(2)]
            tiles = []
            for a in range(AP):
                w = [
                    jnp.broadcast_to(wts[f, pl.ds(l * NA + q * 8 + a, 1), :], (8, NX)) for f in range(6)
                ]
                row = pl.multiple_of((l * 8 + a) * 16, 8)
                rhs = []
                for f in range(2):
                    part = pl.ds(8 * f, 8)
                    j = a + 64 * f
                    x = xe[b, l + 1, a + 1, part, :]
                    with_left = jnp.where(lane == NX - 1, pltpu.roll(near_ends[0], NX - 1 - j, 1), x)
                    with_right = jnp.where(
                        lane == 0, pltpu.roll(near_ends[1], NX - j, 1) if j > 0 else near_ends[1], x
                    )
                    total = spec[pl.ds(row + 8 * f, 8), :]
                    total = total + w[0] * xe[b, l, a + 1, part, :] + w[1] * xe[b, l + 2, a + 1, part, :]
                    total = total + w[2] * xe[b, l + 1, a, part, :] + w[3] * xe[b, l + 1, a + 2, part, :]
                    total = total + w[4] * pltpu.roll(with_left, 1, 1)
                    total = total + w[5] * pltpu.roll(with_right, NX - 1, 1)
                    rhs.append(total)
                x = divide(l, a, rhs[0], rhs[1])
                for f in range(2):
                    if last:
                        xf[pl.ds(row + 8 * f, 8), :] = x[f]
                    else:
                        xe[b + 1, l + 1, a + 1, pl.ds(8 * f, 8), :] = x[f]
                tiles.append(x)
            return packs if last else pack(l, tiles, packs)

        return lax.fori_loop(0, LP, level, (zero, zero))

    for b in range(SWEEPS):
        packs = sweep(b, b == SWEEPS - 1)
        if b < SWEEPS - 1:
            exchange(b + 1, packs)

    def from_spectrum(l, carry):
        x = [xf[pl.ds(l * 128 + k, 8, stride=16), :] for k in range(half)]
        x_half = xf[pl.ds(l * 128 + 8, 8, stride=16), :]
        y = [xf[pl.ds(l * 128 + 8 + k, 8, stride=16), :] for k in range(1, half)]
        even = cosine_sums([x[0] * 0.5] + x[1:] + [x_half * 0.5], steps)
        odd = sine_sums(y, steps)
        at = pl.multiple_of(l * 8, 8)
        ws[0, pl.ds(at, 8), :] = even[0]
        ws[half, pl.ds(at, 8), :] = even[half]
        for n in range(1, half):
            ws[n, pl.ds(at, 8), :] = even[n] - odd[n - 1]
            ws[steps - n, pl.ds(at, 8), :] = even[n] + odd[n - 1]
        return carry

    lax.fori_loop(0, LP, from_spectrum, 0)

    def place(part, zz):
        return wb.at[part, pl.ds(pl.multiple_of(zz * 64, 8), 64), :]

    def back_copy(d):
        to = lax.rem(me + d, steps)
        return remote(ws.at[to], place(q, z), back_s.at[to], back_r.at[me], {"tm": to})

    def start_back(i, carry):
        odd = lax.rem(i, 2)
        d = half + (1 - odd) * lax.div(i, 2) - odd * lax.div(i + 1, 2)
        back_copy(d).start()
        return carry

    lax.fori_loop(0, steps - 1, start_back, 0)
    wb[q, pl.ds(pl.multiple_of(z * 64, 8), 64), :] = ws[me]
    share = pick(me, [2.0 / (steps * g) for g in gamma])

    def finish(i, carry):
        odd = lax.rem(i, 2)
        away = lax.div(i + 1, 2)
        src = lax.rem(me + steps + odd * away - (1 - odd) * away, steps)
        zz = lax.div(src, 2)
        part = lax.rem(lax.rem(src, 2) + lat, 2)

        @pl.when(i > 0)
        def _():
            remote(ws.at[src], place(part, zz), back_s.at[src], back_r.at[src], {"tm": src}).wait_recv()

        for l in range(LP):
            at = pl.multiple_of((zz * LP + l) * NA + part * 8, 8)
            w = wb[part, pl.ds(pl.multiple_of(zz * 64, 8) + l * 8, 8), :]
            out_ref[pl.ds(at, 8), :] = u_ref[pl.ds(at, 8), :] + w * share
        return carry

    lax.fori_loop(0, steps, finish, 0)

    @pl.when(me < steps - 1)
    def _():
        for i in range(zs):
            shift_copy(i, later_z, later).wait_send()

    for d in range(4):
        guarded(sides[d][0], lambda d=d: side_copy(d).wait_send())

    def sent(d, carry):
        to = lax.rem(me + d, steps)
        fwd_copy(0, 0, to).wait_send()
        back_copy(d).wait_send()
        return carry

    lax.fori_loop(1, steps, sent, 0)
    for b in range(SWEEPS):
        for d in range(6):
            guarded(homes[d][0], lambda b=b, d=d: halo_copy(b, d).wait_send())


def on_device(steps, nlat, nlon, iterate, heating, initial, region, cond_table):
    levels = initial.shape[0]
    rows = levels * NA
    zs = steps // 2
    vmem = pl.BlockSpec(memory_space=pltpu.VMEM)
    flat = lambda value: value.reshape(rows, NX)
    dma = pltpu.SemaphoreType.DMA
    out = pl.pallas_call(
        functools.partial(kernel, steps, nlat, nlon),
        out_shape=jax.ShapeDtypeStruct((rows, NX), F32),
        in_specs=[vmem, vmem, vmem, pl.BlockSpec(memory_space=pltpu.SMEM), pl.BlockSpec(memory_space=pl.ANY)],
        out_specs=vmem,
        scratch_shapes=[
            pltpu.VMEM((rows + 2 * NA, NX), F32),
            pltpu.VMEM((6, LP * NA, NX), F32),
            pltpu.VMEM((rows, NX), F32),
            pltpu.VMEM((2, 2 * levels, NX), F32),
            pltpu.VMEM((2, 2 * levels, NX), F32),
            pltpu.VMEM((2, 16, NX), F32),
            pltpu.VMEM((2, 16, NX), F32),
            pltpu.VMEM((2, levels * 8, NX), F32),
            pltpu.VMEM((steps, 64, NX), F32),
            pltpu.VMEM((64 * 16, NX), F32),
            pltpu.VMEM((64 * 24, NX), F32),
            pltpu.VMEM((SWEEPS, LP + 2, AP + 2, 16, NX), F32),
            pltpu.VMEM((64 * 16, NX), F32),
            pltpu.VMEM((SWEEPS, 2, 8, NX), F32),
            pltpu.VMEM((SWEEPS, 2, 8, NX), F32),
            pltpu.VMEM((steps, 64, NX), F32),
            pltpu.VMEM((2, levels * 8, NX), F32),
            dma,
            dma((zs,)),
            dma((zs,)),
            dma((4,)),
            dma((4,)),
            dma((steps,)),
            dma((steps,)),
            dma((SWEEPS, 6)),
            dma((SWEEPS, 6)),
            dma((steps,)),
            dma((steps,)),
        ],
        compiler_params=pltpu.CompilerParams(
            collective_id=0, has_side_effects=True, vmem_limit_bytes=40 * 1024 * 1024
        ),
    )(flat(iterate), flat(heating), flat(region), cond_table, flat(initial))
    return out.reshape(iterate.shape)


def solution(mesh):
    sizes = mesh.shape
    return jax.shard_map(
        functools.partial(on_device, sizes["tm"], sizes["lat"], sizes["lon"]),
        mesh=mesh,
        in_specs=(
            P("tm", None, "lat", "lon"),
            P("tm", None, "lat", "lon"),
            P(None, "lat", "lon"),
            P(None, "lat", "lon"),
            P(),
        ),
        out_specs=P("tm", None, "lat", "lon"),
        check_vma=False,
    )
```

```python
import functools
import math

import jax
import jax.numpy as jnp
from jax import lax
from jax.experimental import pallas as pl
from jax.experimental.pallas import tpu as pltpu
from jax.sharding import PartitionSpec as P

MESH = pl.DeviceIdType.MESH
F32 = jnp.float32
CORNER = 0.1
SWEEPS = 3
LP = 8
AP = 8
NA = 16
NX = 128
VMEM_LIMIT = 62 * 1024 * 1024


def harmonic(first, second):
    return 2.0 * first * second / (first + second)


def weighted(pairs):
    total = None
    for coefficient, value in pairs:
        if abs(coefficient) < 1e-12:
            continue
        if abs(coefficient - 1.0) < 1e-12:
            term = value
        elif abs(coefficient + 1.0) < 1e-12:
            total = -value if total is None else total - value
            continue
        else:
            term = value * coefficient
        total = term if total is None else total + term
    return total


def cosine_sums(e, n):
    half, quarter = n // 2, n // 4
    even = [e[m] + e[half - m] for m in range(quarter)]
    odd = [e[m] - e[half - m] for m in range(quarter)]
    out = []
    for k in range(half + 1):
        parts = even if k % 2 == 0 else odd
        pairs = [(math.cos(2 * math.pi * k * m / n), parts[m]) for m in range(quarter)]
        pairs.append((math.cos(2 * math.pi * k * quarter / n), e[quarter]))
        out.append(weighted(pairs))
    return out


def sine_sums(o, n):
    half, quarter = n // 2, n // 4
    plus = [o[m - 1] + o[half - m - 1] for m in range(1, quarter)]
    minus = [o[m - 1] - o[half - m - 1] for m in range(1, quarter)]
    out = []
    for k in range(1, half):
        parts = plus if k % 2 == 1 else minus
        pairs = [(math.sin(2 * math.pi * k * m / n), parts[m - 1]) for m in range(1, quarter)]
        pairs.append((math.sin(2 * math.pi * k * quarter / n), o[quarter - 1]))
        total = weighted(pairs)
        out.append(total if total is not None else jnp.zeros_like(o[0]))
    return out


def pick(index, values):
    chosen = jnp.float32(values[0])
    for i, value in enumerate(values):
        if i > 0:
            chosen = jnp.where(index == i, jnp.float32(value), chosen)
    return chosen


def kernel(
    steps, nlat, nlon,
    u_hbm, u_parts, h_hbm, reg_hbm, init_hbm, table_ref, out_ref,
    u_ref, h_ref, reg_ref, kap, wts, pbuf, lat_out, lat_in, lon_out, lon_in, lon_mix,
    rs, rr, ur, spec, coef, xe, xf, edge_out, edge_in, ws, wb,
    local, shift_s, shift_r, side_s, side_r, state_s, state_r, fwd_s, fwd_r,
    lev_s, lev_r, lat_s, lat_r, lon_s, lon_r, back_s, back_r,
):
    levels = u_ref.shape[0] // NA
    zs = steps // 2
    half = steps // 2
    me = lax.axis_index("tm")
    lat = lax.axis_index("lat")
    lon = lax.axis_index("lon")
    z = lax.div(me, 2)
    xl = lax.rem(me, 2)
    q = lax.rem(xl + lat, 2)
    left = lax.rem(lon + nlon - 1, nlon)
    right = lax.rem(lon + 1, nlon)
    sub = lax.broadcasted_iota(jnp.int32, (8, NX), 0)
    lane = lax.broadcasted_iota(jnp.int32, (8, NX), 1)
    lane_pair = lax.div(lane, 2)
    odd_lane = lax.rem(lane, 2) == 1
    first_lane = lane == 0
    last_lane = lane == NX - 1
    zero = jnp.zeros((8, NX), F32)

    def remote(src, dst, send, recv, device):
        return pltpu.make_async_remote_copy(
            src_ref=src, dst_ref=dst, send_sem=send, recv_sem=recv, device_id=device, device_id_type=MESH
        )

    def guarded(condition, act):
        if condition is None:
            act()
        else:
            pl.when(condition)(act)

    sides = (
        (lat > 0, {"lat": lat - 1}),
        (lat < nlat - 1, {"lat": lat + 1}),
        (None, {"lon": left}),
        (None, {"lon": right}),
    )
    x_low = xl * (1 - q) + (1 - xl) * q
    x_high = xl * q + (1 - xl) * (1 - q)
    lev_sides = ((z > 0, {"tm": me - 2}), (z < zs - 1, {"tm": me + 2}))
    lat_sides = (
        (q + lat > 0, {"tm": z * 2 + x_low, "lat": lat - (1 - q)}),
        ((1 - q) + (nlat - 1 - lat) > 0, {"tm": z * 2 + x_high, "lat": lat + q}),
    )
    lon_sides = ((None, {"lon": left}), (None, {"lon": right}))

    barrier = pltpu.get_barrier_semaphore()
    for d in range(1, steps):
        pl.semaphore_signal(barrier, inc=1, device_id={"tm": lax.rem(me + d, steps)}, device_id_type=MESH)
    for condition, device in sides:
        guarded(
            condition,
            functools.partial(pl.semaphore_signal, barrier, inc=1, device_id=device, device_id_type=MESH),
        )

    take_reg = pltpu.make_async_copy(reg_hbm, reg_ref, local.at[0])
    take_u = pltpu.make_async_copy(u_hbm, u_ref, local.at[1])
    take_h = pltpu.make_async_copy(h_hbm, h_ref, local.at[2])
    take_init = pltpu.make_async_copy(init_hbm, pbuf, local.at[3])
    take_reg.start()
    take_u.start()
    take_h.start()

    @pl.when(me == 0)
    def _():
        take_init.start()

    for b in range(SWEEPS):
        for condition, place in (
            (z == 0, (b, 0, slice(None))),
            (z == zs - 1, (b, 1, slice(None))),
            (q + lat == 0, (b, slice(None), 0)),
            ((1 - q) + (nlat - 1 - lat) == 0, (b, slice(None), AP + 1)),
        ):
            def clear(place=place):
                xe[place] = jnp.zeros((10, 16, NX), F32)

            pl.when(condition)(clear)

    @pl.when(lat == 0)
    def _():
        lat_in[0] = jnp.zeros(lat_in.shape[1:], F32)

    @pl.when(lat == nlat - 1)
    def _():
        lat_in[1] = jnp.zeros(lat_in.shape[1:], F32)

    @pl.when(jnp.logical_and(me > 0, xl == 0))
    def _():
        pbuf[...] = jnp.zeros(pbuf.shape, F32)

    kap[pl.ds(0, NA), :] = jnp.zeros((NA, NX), F32)
    kap[pl.ds((levels + 1) * NA, NA), :] = jnp.zeros((NA, NX), F32)
    table = [table_ref[c] for c in range(8)]
    take_reg.wait()
    take_u.wait()

    for group in range((levels + 31) // 32):
        def conduct(g, packs):
            gathered = [zero, zero]
            for j in range(16):
                at = pl.multiple_of((group * 4 + g) * 128, 8) + j * 8
                reg = reg_ref[pl.ds(at, 8), :]
                k = jnp.full((8, NX), table[0], F32)
                for c in range(1, 8):
                    k = jnp.where(reg == c, table[c], k)
                kap[pl.ds(at + NA, 8), :] = k
                u = u_ref[pl.ds(at, 8), :]
                for f, tile in ((0, u), (1, k)):
                    gathered[f] = jnp.where(lane_pair == j, pltpu.roll(tile, 2 * j + 1, 1), gathered[f])
            mask = lax.div(lane, 32) == g
            return tuple(jnp.where(mask, pltpu.roll(gathered[f], g * 32, 1), packs[f]) for f in range(2))

        packs = lax.fori_loop(0, min(4, levels // 8 - 4 * group), conduct, (zero, zero))
        for f in range(2):
            lon_out[group, f] = packs[f]
    for g in range(levels // 8):
        for side, row in ((0, 0), (1, NA - 1)):
            lat_out[side, pl.ds(g * 8, 8), :] = u_ref[pl.ds(g * 128 + row, 8, stride=NA), :]
            lat_out[side, pl.ds(levels + g * 8, 8), :] = kap[pl.ds(NA + g * 128 + row, 8, stride=NA), :]

    lat_count = jnp.where(lat > 0, 1, 0) + jnp.where(lat < nlat - 1, 1, 0)
    pl.semaphore_wait(barrier, steps - 1 + 2 + lat_count)

    def side_copy(d):
        if d < 2:
            return remote(lat_out.at[d], lat_in.at[1 - d], side_s.at[d], side_r.at[1 - d], sides[d][1])
        return remote(lon_out, lon_in.at[3 - d], side_s.at[d], side_r.at[5 - d], sides[d][1])

    def side_arrival(d):
        if d < 2:
            return remote(lat_out.at[d], lat_in.at[d], side_s.at[d], side_r.at[d], sides[d][1])
        return remote(lon_out, lon_in.at[d - 2], side_s.at[d], side_r.at[d], sides[d][1])

    for d in range(4):
        guarded(sides[d][0], lambda d=d: side_copy(d).start())

    def order(i, at):
        odd = lax.rem(i, 2)
        away = zs // 2 + (1 - odd) * lax.div(i, 2) - odd * lax.div(i + 1, 2)
        return lax.rem(at + away, zs)

    rows = LP * NA

    def shift_copy(i):
        part = pl.ds(pl.multiple_of(order(i, z) * rows, 8), rows)
        return remote(u_hbm.at[part, :], pbuf.at[part, :], shift_s.at[i], shift_r.at[i], {"tm": me + 1 - 2 * xl})

    @pl.when(xl == 0)
    def _():
        for i in range(zs):
            shift_copy(i).start()

    def state_copy(to):
        part = lax.rem(lax.rem(to, 2) + lat, 2)
        return remote(
            u_parts.at[pl.ds(lax.div(to, 2) * LP, LP), part], ur.at[z], state_s.at[to], state_r.at[z], {"tm": to}
        )

    sends_state = jnp.logical_and(xl == 1, z < zs - 1)

    @pl.when(sends_state)
    def _():
        def send(i, carry):
            odd = lax.rem(i, 2)
            d = half + (1 - odd) * lax.div(i, 2) - odd * lax.div(i + 1, 2)
            state_copy(lax.rem(me + d, steps)).start()
            return carry

        lax.fori_loop(0, steps - 1, send, 0)
        for l in range(LP):
            row = pl.multiple_of((z * LP + l) * NA + q * 8, 8)
            ur[z, l] = u_ref[pl.ds(row, 8), :]

    take_h.wait()

    @pl.when(me == 0)
    def _():
        take_init.wait()

    for d in range(4):
        guarded(sides[d][0], lambda d=d: side_arrival(d).wait_recv())
    for group in range((levels + 31) // 32):
        for f in range(2):
            lon_mix[group, f] = jnp.where(odd_lane, lon_in[1, group, f], lon_in[0, group, f])

    gamma = [CORNER ** (n / steps) for n in range(steps)]
    scale = pick(me, gamma)

    def fwd_copy(part, zd, to):
        return remote(
            rs.at[part, pl.ds(pl.multiple_of(zd * 64, 8), 64), :], rr.at[me], fwd_s.at[to], fwd_r.at[me], {"tm": to}
        )

    def chunk(i, carry):
        zd = order(i, z)

        @pl.when(xl == 1)
        def _():
            shift_copy(i).wait_recv()

        def level(l):
            lev = zd * LP + l
            base = pl.multiple_of(lev * NA, 8)
            under = pl.multiple_of(jnp.maximum(lev - 1, 0) * NA, 8)
            over = pl.multiple_of(jnp.minimum(lev + 1, levels - 1) * NA, 8)
            group = lax.div(lev, 32)
            fields = []
            for f, ref, low, mid, high in (
                (0, u_ref, under, base, over),
                (1, kap, base, base + NA, base + 2 * NA),
            ):
                tile = [ref[pl.ds(mid + 8 * t, 8), :] for t in range(2)]
                down = [ref[pl.ds(low + 8 * t, 8), :] for t in range(2)]
                up = [ref[pl.ds(high + 8 * t, 8), :] for t in range(2)]
                row = [
                    jnp.broadcast_to(lat_in[s, pl.ds(f * levels + lev, 1), :], (8, NX)) for s in range(2)
                ]
                one = [pltpu.roll(tile[t], 1, 0) for t in range(2)]
                seven = [pltpu.roll(tile[t], 7, 0) for t in range(2)]
                before = [jnp.where(sub == 0, row[0], one[0]), jnp.where(sub == 0, one[0], one[1])]
                after = [jnp.where(sub == 7, seven[1], seven[0]), jnp.where(sub == 7, row[1], seven[1])]
                ends = lon_mix[group, f]
                west, east = [], []
                for t in range(2):
                    halo = pltpu.roll(ends, NX - 1 - 2 * (lax.rem(lev, 32) * 2 + t), 1)
                    west.append(pltpu.roll(jnp.where(last_lane, halo, tile[t]), 1, 1))
                    east.append(pltpu.roll(jnp.where(first_lane, halo, tile[t]), NX - 1, 1))
                fields.append((tile, (down, up, before, after, west, east)))
            (u, u_near), (k, k_near) = fields
            for t in range(2):
                at = pl.multiple_of(l * NA, 8) + 8 * t
                total = None
                for f in range(6):
                    w = harmonic(k[t], k_near[f][t])
                    wts[f, pl.ds(at, 8), :] = w
                    term = w * (u_near[f][t] - u[t])
                    total = term if total is None else total + term
                r = (h_ref[pl.ds(base + 8 * t, 8), :] + pbuf[pl.ds(base + 8 * t, 8), :]) - (u[t] - total)
                rs[t, pl.ds(pl.multiple_of(lev * 8, 8), 8), :] = r * scale

        def some_levels(m, carry):
            for l in range(4):
                level(m * 4 + l)
            return carry

        lax.fori_loop(0, LP // 4, some_levels, 0)
        for part in range(2):
            to = zd * 2 + lax.rem(part + lat, 2)

            @pl.when(to != me)
            def _():
                fwd_copy(part, zd, to).start()

            @pl.when(to == me)
            def _():
                rr[me] = rs[part, pl.ds(pl.multiple_of(zd * 64, 8), 64), :]

        return carry

    lax.fori_loop(0, zs, chunk, 0)

    beta = CORNER ** (1.0 / steps)
    shift_re = [1.0 - beta * math.cos(2 * math.pi * k / steps) for k in range(half + 1)]
    shift_im = [beta * math.sin(2 * math.pi * k / steps) for k in range(half + 1)]

    def invert(l, carry):
        at = pl.multiple_of(l * NA + q * 8, 8)
        total = wts[0, pl.ds(at, 8), :]
        for f in range(1, 6):
            total = total + wts[f, pl.ds(at, 8), :]
        for k in range(half + 1):
            re = total + shift_re[k]
            if k in (0, half):
                value = 1.0 / re
                row = 0 if k == 0 else 8
                coef[pl.ds(l * 192 + row, 8, stride=24), :] = value
                if k == 0:
                    coef[pl.ds(l * 192 + 16, 8, stride=24), :] = zero
            else:
                share = 1.0 / (re * re + shift_im[k] * shift_im[k])
                real = re * share
                coef[pl.ds(l * 192 + k, 8, stride=24), :] = real
                coef[pl.ds(l * 192 + 8 + k, 8, stride=24), :] = real
                coef[pl.ds(l * 192 + 16 + k, 8, stride=24), :] = share * (-shift_im[k])
        return carry

    lax.fori_loop(0, LP, invert, 0)

    def await_fwd(d, carry):
        src = lax.rem(me + d, steps)
        remote(rs.at[0, pl.ds(0, 64), :], rr.at[src], fwd_s.at[src], fwd_r.at[src], {"tm": src}).wait_recv()
        return carry

    lax.fori_loop(1, steps, await_fwd, 0)
    for i in range(zs - 1):

        @pl.when(me != 2 * i + 1)
        def _():
            remote(u_parts.at[pl.ds(0, LP), 0], ur.at[i], state_s.at[i], state_r.at[i], {"tm": 2 * i + 1}).wait_recv()

    def sent_index(m, s):
        return 2 + 2 * m + s

    def inner_index(m, s):
        return jnp.where(m == LP // 2 - 1, LP + 1 - s, 4 + 2 * m + s)

    def level_of(m, s):
        return m + s * (LP - 1 - 2 * m)

    def divide(l, a, re, im):
        at = pl.multiple_of((l * 8 + a) * 24, 8)
        c_re, c_im, cross = (coef[pl.ds(at + 8 * i, 8), :] for i in range(3))
        return re * c_re - im * cross, im * c_im + re * cross

    class Packed:
        def __init__(self):
            self.parts = [zero, zero]

        def add(self, s, a, f, tile):
            j = (s * AP + a) * 2 + f
            self.parts[f] = jnp.where(lane_pair == j, pltpu.roll(tile, 2 * j + 1, 1), self.parts[f])

        def value(self):
            return jnp.where(lax.rem(lane_pair, 2) == 0, self.parts[0], self.parts[1])

    inner = pl.ds(1, AP)

    def lev_copy(b, d):
        return remote(
            xe.at[b, 2 + d, inner], xe.at[b, 1 - d, inner], lev_s.at[b, d], lev_r.at[b, 1 - d], lev_sides[d][1]
        )

    def lev_arrival(b, d):
        return remote(xe.at[b, 2 + d, inner], xe.at[b, d, inner], lev_s.at[b, d], lev_r.at[b, d], lev_sides[d][1])

    def lat_copy(b, m, d):
        pair = pl.ds(2 + 2 * m, 2)
        return remote(
            xe.at[b, pair, 1 + d * (AP - 1)], xe.at[b, pair, (1 - d) * (AP + 1)],
            lat_s.at[b, m, d], lat_r.at[b, m, 1 - d], lat_sides[d][1],
        )

    def lat_arrival(b, m, d):
        pair = pl.ds(2 + 2 * m, 2)
        return remote(
            xe.at[b, pair, 1 + d * (AP - 1)], xe.at[b, pair, d * (AP + 1)],
            lat_s.at[b, m, d], lat_r.at[b, m, d], lat_sides[d][1],
        )

    def lon_copy(b, m, d):
        return remote(
            edge_out.at[b, m], edge_in.at[b, m, 1 - d], lon_s.at[b, m, d], lon_r.at[b, m, 1 - d], lon_sides[d][1]
        )

    def lon_arrival(b, m, d):
        return remote(edge_out.at[b, m], edge_in.at[b, m, d], lon_s.at[b, m, d], lon_r.at[b, m, d], lon_sides[d][1])

    def send_edges(b, m, packed):
        edge_out[b, m] = packed.value()

        @pl.when(m == 0)
        def _():
            for d in range(2):
                guarded(lev_sides[d][0], lambda d=d: lev_copy(b, d).start())

        for d in range(2):
            lon_copy(b, m, d).start()
        for d in range(2):
            guarded(lat_sides[d][0], lambda d=d: lat_copy(b, m, d).start())

    def await_edges(b, m):
        @pl.when(m == 0)
        def _():
            for d in range(2):
                guarded(lev_sides[d][0], lambda d=d: lev_arrival(b, d).wait_recv())

        for d in range(2):
            guarded(lat_sides[d][0], lambda d=d: lat_arrival(b, m, d).wait_recv())
        for d in range(2):
            lon_arrival(b, m, d).wait_recv()

    def to_spectrum(m, carry):
        packed = Packed()
        for s in range(2):
            l = level_of(m, s)
            at = pl.multiple_of(l * 8, 8)
            r = [rr[n, pl.ds(at, 8), :] for n in range(steps)]
            for n in range(2, steps, 2):
                r[n] = r[n] + ur[n // 2 - 1, l] * gamma[n]
            e = [r[0]] + [r[n] + r[steps - n] for n in range(1, half)] + [r[half]]
            o = [r[n] - r[steps - n] for n in range(1, half)]
            real = cosine_sums(e, steps)
            imag = sine_sums(o, steps)
            for k in range(half):
                spec[pl.ds(l * 128 + k, 8, stride=16), :] = real[k]
            spec[pl.ds(l * 128 + 8, 8, stride=16), :] = real[half]
            for k in range(1, half):
                spec[pl.ds(l * 128 + 8 + k, 8, stride=16), :] = -imag[k - 1]
        for s in range(2):
            l = level_of(m, s)
            for a in range(AP):
                row = pl.multiple_of((l * 8 + a) * 16, 8)
                x = divide(l, a, spec[pl.ds(row, 8), :], spec[pl.ds(row + 8, 8), :])
                for f in range(2):
                    xe[0, sent_index(m, s), a + 1, pl.ds(8 * f, 8), :] = x[f]
                    packed.add(s, a, f, x[f])
        send_edges(0, m, packed)
        return carry

    lax.fori_loop(0, LP // 2, to_spectrum, 0)

    def back_copy(to, first, count):
        part = pl.ds(pl.multiple_of(first, 8), count)
        return remote(ws.at[to, part], wb.at[me, part], back_s.at[to], back_r.at[me], {"tm": to})

    def from_spectrum(m, s):
        base = s * 128
        x = [xf[pl.ds(base + k, 8, stride=16), :] for k in range(half)]
        x_half = xf[pl.ds(base + 8, 8, stride=16), :]
        y = [xf[pl.ds(base + 8 + k, 8, stride=16), :] for k in range(1, half)]
        even = cosine_sums([x[0] * 0.5] + x[1:] + [x_half * 0.5], steps)
        odd = sine_sums(y, steps)
        at = pl.ds(pl.multiple_of(m * 16, 8) + s * 8, 8)
        ws[0, at, :] = even[0]
        ws[half, at, :] = even[half]
        for n in range(1, half):
            ws[n, at, :] = even[n] - odd[n - 1]
            ws[steps - n, at, :] = even[n] + odd[n - 1]

    def sweep(b, last):
        def pair(m, carry):
            await_edges(b, m)
            ends = jnp.where(odd_lane, edge_in[b, m, 1], edge_in[b, m, 0])
            packed = Packed()
            for s in range(2):
                l = level_of(m, s)
                i = sent_index(m, s)
                beyond = (i - 2, inner_index(m, s))
                under, over = beyond if s == 0 else beyond[::-1]
                for a in range(AP):
                    w = [
                        jnp.broadcast_to(wts[f, pl.ds(l * NA + q * 8 + a, 1), :], (8, NX)) for f in range(6)
                    ]
                    row = pl.multiple_of((l * 8 + a) * 16, 8)
                    rhs = []
                    for f in range(2):
                        part = pl.ds(8 * f, 8)
                        j = (s * AP + a) * 2 + f
                        x = xe[b, i, a + 1, part, :]
                        halo = pltpu.roll(ends, NX - 1 - 2 * j, 1)
                        total = spec[pl.ds(row + 8 * f, 8), :]
                        total = total + w[0] * xe[b, under, a + 1, part, :] + w[1] * xe[b, over, a + 1, part, :]
                        total = total + w[2] * xe[b, i, a, part, :] + w[3] * xe[b, i, a + 2, part, :]
                        total = total + w[4] * pltpu.roll(jnp.where(last_lane, halo, x), 1, 1)
                        total = total + w[5] * pltpu.roll(jnp.where(first_lane, halo, x), NX - 1, 1)
                        rhs.append(total)
                    x = divide(l, a, rhs[0], rhs[1])
                    for f in range(2):
                        if last:
                            xf[pl.ds((s * AP + a) * 16 + 8 * f, 8), :] = x[f]
                        else:
                            xe[b + 1, i, a + 1, pl.ds(8 * f, 8), :] = x[f]
                            packed.add(s, a, f, x[f])
            if not last:
                send_edges(b + 1, m, packed)
            else:
                for s in range(2):
                    from_spectrum(m, s)

                @pl.when(lax.rem(m, 2) == 1)
                def _():
                    def send(i, carry):
                        odd = lax.rem(i, 2)
                        d = half + (1 - odd) * lax.div(i, 2) - odd * lax.div(i + 1, 2)
                        back_copy(lax.rem(me + d, steps), (m - 1) * 16, 32).start()
                        return carry

                    lax.fori_loop(0, steps - 1, send, 0)

            return carry

        lax.fori_loop(0, LP // 2, pair, 0)

    for b in range(SWEEPS):
        sweep(b, b == SWEEPS - 1)

    wb[me] = ws[me]
    share = pick(me, [2.0 / (steps * g) for g in gamma])

    def finish(i, carry):
        odd = lax.rem(i, 2)
        away = lax.div(i + 1, 2)
        src = lax.rem(me + steps + odd * away - (1 - odd) * away, steps)
        zz = lax.div(src, 2)
        part = lax.rem(lax.rem(src, 2) + lat, 2)

        @pl.when(i > 0)
        def _():
            remote(ws.at[src], wb.at[src], back_s.at[src], back_r.at[src], {"tm": src}).wait_recv()

        for m in range(LP // 2):
            for s in range(2):
                at = pl.multiple_of((zz * LP + level_of(m, s)) * NA + part * 8, 8)
                out_ref[pl.ds(at, 8), :] = u_ref[pl.ds(at, 8), :] + wb[src, pl.ds(m * 16 + s * 8, 8), :] * share
        return carry

    lax.fori_loop(0, steps, finish, 0)

    @pl.when(xl == 0)
    def _():
        for i in range(zs):
            shift_copy(i).wait_send()

    for d in range(4):
        guarded(sides[d][0], lambda d=d: side_copy(d).wait_send())

    def sent(d, carry):
        to = lax.rem(me + d, steps)
        fwd_copy(0, 0, to).wait_send()
        back_copy(to, 0, 64).wait_send()

        @pl.when(sends_state)
        def _():
            state_copy(to).wait_send()

        return carry

    lax.fori_loop(1, steps, sent, 0)
    for b in range(SWEEPS):
        for d in range(2):
            guarded(lev_sides[d][0], lambda b=b, d=d: lev_copy(b, d).wait_send())

        def edges_sent(m, carry, b=b):
            for d in range(2):
                guarded(lat_sides[d][0], lambda d=d: lat_copy(b, m, d).wait_send())
                lon_copy(b, m, d).wait_send()
            return carry

        lax.fori_loop(0, LP // 2, edges_sent, 0)


def on_device(steps, nlat, nlon, iterate, heating, initial, region, cond_table):
    levels = initial.shape[0]
    rows = levels * NA
    zs = steps // 2
    groups = (levels + 31) // 32
    pairs = LP // 2
    vmem = pl.BlockSpec(memory_space=pltpu.VMEM)
    anywhere = pl.BlockSpec(memory_space=pl.ANY)
    flat = lambda value: value.reshape(rows, NX)
    dma = pltpu.SemaphoreType.DMA
    out = pl.pallas_call(
        functools.partial(kernel, steps, nlat, nlon),
        out_shape=jax.ShapeDtypeStruct((rows, NX), F32),
        in_specs=[anywhere] * 5 + [pl.BlockSpec(memory_space=pltpu.SMEM)],
        out_specs=vmem,
        scratch_shapes=[
            pltpu.VMEM((rows, NX), F32),
            pltpu.VMEM((rows, NX), F32),
            pltpu.VMEM((rows, NX), jnp.int32),
            pltpu.VMEM((rows + 2 * NA, NX), F32),
            pltpu.VMEM((6, LP * NA, NX), F32),
            pltpu.VMEM((rows, NX), F32),
            pltpu.VMEM((2, 2 * levels, NX), F32),
            pltpu.VMEM((2, 2 * levels, NX), F32),
            pltpu.VMEM((groups, 2, 8, NX), F32),
            pltpu.VMEM((2, groups, 2, 8, NX), F32),
            pltpu.VMEM((groups, 2, 8, NX), F32),
            pltpu.VMEM((2, levels * 8, NX), F32),
            pltpu.VMEM((steps, 64, NX), F32),
            pltpu.VMEM((zs, LP, 8, NX), F32),
            pltpu.VMEM((64 * 16, NX), F32),
            pltpu.VMEM((64 * 24, NX), F32),
            pltpu.VMEM((SWEEPS, LP + 2, AP + 2, 16, NX), F32),
            pltpu.VMEM((16 * 16, NX), F32),
            pltpu.VMEM((SWEEPS, pairs, 8, NX), F32),
            pltpu.VMEM((SWEEPS, pairs, 2, 8, NX), F32),
            pltpu.VMEM((steps, 64, NX), F32),
            pltpu.VMEM((steps, 64, NX), F32),
            dma((4,)),
            dma((zs,)),
            dma((zs,)),
            dma((4,)),
            dma((4,)),
            dma((steps,)),
            dma((zs,)),
            dma((steps,)),
            dma((steps,)),
            dma((SWEEPS, 2)),
            dma((SWEEPS, 2)),
            dma((SWEEPS, pairs, 2)),
            dma((SWEEPS, pairs, 2)),
            dma((SWEEPS, pairs, 2)),
            dma((SWEEPS, pairs, 2)),
            dma((steps,)),
            dma((steps,)),
        ],
        compiler_params=pltpu.CompilerParams(
            collective_id=0, has_side_effects=True, vmem_limit_bytes=VMEM_LIMIT
        ),
    )(flat(iterate), iterate.reshape(levels, 2, AP, NX), flat(heating), flat(region), flat(initial), cond_table)
    return out.reshape(iterate.shape)


def solution(mesh):
    sizes = mesh.shape
    return jax.shard_map(
        functools.partial(on_device, sizes["tm"], sizes["lat"], sizes["lon"]),
        mesh=mesh,
        in_specs=(
            P("tm", None, "lat", "lon"),
            P("tm", None, "lat", "lon"),
            P(None, "lat", "lon"),
            P(None, "lat", "lon"),
            P(),
        ),
        out_specs=P("tm", None, "lat", "lon"),
        check_vma=False,
    )
```

```python
import functools
import math

import jax
import jax.numpy as jnp
from jax import lax
from jax.experimental import pallas as pl
from jax.experimental.pallas import tpu as pltpu
from jax.sharding import PartitionSpec as P

MESH = pl.DeviceIdType.MESH
F32 = jnp.float32
CORNER = 0.1
SWEEPS = 3
LP = 8
GROUPS = 2
AP = 8
NA = 16
NX = 128
VMEM_LIMIT = 40 * 1024 * 1024


def harmonic(first, second):
    return 2.0 * first * second / (first + second)


def weighted(pairs):
    total = None
    for coefficient, value in pairs:
        if abs(coefficient) < 1e-12:
            continue
        if abs(coefficient - 1.0) < 1e-12:
            term = value
        elif abs(coefficient + 1.0) < 1e-12:
            total = -value if total is None else total - value
            continue
        else:
            term = value * coefficient
        total = term if total is None else total + term
    return total


def cosine_sums(e, n):
    half, quarter = n // 2, n // 4
    even = [e[m] + e[half - m] for m in range(quarter)]
    odd = [e[m] - e[half - m] for m in range(quarter)]
    out = []
    for k in range(half + 1):
        parts = even if k % 2 == 0 else odd
        pairs = [(math.cos(2 * math.pi * k * m / n), parts[m]) for m in range(quarter)]
        pairs.append((math.cos(2 * math.pi * k * quarter / n), e[quarter]))
        out.append(weighted(pairs))
    return out


def sine_sums(o, n):
    half, quarter = n // 2, n // 4
    plus = [o[m - 1] + o[half - m - 1] for m in range(1, quarter)]
    minus = [o[m - 1] - o[half - m - 1] for m in range(1, quarter)]
    out = []
    for k in range(1, half):
        parts = plus if k % 2 == 1 else minus
        pairs = [(math.sin(2 * math.pi * k * m / n), parts[m - 1]) for m in range(1, quarter)]
        pairs.append((math.sin(2 * math.pi * k * quarter / n), o[quarter - 1]))
        total = weighted(pairs)
        out.append(total if total is not None else jnp.zeros_like(o[0]))
    return out


def pick(index, values):
    chosen = jnp.float32(values[0])
    for i, value in enumerate(values):
        if i > 0:
            chosen = jnp.where(index == i, jnp.float32(value), chosen)
    return chosen


def kernel(
    steps, nlat, nlon,
    u_hbm, u_parts, h_hbm, reg_hbm, init_hbm, table_hbm, out_ref,
    table_ref, u_ref, h_ref, reg_ref, kap, wts, pbuf, lat_out, lat_in, lon_out, lon_in, lon_mix,
    rs, rr, ur, relay, spec, coef, xe, xf, edge_out, edge_in, ws, wb,
    local, shift_s, shift_r, side_s, side_r, relay_s, relay_r, state_s, state_r, fwd_s, fwd_r,
    lev_s, lev_r, lat_s, lat_r, lon_s, lon_r, back_s, back_r,
):
    levels = u_ref.shape[0] // NA
    zs = steps // 2
    half = steps // 2
    me = lax.axis_index("tm")
    lat = lax.axis_index("lat")
    lon = lax.axis_index("lon")
    z = lax.div(me, 2)
    xl = lax.rem(me, 2)
    q = lax.rem(xl + lat, 2)
    left = lax.rem(lon + nlon - 1, nlon)
    right = lax.rem(lon + 1, nlon)
    sub = lax.broadcasted_iota(jnp.int32, (8, NX), 0)
    lane = lax.broadcasted_iota(jnp.int32, (8, NX), 1)
    lane_pair = lax.div(lane, 2)
    odd_lane = lax.rem(lane, 2) == 1
    first_lane = lane == 0
    last_lane = lane == NX - 1
    zero = jnp.zeros((8, NX), F32)

    def remote(src, dst, send, recv, device):
        return pltpu.make_async_remote_copy(
            src_ref=src, dst_ref=dst, send_sem=send, recv_sem=recv, device_id=device, device_id_type=MESH
        )

    def guarded(condition, act):
        if condition is None:
            act()
        else:
            pl.when(condition)(act)

    sides = (
        (lat > 0, {"lat": lat - 1}),
        (lat < nlat - 1, {"lat": lat + 1}),
        (None, {"lon": left}),
        (None, {"lon": right}),
    )
    x_low = xl * (1 - q) + (1 - xl) * q
    x_high = xl * q + (1 - xl) * (1 - q)
    lev_sides = ((z > 0, {"tm": me - 2}), (z < zs - 1, {"tm": me + 2}))
    lat_sides = (
        (q + lat > 0, {"tm": z * 2 + x_low, "lat": lat - (1 - q)}),
        ((1 - q) + (nlat - 1 - lat) > 0, {"tm": z * 2 + x_high, "lat": lat + q}),
    )
    lon_sides = ((None, {"lon": left}), (None, {"lon": right}))

    barrier = pltpu.get_barrier_semaphore()
    for d in range(1, steps):
        pl.semaphore_signal(barrier, inc=1, device_id={"tm": lax.rem(me + d, steps)}, device_id_type=MESH)
    for condition, device in sides:
        guarded(
            condition,
            functools.partial(pl.semaphore_signal, barrier, inc=1, device_id=device, device_id_type=MESH),
        )

    take_reg = pltpu.make_async_copy(reg_hbm, reg_ref, local.at[0])
    take_u = pltpu.make_async_copy(u_hbm, u_ref, local.at[1])
    take_h = pltpu.make_async_copy(h_hbm, h_ref, local.at[2])
    take_init = pltpu.make_async_copy(init_hbm, pbuf, local.at[3])
    take_table = pltpu.make_async_copy(table_hbm, table_ref, local.at[4])
    take_table.start()
    take_reg.start()
    take_u.start()
    take_h.start()

    @pl.when(me == 0)
    def _():
        take_init.start()

    for b in range(SWEEPS):
        for condition, place in (
            (z == 0, (b, 0, slice(None))),
            (z == zs - 1, (b, 1, slice(None))),
            (q + lat == 0, (b, slice(None), 0)),
            ((1 - q) + (nlat - 1 - lat) == 0, (b, slice(None), AP + 1)),
        ):
            def clear(place=place):
                xe[place] = jnp.zeros((10, 16, NX), F32)

            pl.when(condition)(clear)

    @pl.when(lat == 0)
    def _():
        lat_in[0] = jnp.zeros(lat_in.shape[1:], F32)

    @pl.when(lat == nlat - 1)
    def _():
        lat_in[1] = jnp.zeros(lat_in.shape[1:], F32)

    @pl.when(jnp.logical_and(me > 0, xl == 0))
    def _():
        pbuf[...] = jnp.zeros(pbuf.shape, F32)

    kap[pl.ds(0, NA), :] = jnp.zeros((NA, NX), F32)
    kap[pl.ds((levels + 1) * NA, NA), :] = jnp.zeros((NA, NX), F32)
    take_table.wait()
    table = [table_ref[c] for c in range(8)]
    take_reg.wait()
    take_u.wait()

    for group in range((levels + 31) // 32):
        def conduct(g, packs):
            gathered = [zero, zero]
            for j in range(16):
                at = pl.multiple_of((group * 4 + g) * 128, 8) + j * 8
                reg = reg_ref[pl.ds(at, 8), :]
                k = jnp.full((8, NX), table[0], F32)
                for c in range(1, 8):
                    k = jnp.where(reg == c, table[c], k)
                kap[pl.ds(at + NA, 8), :] = k
                u = u_ref[pl.ds(at, 8), :]
                for f, tile in ((0, u), (1, k)):
                    gathered[f] = jnp.where(lane_pair == j, pltpu.roll(tile, 2 * j + 1, 1), gathered[f])
            mask = lax.div(lane, 32) == g
            return tuple(jnp.where(mask, pltpu.roll(gathered[f], g * 32, 1), packs[f]) for f in range(2))

        packs = lax.fori_loop(0, min(4, levels // 8 - 4 * group), conduct, (zero, zero))
        for f in range(2):
            lon_out[group, f] = packs[f]
    for g in range(levels // 8):
        for side, row in ((0, 0), (1, NA - 1)):
            lat_out[side, pl.ds(g * 8, 8), :] = u_ref[pl.ds(g * 128 + row, 8, stride=NA), :]
            lat_out[side, pl.ds(levels + g * 8, 8), :] = kap[pl.ds(NA + g * 128 + row, 8, stride=NA), :]

    lat_count = jnp.where(lat > 0, 1, 0) + jnp.where(lat < nlat - 1, 1, 0)
    pl.semaphore_wait(barrier, steps - 1 + 2 + lat_count)

    def side_copy(d):
        if d < 2:
            return remote(lat_out.at[d], lat_in.at[1 - d], side_s.at[d], side_r.at[1 - d], sides[d][1])
        return remote(lon_out, lon_in.at[3 - d], side_s.at[d], side_r.at[5 - d], sides[d][1])

    def side_arrival(d):
        if d < 2:
            return remote(lat_out.at[d], lat_in.at[d], side_s.at[d], side_r.at[d], sides[d][1])
        return remote(lon_out, lon_in.at[d - 2], side_s.at[d], side_r.at[d], sides[d][1])

    for d in range(4):
        guarded(sides[d][0], lambda d=d: side_copy(d).start())

    def order(i, at):
        odd = lax.rem(i, 2)
        away = zs // 2 + (1 - odd) * lax.div(i, 2) - odd * lax.div(i + 1, 2)
        return lax.rem(at + away, zs)

    rows = LP * NA

    def shift_copy(i):
        part = pl.ds(pl.multiple_of(order(i, z) * rows, 8), rows)
        return remote(u_hbm.at[part, :], pbuf.at[part, :], shift_s.at[i], shift_r.at[i], {"tm": me + 1 - 2 * xl})

    @pl.when(xl == 0)
    def _():
        for i in range(zs):
            shift_copy(i).start()

    sends_state = z < zs - 1

    def state_parts(i, x):
        return u_parts.at[pl.ds(order(i, z) * LP, LP), lax.rem(x + lat, 2)]

    def relay_copy(i):
        return remote(state_parts(i, 0), relay.at[i], relay_s.at[i], relay_r.at[i], {"tm": me + 1 - 2 * xl})

    def state_copy(i):
        to = order(i, z) * 2 + 1
        return remote(state_parts(i, 1), ur.at[z], state_s.at[i], state_r.at[z], {"tm": to})

    def forward_copy(i):
        return remote(relay.at[i], ur.at[z], state_s.at[i], state_r.at[z], {"tm": order(i, z) * 2})

    @pl.when(jnp.logical_and(xl == 1, sends_state))
    def _():
        for i in range(zs):
            relay_copy(i).start()
            if i < zs - 1:
                state_copy(i).start()
        for l in range(LP):
            row = pl.multiple_of((z * LP + l) * NA + q * 8, 8)
            ur[z, l] = u_ref[pl.ds(row, 8), :]

    def forward(i):
        relay_copy(i).wait_recv()

        @pl.when(i < zs - 1)
        def _():
            forward_copy(i).start()

        @pl.when(i == zs - 1)
        def _():
            ur[z] = relay[i]

    forwards = jnp.logical_and(xl == 0, sends_state)
    ahead = min(2, zs - 1)

    @pl.when(forwards)
    def _():
        for i in range(ahead):
            forward(i)

    take_h.wait()

    @pl.when(me == 0)
    def _():
        take_init.wait()

    for d in range(4):
        guarded(sides[d][0], lambda d=d: side_arrival(d).wait_recv())
    for group in range((levels + 31) // 32):
        for f in range(2):
            lon_mix[group, f] = jnp.where(odd_lane, lon_in[1, group, f], lon_in[0, group, f])

    gamma = [CORNER ** (n / steps) for n in range(steps)]
    scale = pick(me, gamma)

    def fwd_copy(part, zd, to):
        return remote(
            rs.at[part, pl.ds(pl.multiple_of(zd * 64, 8), 64), :], rr.at[me], fwd_s.at[to], fwd_r.at[me], {"tm": to}
        )

    def chunk(i, carry):
        zd = order(i, z)

        @pl.when(jnp.logical_and(forwards, i + ahead < zs))
        def _():
            forward(i + ahead)

        @pl.when(xl == 1)
        def _():
            shift_copy(i).wait_recv()

        def level(l):
            lev = zd * LP + l
            base = pl.multiple_of(lev * NA, 8)
            under = pl.multiple_of(jnp.maximum(lev - 1, 0) * NA, 8)
            over = pl.multiple_of(jnp.minimum(lev + 1, levels - 1) * NA, 8)
            group = lax.div(lev, 32)
            fields = []
            for f, ref, low, mid, high in (
                (0, u_ref, under, base, over),
                (1, kap, base, base + NA, base + 2 * NA),
            ):
                tile = [ref[pl.ds(mid + 8 * t, 8), :] for t in range(2)]
                down = [ref[pl.ds(low + 8 * t, 8), :] for t in range(2)]
                up = [ref[pl.ds(high + 8 * t, 8), :] for t in range(2)]
                row = [
                    jnp.broadcast_to(lat_in[s, pl.ds(f * levels + lev, 1), :], (8, NX)) for s in range(2)
                ]
                one = [pltpu.roll(tile[t], 1, 0) for t in range(2)]
                seven = [pltpu.roll(tile[t], 7, 0) for t in range(2)]
                before = [jnp.where(sub == 0, row[0], one[0]), jnp.where(sub == 0, one[0], one[1])]
                after = [jnp.where(sub == 7, seven[1], seven[0]), jnp.where(sub == 7, row[1], seven[1])]
                ends = lon_mix[group, f]
                west, east = [], []
                for t in range(2):
                    halo = pltpu.roll(ends, NX - 1 - 2 * (lax.rem(lev, 32) * 2 + t), 1)
                    west.append(pltpu.roll(jnp.where(last_lane, halo, tile[t]), 1, 1))
                    east.append(pltpu.roll(jnp.where(first_lane, halo, tile[t]), NX - 1, 1))
                fields.append((tile, (down, up, before, after, west, east)))
            (u, u_near), (k, k_near) = fields
            for t in range(2):
                at = pl.multiple_of(l * NA, 8) + 8 * t
                total = None
                for f in range(6):
                    w = harmonic(k[t], k_near[f][t])
                    wts[f, pl.ds(at, 8), :] = w
                    term = w * (u_near[f][t] - u[t])
                    total = term if total is None else total + term
                r = (h_ref[pl.ds(base + 8 * t, 8), :] + pbuf[pl.ds(base + 8 * t, 8), :]) - (u[t] - total)
                rs[t, pl.ds(pl.multiple_of(lev * 8, 8), 8), :] = r * scale

        def some_levels(m, carry):
            for l in range(4):
                level(m * 4 + l)
            return carry

        lax.fori_loop(0, LP // 4, some_levels, 0)
        for part in range(2):
            to = zd * 2 + lax.rem(part + lat, 2)

            @pl.when(to != me)
            def _():
                fwd_copy(part, zd, to).start()

            @pl.when(to == me)
            def _():
                rr[me] = rs[part, pl.ds(pl.multiple_of(zd * 64, 8), 64), :]

        return carry

    lax.fori_loop(0, zs, chunk, 0)

    beta = CORNER ** (1.0 / steps)
    shift_re = [1.0 - beta * math.cos(2 * math.pi * k / steps) for k in range(half + 1)]
    shift_im = [beta * math.sin(2 * math.pi * k / steps) for k in range(half + 1)]

    def invert(l, carry):
        at = pl.multiple_of(l * NA + q * 8, 8)
        total = wts[0, pl.ds(at, 8), :]
        for f in range(1, 6):
            total = total + wts[f, pl.ds(at, 8), :]
        for k in range(half + 1):
            re = total + shift_re[k]
            if k in (0, half):
                value = 1.0 / re
                row = 0 if k == 0 else 8
                coef[pl.ds(l * 192 + row, 8, stride=24), :] = value
                if k == 0:
                    coef[pl.ds(l * 192 + 16, 8, stride=24), :] = zero
            else:
                share = 1.0 / (re * re + shift_im[k] * shift_im[k])
                real = re * share
                coef[pl.ds(l * 192 + k, 8, stride=24), :] = real
                coef[pl.ds(l * 192 + 8 + k, 8, stride=24), :] = real
                coef[pl.ds(l * 192 + 16 + k, 8, stride=24), :] = share * (-shift_im[k])
        return carry

    lax.fori_loop(0, LP, invert, 0)

    def await_fwd(d, carry):
        src = lax.rem(me + d, steps)
        remote(rs.at[0, pl.ds(0, 64), :], rr.at[src], fwd_s.at[src], fwd_r.at[src], {"tm": src}).wait_recv()
        return carry

    lax.fori_loop(1, steps, await_fwd, 0)
    for i in range(zs - 1):

        @pl.when(z != i)
        def _():
            remote(relay.at[0], ur.at[i], state_s.at[i], state_r.at[i], {"tm": 2 * i + xl}).wait_recv()

    def sent_index(m, s):
        return 2 + 2 * m + s

    def inner_index(m, s):
        return jnp.where(m == LP // 2 - 1, LP + 1 - s, 4 + 2 * m + s)

    def level_of(m, s):
        return m + s * (LP - 1 - 2 * m)

    def divide(l, a, re, im):
        at = pl.multiple_of((l * 8 + a) * 24, 8)
        c_re, c_im, cross = (coef[pl.ds(at + 8 * i, 8), :] for i in range(3))
        return re * c_re - im * cross, im * c_im + re * cross

    class Packed:
        def __init__(self):
            self.parts = [zero, zero]

        def add(self, p, a, f, tile):
            j = (p * AP + a) * 2 + f
            self.parts[f] = jnp.where(lane_pair == j, pltpu.roll(tile, 2 * j + 1, 1), self.parts[f])

        def value(self):
            return jnp.where(lax.rem(lane_pair, 2) == 0, self.parts[0], self.parts[1])

    inner = pl.ds(1, AP)

    def lev_copy(b, d):
        return remote(
            xe.at[b, 2 + d, inner], xe.at[b, 1 - d, inner], lev_s.at[b, d], lev_r.at[b, 1 - d], lev_sides[d][1]
        )

    def lev_arrival(b, d):
        return remote(xe.at[b, 2 + d, inner], xe.at[b, d, inner], lev_s.at[b, d], lev_r.at[b, d], lev_sides[d][1])

    def lat_copy(b, m, d):
        pair = pl.ds(2 + 4 * m, 4)
        return remote(
            xe.at[b, pair, 1 + d * (AP - 1)], xe.at[b, pair, (1 - d) * (AP + 1)],
            lat_s.at[b, m, d], lat_r.at[b, m, 1 - d], lat_sides[d][1],
        )

    def lat_arrival(b, m, d):
        pair = pl.ds(2 + 4 * m, 4)
        return remote(
            xe.at[b, pair, 1 + d * (AP - 1)], xe.at[b, pair, d * (AP + 1)],
            lat_s.at[b, m, d], lat_r.at[b, m, d], lat_sides[d][1],
        )

    def lon_copy(b, m, d):
        return remote(
            edge_out.at[b, m], edge_in.at[b, m, 1 - d], lon_s.at[b, m, d], lon_r.at[b, m, 1 - d], lon_sides[d][1]
        )

    def lon_arrival(b, m, d):
        return remote(edge_out.at[b, m], edge_in.at[b, m, d], lon_s.at[b, m, d], lon_r.at[b, m, d], lon_sides[d][1])

    def send_edges(b, m, packed):
        edge_out[b, m] = packed.value()

        @pl.when(m == 0)
        def _():
            for d in range(2):
                guarded(lev_sides[d][0], lambda d=d: lev_copy(b, d).start())

        for d in range(2):
            lon_copy(b, m, d).start()
        for d in range(2):
            guarded(lat_sides[d][0], lambda d=d: lat_copy(b, m, d).start())

    def await_edges(b, m):
        @pl.when(m == 0)
        def _():
            for d in range(2):
                guarded(lev_sides[d][0], lambda d=d: lev_arrival(b, d).wait_recv())

        for d in range(2):
            guarded(lat_sides[d][0], lambda d=d: lat_arrival(b, m, d).wait_recv())
        for d in range(2):
            lon_arrival(b, m, d).wait_recv()

    members = ((0, 0), (0, 1), (1, 0), (1, 1))

    def to_spectrum(g, carry):
        packed = Packed()
        for mm, s in members:
            l = level_of(2 * g + mm, s)
            at = pl.multiple_of(l * 8, 8)
            r = [rr[n, pl.ds(at, 8), :] for n in range(steps)]
            for n in range(2, steps, 2):
                r[n] = r[n] + ur[n // 2 - 1, l] * gamma[n]
            e = [r[0]] + [r[n] + r[steps - n] for n in range(1, half)] + [r[half]]
            o = [r[n] - r[steps - n] for n in range(1, half)]
            real = cosine_sums(e, steps)
            imag = sine_sums(o, steps)
            for k in range(half):
                spec[pl.ds(l * 128 + k, 8, stride=16), :] = real[k]
            spec[pl.ds(l * 128 + 8, 8, stride=16), :] = real[half]
            for k in range(1, half):
                spec[pl.ds(l * 128 + 8 + k, 8, stride=16), :] = -imag[k - 1]
        for p, (mm, s) in enumerate(members):
            m = 2 * g + mm
            l = level_of(m, s)
            for a in range(AP):
                row = pl.multiple_of((l * 8 + a) * 16, 8)
                x = divide(l, a, spec[pl.ds(row, 8), :], spec[pl.ds(row + 8, 8), :])
                for f in range(2):
                    xe[0, sent_index(m, s), a + 1, pl.ds(8 * f, 8), :] = x[f]
                    packed.add(p, a, f, x[f])
        send_edges(0, g, packed)
        return carry

    lax.fori_loop(0, GROUPS, to_spectrum, 0)

    def back_copy(to, first, count):
        part = pl.ds(pl.multiple_of(first, 8), count)
        return remote(ws.at[to, part], wb.at[me, part], back_s.at[to], back_r.at[me], {"tm": to})

    def from_spectrum(g, p):
        base = p * 128
        x = [xf[pl.ds(base + k, 8, stride=16), :] for k in range(half)]
        x_half = xf[pl.ds(base + 8, 8, stride=16), :]
        y = [xf[pl.ds(base + 8 + k, 8, stride=16), :] for k in range(1, half)]
        even = cosine_sums([x[0] * 0.5] + x[1:] + [x_half * 0.5], steps)
        odd = sine_sums(y, steps)
        at = pl.ds(pl.multiple_of(g * 32, 8) + p * 8, 8)
        ws[0, at, :] = even[0]
        ws[half, at, :] = even[half]
        for n in range(1, half):
            ws[n, at, :] = even[n] - odd[n - 1]
            ws[steps - n, at, :] = even[n] + odd[n - 1]

    def sweep(b, last):
        def some_pairs(g, carry):
            await_edges(b, g)
            ends = jnp.where(odd_lane, edge_in[b, g, 1], edge_in[b, g, 0])
            packed = Packed()
            for p, (mm, s) in enumerate(members):
                m = 2 * g + mm
                l = level_of(m, s)
                i = sent_index(m, s)
                beyond = (i - 2, inner_index(m, s))
                under, over = beyond if s == 0 else beyond[::-1]
                for a in range(AP):
                    w = [
                        jnp.broadcast_to(wts[f, pl.ds(l * NA + q * 8 + a, 1), :], (8, NX)) for f in range(6)
                    ]
                    row = pl.multiple_of((l * 8 + a) * 16, 8)
                    rhs = []
                    for f in range(2):
                        part = pl.ds(8 * f, 8)
                        j = (p * AP + a) * 2 + f
                        x = xe[b, i, a + 1, part, :]
                        halo = pltpu.roll(ends, NX - 1 - 2 * j, 1)
                        total = spec[pl.ds(row + 8 * f, 8), :]
                        total = total + w[0] * xe[b, under, a + 1, part, :] + w[1] * xe[b, over, a + 1, part, :]
                        total = total + w[2] * xe[b, i, a, part, :] + w[3] * xe[b, i, a + 2, part, :]
                        total = total + w[4] * pltpu.roll(jnp.where(last_lane, halo, x), 1, 1)
                        total = total + w[5] * pltpu.roll(jnp.where(first_lane, halo, x), NX - 1, 1)
                        rhs.append(total)
                    x = divide(l, a, rhs[0], rhs[1])
                    for f in range(2):
                        if last:
                            xf[pl.ds((p * AP + a) * 16 + 8 * f, 8), :] = x[f]
                        else:
                            xe[b + 1, i, a + 1, pl.ds(8 * f, 8), :] = x[f]
                            packed.add(p, a, f, x[f])
            if not last:
                send_edges(b + 1, g, packed)
            else:
                for p in range(4):
                    from_spectrum(g, p)

                def send(i, carry):
                    odd = lax.rem(i, 2)
                    d = half + (1 - odd) * lax.div(i, 2) - odd * lax.div(i + 1, 2)
                    back_copy(lax.rem(me + d, steps), g * 32, 32).start()
                    return carry

                lax.fori_loop(0, steps - 1, send, 0)
            return carry

        lax.fori_loop(0, GROUPS, some_pairs, 0)

    for b in range(SWEEPS):
        sweep(b, b == SWEEPS - 1)

    wb[me] = ws[me]
    share = pick(me, [2.0 / (steps * g) for g in gamma])

    def finish(i, carry):
        odd = lax.rem(i, 2)
        away = lax.div(i + 1, 2)
        src = lax.rem(me + steps + odd * away - (1 - odd) * away, steps)
        zz = lax.div(src, 2)
        part = lax.rem(lax.rem(src, 2) + lat, 2)

        @pl.when(i > 0)
        def _():
            remote(ws.at[src], wb.at[src], back_s.at[src], back_r.at[src], {"tm": src}).wait_recv()

        for m in range(LP // 2):
            for s in range(2):
                at = pl.multiple_of((zz * LP + level_of(m, s)) * NA + part * 8, 8)
                out_ref[pl.ds(at, 8), :] = u_ref[pl.ds(at, 8), :] + wb[src, pl.ds(m * 16 + s * 8, 8), :] * share
        return carry

    lax.fori_loop(0, steps, finish, 0)

    @pl.when(xl == 0)
    def _():
        for i in range(zs):
            shift_copy(i).wait_send()

    for d in range(4):
        guarded(sides[d][0], lambda d=d: side_copy(d).wait_send())

    def sent(d, carry):
        to = lax.rem(me + d, steps)
        fwd_copy(0, 0, to).wait_send()
        back_copy(to, 0, 64).wait_send()
        return carry

    lax.fori_loop(1, steps, sent, 0)

    @pl.when(sends_state)
    def _():
        for i in range(zs - 1):
            forward_copy(i).wait_send()

    @pl.when(jnp.logical_and(xl == 1, sends_state))
    def _():
        for i in range(zs):
            relay_copy(i).wait_send()

    for b in range(SWEEPS):
        for d in range(2):
            guarded(lev_sides[d][0], lambda b=b, d=d: lev_copy(b, d).wait_send())

        def edges_sent(m, carry, b=b):
            for d in range(2):
                guarded(lat_sides[d][0], lambda d=d: lat_copy(b, m, d).wait_send())
                lon_copy(b, m, d).wait_send()
            return carry

        lax.fori_loop(0, GROUPS, edges_sent, 0)


def on_device(steps, nlat, nlon, iterate, heating, initial, region, cond_table):
    levels = initial.shape[0]
    rows = levels * NA
    zs = steps // 2
    groups = (levels + 31) // 32
    vmem = pl.BlockSpec(memory_space=pltpu.VMEM)
    anywhere = pl.BlockSpec(memory_space=pl.ANY)
    flat = lambda value: value.reshape(rows, NX)
    dma = pltpu.SemaphoreType.DMA
    out = pl.pallas_call(
        functools.partial(kernel, steps, nlat, nlon),
        out_shape=jax.ShapeDtypeStruct((rows, NX), F32),
        in_specs=[anywhere] * 6,
        out_specs=vmem,
        scratch_shapes=[
            pltpu.SMEM(cond_table.shape, F32),
            pltpu.VMEM((rows, NX), F32),
            pltpu.VMEM((rows, NX), F32),
            pltpu.VMEM((rows, NX), jnp.int32),
            pltpu.VMEM((rows + 2 * NA, NX), F32),
            pltpu.VMEM((6, LP * NA, NX), F32),
            pltpu.VMEM((rows, NX), F32),
            pltpu.VMEM((2, 2 * levels, NX), F32),
            pltpu.VMEM((2, 2 * levels, NX), F32),
            pltpu.VMEM((groups, 2, 8, NX), F32),
            pltpu.VMEM((2, groups, 2, 8, NX), F32),
            pltpu.VMEM((groups, 2, 8, NX), F32),
            pltpu.VMEM((2, levels * 8, NX), F32),
            pltpu.VMEM((steps, 64, NX), F32),
            pltpu.VMEM((zs, LP, 8, NX), F32),
            pltpu.VMEM((zs, LP, 8, NX), F32),
            pltpu.VMEM((64 * 16, NX), F32),
            pltpu.VMEM((64 * 24, NX), F32),
            pltpu.VMEM((SWEEPS, LP + 2, AP + 2, 16, NX), F32),
            pltpu.VMEM((32 * 16, NX), F32),
            pltpu.VMEM((SWEEPS, GROUPS, 8, NX), F32),
            pltpu.VMEM((SWEEPS, GROUPS, 2, 8, NX), F32),
            pltpu.VMEM((steps, 64, NX), F32),
            pltpu.VMEM((steps, 64, NX), F32),
            dma((5,)),
            dma((zs,)),
            dma((zs,)),
            dma((4,)),
            dma((4,)),
            dma((zs,)),
            dma((zs,)),
            dma((zs,)),
            dma((zs,)),
            dma((steps,)),
            dma((steps,)),
            dma((SWEEPS, 2)),
            dma((SWEEPS, 2)),
            dma((SWEEPS, GROUPS, 2)),
            dma((SWEEPS, GROUPS, 2)),
            dma((SWEEPS, GROUPS, 2)),
            dma((SWEEPS, GROUPS, 2)),
            dma((steps,)),
            dma((steps,)),
        ],
        compiler_params=pltpu.CompilerParams(
            collective_id=0, has_side_effects=True, vmem_limit_bytes=VMEM_LIMIT
        ),
    )(*(
        pltpu.with_memory_space_constraint(value, pltpu.HBM)
        for value in (
            flat(iterate), iterate.reshape(levels, 2, AP, NX), flat(heating), flat(region), flat(initial), cond_table
        )
    ))
    return out.reshape(iterate.shape)


def solution(mesh):
    sizes = mesh.shape
    return jax.shard_map(
        functools.partial(on_device, sizes["tm"], sizes["lat"], sizes["lon"]),
        mesh=mesh,
        in_specs=(
            P("tm", None, "lat", "lon"),
            P("tm", None, "lat", "lon"),
            P(None, "lat", "lon"),
            P(None, "lat", "lon"),
            P(),
        ),
        out_specs=P("tm", None, "lat", "lon"),
        check_vma=False,
    )
```

```python
import functools
import math

import jax
import jax.numpy as jnp
from jax import lax
from jax.experimental import pallas as pl
from jax.experimental.pallas import tpu as pltpu
from jax.sharding import PartitionSpec as P

MESH = pl.DeviceIdType.MESH
F32 = jnp.float32
CORNER = 0.1
SWEEPS = 3
LP = 8
GROUPS = 2
AP = 8
NA = 16
NX = 128
VMEM_LIMIT = 40 * 1024 * 1024


def harmonic(first, second):
    return 2.0 * first * second / (first + second)


def weighted(pairs):
    total = None
    for coefficient, value in pairs:
        if abs(coefficient) < 1e-12:
            continue
        if abs(coefficient - 1.0) < 1e-12:
            term = value
        elif abs(coefficient + 1.0) < 1e-12:
            total = -value if total is None else total - value
            continue
        else:
            term = value * coefficient
        total = term if total is None else total + term
    return total


def cosine_sums(e, n):
    half, quarter = n // 2, n // 4
    even = [e[m] + e[half - m] for m in range(quarter)]
    odd = [e[m] - e[half - m] for m in range(quarter)]
    out = []
    for k in range(half + 1):
        parts = even if k % 2 == 0 else odd
        pairs = [(math.cos(2 * math.pi * k * m / n), parts[m]) for m in range(quarter)]
        pairs.append((math.cos(2 * math.pi * k * quarter / n), e[quarter]))
        out.append(weighted(pairs))
    return out


def sine_sums(o, n):
    half, quarter = n // 2, n // 4
    plus = [o[m - 1] + o[half - m - 1] for m in range(1, quarter)]
    minus = [o[m - 1] - o[half - m - 1] for m in range(1, quarter)]
    out = []
    for k in range(1, half):
        parts = plus if k % 2 == 1 else minus
        pairs = [(math.sin(2 * math.pi * k * m / n), parts[m - 1]) for m in range(1, quarter)]
        pairs.append((math.sin(2 * math.pi * k * quarter / n), o[quarter - 1]))
        total = weighted(pairs)
        out.append(total if total is not None else jnp.zeros_like(o[0]))
    return out


def pick(index, values):
    chosen = jnp.float32(values[0])
    for i, value in enumerate(values):
        if i > 0:
            chosen = jnp.where(index == i, jnp.float32(value), chosen)
    return chosen


def kernel(
    steps, nlat, nlon,
    u_hbm, u_parts, h_hbm, reg_hbm, init_hbm, table_hbm, out_ref,
    table_ref, u_ref, h_ref, reg_ref, kap, wts, own, pbuf, lat_out, lat_in, lon_out, lon_in, lon_mix,
    rs, rr, ur, relay, spec, coef, xe0, xe1, xe2, xf, edge_out, edge_in, ws, wb,
    local, shift_s, shift_r, side_s, side_r, relay_s, relay_r, state_s, state_r, fwd_s, fwd_r,
    lev_s, lev_r, lat_s, lat_r, lon_s, lon_r, back_s, back_r,
):
    levels = u_ref.shape[0] // NA
    xe = (xe0, xe1, xe2)
    zs = steps // 2
    half = steps // 2
    me = lax.axis_index("tm")
    lat = lax.axis_index("lat")
    lon = lax.axis_index("lon")
    z = lax.div(me, 2)
    xl = lax.rem(me, 2)
    q = lax.rem(xl + lat, 2)
    left = lax.rem(lon + nlon - 1, nlon)
    right = lax.rem(lon + 1, nlon)
    sub = lax.broadcasted_iota(jnp.int32, (8, NX), 0)
    lane = lax.broadcasted_iota(jnp.int32, (8, NX), 1)
    lane_pair = lax.div(lane, 2)
    odd_lane = lax.rem(lane, 2) == 1
    first_lane = lane == 0
    last_lane = lane == NX - 1
    zero = jnp.zeros((8, NX), F32)

    def remote(src, dst, send, recv, device):
        return pltpu.make_async_remote_copy(
            src_ref=src, dst_ref=dst, send_sem=send, recv_sem=recv, device_id=device, device_id_type=MESH
        )

    def guarded(condition, act):
        if condition is None:
            act()
        else:
            pl.when(condition)(act)

    sides = (
        (lat > 0, {"lat": lat - 1}),
        (lat < nlat - 1, {"lat": lat + 1}),
        (None, {"lon": left}),
        (None, {"lon": right}),
    )
    x_low = xl * (1 - q) + (1 - xl) * q
    x_high = xl * q + (1 - xl) * (1 - q)
    lev_sides = ((z > 0, {"tm": me - 2}), (z < zs - 1, {"tm": me + 2}))
    lat_sides = (
        (q + lat > 0, {"tm": z * 2 + x_low, "lat": lat - (1 - q)}),
        ((1 - q) + (nlat - 1 - lat) > 0, {"tm": z * 2 + x_high, "lat": lat + q}),
    )
    lon_sides = ((None, {"lon": left}), (None, {"lon": right}))

    barrier = pltpu.get_barrier_semaphore()
    for d in range(1, steps):
        pl.semaphore_signal(barrier, inc=1, device_id={"tm": lax.rem(me + d, steps)}, device_id_type=MESH)
    for condition, device in sides:
        guarded(
            condition,
            functools.partial(pl.semaphore_signal, barrier, inc=1, device_id=device, device_id_type=MESH),
        )

    take_reg = pltpu.make_async_copy(reg_hbm, reg_ref, local.at[0])
    take_u = pltpu.make_async_copy(u_hbm, u_ref, local.at[1])
    take_h = pltpu.make_async_copy(h_hbm, h_ref, local.at[2])
    take_init = pltpu.make_async_copy(init_hbm, pbuf, local.at[3])
    take_table = pltpu.make_async_copy(table_hbm, table_ref, local.at[4])
    take_table.start()
    take_reg.start()
    take_u.start()
    take_h.start()

    @pl.when(me == 0)
    def _():
        take_init.start()

    for b in range(SWEEPS):
        for condition, place in (
            (z == 0, (b, 0, slice(None))),
            (z == zs - 1, (b, 1, slice(None))),
            (q + lat == 0, (b, slice(None), 0)),
            ((1 - q) + (nlat - 1 - lat) == 0, (b, slice(None), AP + 1)),
        ):
            def clear(place=place):
                xe[place[0]][place[1:]] = jnp.zeros((10, 16, NX), F32)

            pl.when(condition)(clear)

    @pl.when(lat == 0)
    def _():
        lat_in[0] = jnp.zeros(lat_in.shape[1:], F32)

    @pl.when(lat == nlat - 1)
    def _():
        lat_in[1] = jnp.zeros(lat_in.shape[1:], F32)

    @pl.when(jnp.logical_and(me > 0, xl == 0))
    def _():
        pbuf[...] = jnp.zeros(pbuf.shape, F32)

    kap[pl.ds(0, NA), :] = jnp.zeros((NA, NX), F32)
    kap[pl.ds((levels + 1) * NA, NA), :] = jnp.zeros((NA, NX), F32)
    take_table.wait()
    table = [table_ref[c] for c in range(8)]
    take_reg.wait()
    take_u.wait()

    for group in range((levels + 31) // 32):
        def conduct(g, packs):
            gathered = [zero, zero]
            for j in range(16):
                at = pl.multiple_of((group * 4 + g) * 128, 8) + j * 8
                reg = reg_ref[pl.ds(at, 8), :]
                k = jnp.full((8, NX), table[0], F32)
                for c in range(1, 8):
                    k = jnp.where(reg == c, table[c], k)
                kap[pl.ds(at + NA, 8), :] = k
                u = u_ref[pl.ds(at, 8), :]
                for f, tile in ((0, u), (1, k)):
                    gathered[f] = jnp.where(lane_pair == j, pltpu.roll(tile, 2 * j + 1, 1), gathered[f])
            mask = lax.div(lane, 32) == g
            return tuple(jnp.where(mask, pltpu.roll(gathered[f], g * 32, 1), packs[f]) for f in range(2))

        packs = lax.fori_loop(0, min(4, levels // 8 - 4 * group), conduct, (zero, zero))
        for f in range(2):
            lon_out[group, f] = packs[f]
    for g in range(zs):
        e = lax.rem(g + zs - z, zs) - zs // 2
        at = pl.multiple_of(jnp.where(e < 0, -2 * e - 1, 2 * e) * 16, 8)
        for side, row in ((0, 0), (1, NA - 1)):
            lat_out[side, pl.ds(at, 8), :] = u_ref[pl.ds(g * 128 + row, 8, stride=NA), :]
            lat_out[side, pl.ds(at + 8, 8), :] = kap[pl.ds(NA + g * 128 + row, 8, stride=NA), :]

    lat_count = jnp.where(lat > 0, 1, 0) + jnp.where(lat < nlat - 1, 1, 0)
    pl.semaphore_wait(barrier, steps - 1 + 2 + lat_count)

    def lat_rows(d):
        return pl.ds(0, 16) if d < 2 else pl.ds(16, 2 * levels - 16)

    def side_copy(d):
        if d in (2, 3):
            return remote(lon_out, lon_in.at[3 - d], side_s.at[d], side_r.at[5 - d], sides[d][1])
        e = d % 2
        return remote(
            lat_out.at[e, lat_rows(d)], lat_in.at[1 - e, lat_rows(d)], side_s.at[d], side_r.at[d + 1 - 2 * e], sides[e][1]
        )

    def side_arrival(d):
        if d in (2, 3):
            return remote(lon_out, lon_in.at[d - 2], side_s.at[d], side_r.at[d], sides[d][1])
        e = d % 2
        return remote(lat_out.at[e, lat_rows(d)], lat_in.at[e, lat_rows(d)], side_s.at[d], side_r.at[d], sides[e][1])

    def side_there(d):
        return None if d in (2, 3) else sides[d % 2][0]

    for d in (2, 3, 0, 1, 4, 5):
        guarded(side_there(d), lambda d=d: side_copy(d).start())

    def order(i, at):
        odd = lax.rem(i, 2)
        away = zs // 2 + (1 - odd) * lax.div(i, 2) - odd * lax.div(i + 1, 2)
        return lax.rem(at + away, zs)

    rows = LP * NA

    def shift_copy(i):
        part = pl.ds(pl.multiple_of(order(i, z) * rows, 8), rows)
        return remote(u_hbm.at[part, :], pbuf.at[part, :], shift_s.at[i], shift_r.at[i], {"tm": me + 1 - 2 * xl})

    @pl.when(xl == 0)
    def _():
        for i in range(zs):
            shift_copy(i).start()

    sends_state = z < zs - 1
    relayed = min(4, zs // 2 + 0)

    def state_parts(i, x):
        return u_parts.at[pl.ds(order(i, z) * LP, LP), lax.rem(x + lat, 2)]

    def relay_copy(i):
        return remote(state_parts(i, 0), relay.at[i], relay_s.at[i], relay_r.at[i], {"tm": me + 1 - 2 * xl})

    def state_copy(i):
        to = order(i, z) * 2 + 1
        return remote(state_parts(i, 1), ur.at[z], state_s.at[i], state_r.at[z], {"tm": to})

    def direct_copy(i):
        return remote(state_parts(i, 0), ur.at[z], relay_s.at[i], state_r.at[z], {"tm": order(i, z) * 2})

    def forward_copy(i):
        return remote(relay.at[i], ur.at[z], state_s.at[i], state_r.at[z], {"tm": order(i, z) * 2})

    @pl.when(jnp.logical_and(xl == 1, sends_state))
    def _():
        for i in range(zs):
            if i < relayed:
                relay_copy(i).start()
            if i < zs - 1:
                state_copy(i).start()
            if i >= relayed:
                direct_copy(i).start()
        for l in range(LP):
            row = pl.multiple_of((z * LP + l) * NA + q * 8, 8)
            ur[z, l] = u_ref[pl.ds(row, 8), :]

    forwards = jnp.logical_and(xl == 0, sends_state)

    @pl.when(forwards)
    def _():
        for i in range(relayed):
            relay_copy(i).wait_recv()
            forward_copy(i).start()

    take_h.wait()

    @pl.when(me == 0)
    def _():
        take_init.wait()

    for d in range(4):
        guarded(side_there(d), lambda d=d: side_arrival(d).wait_recv())
    for group in range((levels + 31) // 32):
        for f in range(2):
            lon_mix[group, f] = jnp.where(odd_lane, lon_in[1, group, f], lon_in[0, group, f])

    gamma = [CORNER ** (n / steps) for n in range(steps)]
    scale = pick(me, gamma)

    def fwd_copy(part, zd, to):
        return remote(
            rs.at[part, pl.ds(pl.multiple_of(zd * 64, 8), 64), :], rr.at[me], fwd_s.at[to], fwd_r.at[me], {"tm": to}
        )

    def chunk(i, carry):
        zd = order(i, z)

        @pl.when(i == 1)
        def _():
            for d in (4, 5):
                guarded(side_there(d), lambda d=d: side_arrival(d).wait_recv())

        @pl.when(xl == 1)
        def _():
            shift_copy(i).wait_recv()

        def level(l):
            lev = zd * LP + l
            base = pl.multiple_of(lev * NA, 8)
            under = pl.multiple_of(jnp.maximum(lev - 1, 0) * NA, 8)
            over = pl.multiple_of(jnp.minimum(lev + 1, levels - 1) * NA, 8)
            group = lax.div(lev, 32)
            fields = []
            for f, ref, low, mid, high in (
                (0, u_ref, under, base, over),
                (1, kap, base, base + NA, base + 2 * NA),
            ):
                tile = [ref[pl.ds(mid + 8 * t, 8), :] for t in range(2)]
                down = [ref[pl.ds(low + 8 * t, 8), :] for t in range(2)]
                up = [ref[pl.ds(high + 8 * t, 8), :] for t in range(2)]
                row = [
                    jnp.broadcast_to(lat_in[s, pl.ds(i * 16 + f * 8 + l, 1), :], (8, NX)) for s in range(2)
                ]
                one = [pltpu.roll(tile[t], 1, 0) for t in range(2)]
                seven = [pltpu.roll(tile[t], 7, 0) for t in range(2)]
                before = [jnp.where(sub == 0, row[0], one[0]), jnp.where(sub == 0, one[0], one[1])]
                after = [jnp.where(sub == 7, seven[1], seven[0]), jnp.where(sub == 7, row[1], seven[1])]
                ends = lon_mix[group, f]
                west, east = [], []
                for t in range(2):
                    halo = pltpu.roll(ends, NX - 1 - 2 * (lax.rem(lev, 32) * 2 + t), 1)
                    west.append(pltpu.roll(jnp.where(last_lane, halo, tile[t]), 1, 1))
                    east.append(pltpu.roll(jnp.where(first_lane, halo, tile[t]), NX - 1, 1))
                fields.append((tile, (down, up, before, after, west, east)))
            (u, u_near), (k, k_near) = fields
            for t in range(2):
                at = pl.multiple_of(l * NA, 8) + 8 * t
                total = None
                for f in range(6):
                    w = harmonic(k[t], k_near[f][t])
                    wts[f, pl.ds(at, 8), :] = w
                    term = w * (u_near[f][t] - u[t])
                    total = term if total is None else total + term
                r = (h_ref[pl.ds(base + 8 * t, 8), :] + pbuf[pl.ds(base + 8 * t, 8), :]) - (u[t] - total)
                rs[t, pl.ds(pl.multiple_of(lev * 8, 8), 8), :] = r * scale

        def some_levels(m, carry):
            for l in range(4):
                level(m * 4 + l)
            return carry

        lax.fori_loop(0, LP // 4, some_levels, 0)
        for part in range(2):
            to = zd * 2 + lax.rem(part + lat, 2)

            @pl.when(to != me)
            def _():
                fwd_copy(part, zd, to).start()

            @pl.when(to == me)
            def _():
                rr[me] = rs[part, pl.ds(pl.multiple_of(zd * 64, 8), 64), :]

        return carry

    lax.fori_loop(0, zs, chunk, 0)

    beta = CORNER ** (1.0 / steps)
    shift_re = [1.0 - beta * math.cos(2 * math.pi * k / steps) for k in range(half + 1)]
    shift_im = [beta * math.sin(2 * math.pi * k / steps) for k in range(half + 1)]

    def invert(l, carry):
        at = pl.multiple_of(l * NA + q * 8, 8)
        total = None
        for f in range(6):
            w = wts[f, pl.ds(at, 8), :]
            own[f, l] = w
            total = w if total is None else total + w
        for k in range(half + 1):
            re = total + shift_re[k]
            if k in (0, half):
                value = 1.0 / re
                row = 0 if k == 0 else 8
                coef[pl.ds(l * 192 + row, 8, stride=24), :] = value
                if k == 0:
                    coef[pl.ds(l * 192 + 16, 8, stride=24), :] = zero
            else:
                share = 1.0 / (re * re + shift_im[k] * shift_im[k])
                real = re * share
                coef[pl.ds(l * 192 + k, 8, stride=24), :] = real
                coef[pl.ds(l * 192 + 8 + k, 8, stride=24), :] = real
                coef[pl.ds(l * 192 + 16 + k, 8, stride=24), :] = share * (-shift_im[k])
        return carry

    lax.fori_loop(0, LP, invert, 0)

    def await_fwd(d, carry):
        src = lax.rem(me + d, steps)
        remote(rs.at[0, pl.ds(0, 64), :], rr.at[src], fwd_s.at[src], fwd_r.at[src], {"tm": src}).wait_recv()
        return carry

    lax.fori_loop(1, steps, await_fwd, 0)
    for i in range(zs - 1):

        @pl.when(jnp.logical_or(z != i, xl == 0))
        def _():
            remote(relay.at[0], ur.at[i], state_s.at[i], state_r.at[i], {"tm": 2 * i + xl}).wait_recv()

    def sent_index(m, s):
        return 2 + 2 * m + s

    def inner_index(m, s):
        return jnp.where(m == LP // 2 - 1, LP + 1 - s, 4 + 2 * m + s)

    def level_of(m, s):
        return m + s * (LP - 1 - 2 * m)

    def divide(l, a, re, im):
        at = pl.multiple_of((l * 8 + a) * 24, 8)
        c_re, c_im, cross = (coef[pl.ds(at + 8 * i, 8), :] for i in range(3))
        return re * c_re - im * cross, im * c_im + re * cross

    class Packed:
        def __init__(self):
            self.parts = [zero, zero]

        def add(self, p, a, f, tile):
            j = (p * AP + a) * 2 + f
            self.parts[f] = jnp.where(lane_pair == j, pltpu.roll(tile, 2 * j + 1, 1), self.parts[f])

        def value(self):
            return jnp.where(lax.rem(lane_pair, 2) == 0, self.parts[0], self.parts[1])

    inner = pl.ds(1, AP)

    def lev_copy(b, d):
        return remote(
            xe[b].at[2 + d, inner], xe[b].at[1 - d, inner], lev_s.at[b, d], lev_r.at[b, 1 - d], lev_sides[d][1]
        )

    def lev_arrival(b, d):
        return remote(xe[b].at[2 + d, inner], xe[b].at[d, inner], lev_s.at[b, d], lev_r.at[b, d], lev_sides[d][1])

    def lat_copy(b, m, d):
        pair = pl.ds(2 + 4 * m, 4)
        return remote(
            xe[b].at[pair, 1 + d * (AP - 1)], xe[b].at[pair, (1 - d) * (AP + 1)],
            lat_s.at[b, m, d], lat_r.at[b, m, 1 - d], lat_sides[d][1],
        )

    def lat_arrival(b, m, d):
        pair = pl.ds(2 + 4 * m, 4)
        return remote(
            xe[b].at[pair, 1 + d * (AP - 1)], xe[b].at[pair, d * (AP + 1)],
            lat_s.at[b, m, d], lat_r.at[b, m, d], lat_sides[d][1],
        )

    def lon_copy(b, m, d):
        return remote(
            edge_out.at[b, m], edge_in.at[b, m, 1 - d], lon_s.at[b, m, d], lon_r.at[b, m, 1 - d], lon_sides[d][1]
        )

    def lon_arrival(b, m, d):
        return remote(edge_out.at[b, m], edge_in.at[b, m, d], lon_s.at[b, m, d], lon_r.at[b, m, d], lon_sides[d][1])

    def send_edges(b, m, packed):
        edge_out[b, m] = packed.value()

        for d in range(2):
            lon_copy(b, m, d).start()
        for d in range(2):
            guarded(lat_sides[d][0], lambda d=d: lat_copy(b, m, d).start())

    def send_levels(b, m):
        @pl.when(m == 0)
        def _():
            for d in range(2):
                guarded(lev_sides[d][0], lambda d=d: lev_copy(b, d).start())

    def await_edges(b, m):
        @pl.when(m == 0)
        def _():
            for d in range(2):
                guarded(lev_sides[d][0], lambda d=d: lev_arrival(b, d).wait_recv())

        for d in range(2):
            guarded(lat_sides[d][0], lambda d=d: lat_arrival(b, m, d).wait_recv())
        for d in range(2):
            lon_arrival(b, m, d).wait_recv()

    members = ((0, 0), (0, 1), (1, 0), (1, 1))

    def to_spectrum(g, carry):
        packed = Packed()
        for mm, s in members:
            l = level_of(2 * g + mm, s)
            at = pl.multiple_of(l * 8, 8)
            r = [rr[n, pl.ds(at, 8), :] for n in range(steps)]
            for n in range(2, steps, 2):
                r[n] = r[n] + ur[n // 2 - 1, l] * gamma[n]
            e = [r[0]] + [r[n] + r[steps - n] for n in range(1, half)] + [r[half]]
            o = [r[n] - r[steps - n] for n in range(1, half)]
            real = cosine_sums(e, steps)
            imag = sine_sums(o, steps)
            for k in range(half):
                spec[pl.ds(l * 128 + k, 8, stride=16), :] = real[k]
            spec[pl.ds(l * 128 + 8, 8, stride=16), :] = real[half]
            for k in range(1, half):
                spec[pl.ds(l * 128 + 8 + k, 8, stride=16), :] = -imag[k - 1]
        for p, (mm, s) in enumerate(members):
            m = 2 * g + mm
            l = level_of(m, s)
            for a in range(AP):
                row = pl.multiple_of((l * 8 + a) * 16, 8)
                x = divide(l, a, spec[pl.ds(row, 8), :], spec[pl.ds(row + 8, 8), :])
                for f in range(2):
                    xe[0][sent_index(m, s), a + 1, pl.ds(8 * f, 8), :] = x[f]
                    packed.add(p, a, f, x[f])
            if p == 1:
                send_levels(0, g)
        send_edges(0, g, packed)
        return carry

    lax.fori_loop(0, GROUPS, to_spectrum, 0)

    def back_copy(to, first, count):
        part = pl.ds(pl.multiple_of(first, 8), count)
        return remote(ws.at[to, part], wb.at[me, part], back_s.at[to], back_r.at[me], {"tm": to})

    def from_spectrum(g, p):
        base = p * 128
        x = [xf[pl.ds(base + k, 8, stride=16), :] for k in range(half)]
        x_half = xf[pl.ds(base + 8, 8, stride=16), :]
        y = [xf[pl.ds(base + 8 + k, 8, stride=16), :] for k in range(1, half)]
        even = cosine_sums([x[0] * 0.5] + x[1:] + [x_half * 0.5], steps)
        odd = sine_sums(y, steps)
        at = pl.ds(pl.multiple_of(g * 32, 8) + p * 8, 8)
        ws[0, at, :] = even[0]
        ws[half, at, :] = even[half]
        for n in range(1, half):
            ws[n, at, :] = even[n] - odd[n - 1]
            ws[steps - n, at, :] = even[n] + odd[n - 1]

    def sweep(b, last):
        def some_pairs(g, carry):
            await_edges(b, g)
            ends = jnp.where(odd_lane, edge_in[b, g, 1], edge_in[b, g, 0])
            packed = Packed()
            for p, (mm, s) in enumerate(members):
                m = 2 * g + mm
                l = level_of(m, s)
                i = sent_index(m, s)
                beyond = (i - 2, inner_index(m, s))
                under, over = beyond if s == 0 else beyond[::-1]
                for a in range(AP):
                    w = [
                        jnp.broadcast_to(own[f, l, pl.ds(a, 1), :], (8, NX)) for f in range(6)
                    ]
                    row = pl.multiple_of((l * 8 + a) * 16, 8)
                    rhs = []
                    for f in range(2):
                        part = pl.ds(8 * f, 8)
                        j = (p * AP + a) * 2 + f
                        x = xe[b][i, a + 1, part, :]
                        halo = pltpu.roll(ends, NX - 1 - 2 * j, 1)
                        total = spec[pl.ds(row + 8 * f, 8), :]
                        total = total + w[0] * xe[b][under, a + 1, part, :] + w[1] * xe[b][over, a + 1, part, :]
                        total = total + w[2] * xe[b][i, a, part, :] + w[3] * xe[b][i, a + 2, part, :]
                        total = total + w[4] * pltpu.roll(jnp.where(last_lane, halo, x), 1, 1)
                        total = total + w[5] * pltpu.roll(jnp.where(first_lane, halo, x), NX - 1, 1)
                        rhs.append(total)
                    x = divide(l, a, rhs[0], rhs[1])
                    for f in range(2):
                        if last:
                            xf[pl.ds((p * AP + a) * 16 + 8 * f, 8), :] = x[f]
                        else:
                            xe[b + 1][i, a + 1, pl.ds(8 * f, 8), :] = x[f]
                            packed.add(p, a, f, x[f])
                if p == 1 and not last:
                    send_levels(b + 1, g)
            if not last:
                send_edges(b + 1, g, packed)
            else:
                for p in range(4):
                    from_spectrum(g, p)

                def send(i, carry):
                    odd = lax.rem(i, 2)
                    d = half + (1 - odd) * lax.div(i, 2) - odd * lax.div(i + 1, 2)
                    back_copy(lax.rem(me + d, steps), g * 32, 32).start()
                    return carry

                lax.fori_loop(0, steps - 1, send, 0)
            return carry

        lax.fori_loop(0, GROUPS, some_pairs, 0)

    for b in range(SWEEPS):
        sweep(b, b == SWEEPS - 1)

    wb[me] = ws[me]
    share = pick(me, [2.0 / (steps * g) for g in gamma])

    def finish(i, carry):
        odd = lax.rem(i, 2)
        away = lax.div(i + 1, 2)
        src = lax.rem(me + steps + odd * away - (1 - odd) * away, steps)
        zz = lax.div(src, 2)
        part = lax.rem(lax.rem(src, 2) + lat, 2)

        @pl.when(i > 0)
        def _():
            remote(ws.at[src], wb.at[src], back_s.at[src], back_r.at[src], {"tm": src}).wait_recv()

        for m in range(LP // 2):
            for s in range(2):
                at = pl.multiple_of((zz * LP + level_of(m, s)) * NA + part * 8, 8)
                out_ref[pl.ds(at, 8), :] = u_ref[pl.ds(at, 8), :] + wb[src, pl.ds(m * 16 + s * 8, 8), :] * share
        return carry

    lax.fori_loop(0, steps, finish, 0)

    @pl.when(xl == 0)
    def _():
        for i in range(zs):
            shift_copy(i).wait_send()

    for d in range(6):
        guarded(side_there(d), lambda d=d: side_copy(d).wait_send())

    def sent(d, carry):
        to = lax.rem(me + d, steps)
        fwd_copy(0, 0, to).wait_send()
        back_copy(to, 0, 64).wait_send()
        return carry

    lax.fori_loop(1, steps, sent, 0)

    @pl.when(forwards)
    def _():
        for i in range(relayed):
            forward_copy(i).wait_send()

    @pl.when(jnp.logical_and(xl == 1, sends_state))
    def _():
        for i in range(zs):
            relay_copy(i).wait_send()
            if i < zs - 1:
                state_copy(i).wait_send()

    for b in range(SWEEPS):
        for d in range(2):
            guarded(lev_sides[d][0], lambda b=b, d=d: lev_copy(b, d).wait_send())

        def edges_sent(m, carry, b=b):
            for d in range(2):
                guarded(lat_sides[d][0], lambda d=d: lat_copy(b, m, d).wait_send())
                lon_copy(b, m, d).wait_send()
            return carry

        lax.fori_loop(0, GROUPS, edges_sent, 0)


def on_device(steps, nlat, nlon, iterate, heating, initial, region, cond_table):
    levels = initial.shape[0]
    rows = levels * NA
    zs = steps // 2
    groups = (levels + 31) // 32
    vmem = pl.BlockSpec(memory_space=pltpu.VMEM)
    anywhere = pl.BlockSpec(memory_space=pl.ANY)
    flat = lambda value: value.reshape(rows, NX)
    dma = pltpu.SemaphoreType.DMA
    out = pl.pallas_call(
        functools.partial(kernel, steps, nlat, nlon),
        out_shape=jax.ShapeDtypeStruct((rows, NX), F32),
        in_specs=[anywhere] * 6,
        out_specs=vmem,
        scratch_shapes=[
            pltpu.SMEM(cond_table.shape, F32),
            pltpu.VMEM((rows, NX), F32),
            pltpu.VMEM((rows, NX), F32),
            pltpu.VMEM((rows, NX), jnp.int32),
            pltpu.VMEM((rows + 2 * NA, NX), F32),
            pltpu.VMEM((6, LP * NA, NX), F32),
            pltpu.VMEM((6, LP, AP, NX), F32),
            pltpu.VMEM((rows, NX), F32),
            pltpu.VMEM((2, 2 * levels, NX), F32),
            pltpu.VMEM((2, 2 * levels, NX), F32),
            pltpu.VMEM((groups, 2, 8, NX), F32),
            pltpu.VMEM((2, groups, 2, 8, NX), F32),
            pltpu.VMEM((groups, 2, 8, NX), F32),
            pltpu.VMEM((2, levels * 8, NX), F32),
            pltpu.VMEM((steps, 64, NX), F32),
            pltpu.VMEM((zs, LP, 8, NX), F32),
            pltpu.VMEM((zs, LP, 8, NX), F32),
            pltpu.VMEM((64 * 16, NX), F32),
            pltpu.VMEM((64 * 24, NX), F32),
            *[pltpu.VMEM((LP + 2, AP + 2, 16, NX), F32) for _ in range(SWEEPS)],
            pltpu.VMEM((32 * 16, NX), F32),
            pltpu.VMEM((SWEEPS, GROUPS, 8, NX), F32),
            pltpu.VMEM((SWEEPS, GROUPS, 2, 8, NX), F32),
            pltpu.VMEM((steps, 64, NX), F32),
            pltpu.VMEM((steps, 64, NX), F32),
            dma((5,)),
            dma((zs,)),
            dma((zs,)),
            dma((6,)),
            dma((6,)),
            dma((zs,)),
            dma((zs,)),
            dma((zs,)),
            dma((zs,)),
            dma((steps,)),
            dma((steps,)),
            dma((SWEEPS, 2)),
            dma((SWEEPS, 2)),
            dma((SWEEPS, GROUPS, 2)),
            dma((SWEEPS, GROUPS, 2)),
            dma((SWEEPS, GROUPS, 2)),
            dma((SWEEPS, GROUPS, 2)),
            dma((steps,)),
            dma((steps,)),
        ],
        compiler_params=pltpu.CompilerParams(
            collective_id=0, has_side_effects=True, vmem_limit_bytes=VMEM_LIMIT
        ),
    )(*(
        pltpu.with_memory_space_constraint(value, pltpu.HBM)
        for value in (
            flat(iterate), iterate.reshape(levels, 2, AP, NX), flat(heating), flat(region), flat(initial), cond_table
        )
    ))
    return out.reshape(iterate.shape)


def solution(mesh):
    sizes = mesh.shape
    return jax.shard_map(
        functools.partial(on_device, sizes["tm"], sizes["lat"], sizes["lon"]),
        mesh=mesh,
        in_specs=(
            P("tm", None, "lat", "lon"),
            P("tm", None, "lat", "lon"),
            P(None, "lat", "lon"),
            P(None, "lat", "lon"),
            P(),
        ),
        out_specs=P("tm", None, "lat", "lon"),
        check_vma=False,
    )
```

```python
import functools
import math

import jax
import jax.numpy as jnp
from jax import lax
from jax.experimental import pallas as pl
from jax.experimental.pallas import tpu as pltpu
from jax.sharding import PartitionSpec as P

MESH = pl.DeviceIdType.MESH
F32 = jnp.float32
CORNER = 0.1
SWEEPS = 3
LP = 8
GROUPS = 2
AP = 8
NA = 16
NX = 128
VMEM_LIMIT = 40 * 1024 * 1024


def harmonic(first, second):
    return 2.0 * first * second / (first + second)


def weighted(pairs):
    total = None
    for coefficient, value in pairs:
        if abs(coefficient) < 1e-12:
            continue
        if abs(coefficient - 1.0) < 1e-12:
            term = value
        elif abs(coefficient + 1.0) < 1e-12:
            total = -value if total is None else total - value
            continue
        else:
            term = value * coefficient
        total = term if total is None else total + term
    return total


def cosine_sums(e, n):
    half, quarter = n // 2, n // 4
    even = [e[m] + e[half - m] for m in range(quarter)]
    odd = [e[m] - e[half - m] for m in range(quarter)]
    out = []
    for k in range(half + 1):
        parts = even if k % 2 == 0 else odd
        pairs = [(math.cos(2 * math.pi * k * m / n), parts[m]) for m in range(quarter)]
        pairs.append((math.cos(2 * math.pi * k * quarter / n), e[quarter]))
        out.append(weighted(pairs))
    return out


def sine_sums(o, n):
    half, quarter = n // 2, n // 4
    plus = [o[m - 1] + o[half - m - 1] for m in range(1, quarter)]
    minus = [o[m - 1] - o[half - m - 1] for m in range(1, quarter)]
    out = []
    for k in range(1, half):
        parts = plus if k % 2 == 1 else minus
        pairs = [(math.sin(2 * math.pi * k * m / n), parts[m - 1]) for m in range(1, quarter)]
        pairs.append((math.sin(2 * math.pi * k * quarter / n), o[quarter - 1]))
        total = weighted(pairs)
        out.append(total if total is not None else jnp.zeros_like(o[0]))
    return out


def pick(index, values):
    chosen = jnp.float32(values[0])
    for i, value in enumerate(values):
        if i > 0:
            chosen = jnp.where(index == i, jnp.float32(value), chosen)
    return chosen


def kernel(
    steps, nlat, nlon,
    u_hbm, u_parts, h_hbm, reg_hbm, init_hbm, table_hbm, out_ref,
    table_ref, u_ref, h_ref, reg_ref, kap, wts, own, pbuf, lat_out, lat_in, lon_out, lon_in, lon_mix,
    rs, rr, ur, relay, spec, coef, xe0, xe1, xe2, rot0, rot1, rot2, xf, edge_out, edge_in, ws, wb,
    local, shift_s, shift_r, side_s, side_r, relay_s, relay_r, state_s, state_r, fwd_s, fwd_r,
    lev_s, lev_r, lat_s, lat_r, lon_s, lon_r, back_s, back_r,
):
    levels = u_ref.shape[0] // NA
    xe = (xe0, xe1, xe2)
    rot = (rot0, rot1, rot2)
    zs = steps // 2
    half = steps // 2
    me = lax.axis_index("tm")
    lat = lax.axis_index("lat")
    lon = lax.axis_index("lon")
    z = lax.div(me, 2)
    xl = lax.rem(me, 2)
    q = lax.rem(xl + lat, 2)
    left = lax.rem(lon + nlon - 1, nlon)
    right = lax.rem(lon + 1, nlon)
    sub = lax.broadcasted_iota(jnp.int32, (8, NX), 0)
    lane = lax.broadcasted_iota(jnp.int32, (8, NX), 1)
    lane_pair = lax.div(lane, 2)
    odd_lane = lax.rem(lane, 2) == 1
    first_lane = lane == 0
    last_lane = lane == NX - 1
    zero = jnp.zeros((8, NX), F32)

    def remote(src, dst, send, recv, device):
        return pltpu.make_async_remote_copy(
            src_ref=src, dst_ref=dst, send_sem=send, recv_sem=recv, device_id=device, device_id_type=MESH
        )

    def guarded(condition, act):
        if condition is None:
            act()
        else:
            pl.when(condition)(act)

    sides = (
        (lat > 0, {"lat": lat - 1}),
        (lat < nlat - 1, {"lat": lat + 1}),
        (None, {"lon": left}),
        (None, {"lon": right}),
    )
    x_low = xl * (1 - q) + (1 - xl) * q
    x_high = xl * q + (1 - xl) * (1 - q)
    lev_sides = ((z > 0, {"tm": me - 2}), (z < zs - 1, {"tm": me + 2}))
    lat_sides = (
        (q + lat > 0, {"tm": z * 2 + x_low, "lat": lat - (1 - q)}),
        ((1 - q) + (nlat - 1 - lat) > 0, {"tm": z * 2 + x_high, "lat": lat + q}),
    )
    lon_sides = ((None, {"lon": left}), (None, {"lon": right}))

    barrier = pltpu.get_barrier_semaphore()
    for d in range(1, steps):
        pl.semaphore_signal(barrier, inc=1, device_id={"tm": lax.rem(me + d, steps)}, device_id_type=MESH)
    for condition, device in sides:
        guarded(
            condition,
            functools.partial(pl.semaphore_signal, barrier, inc=1, device_id=device, device_id_type=MESH),
        )

    take_reg = pltpu.make_async_copy(reg_hbm, reg_ref, local.at[0])
    take_u = pltpu.make_async_copy(u_hbm, u_ref, local.at[1])
    take_h = pltpu.make_async_copy(h_hbm, h_ref, local.at[2])
    take_init = pltpu.make_async_copy(init_hbm, pbuf, local.at[3])
    take_table = pltpu.make_async_copy(table_hbm, table_ref, local.at[4])
    take_table.start()
    take_reg.start()
    take_u.start()
    take_h.start()

    @pl.when(me == 0)
    def _():
        take_init.start()

    for b in range(SWEEPS):
        for condition, place in (
            (z == 0, (b, 0, slice(None))),
            (z == zs - 1, (b, 1, slice(None))),
            (q + lat == 0, (b, slice(None), 0)),
            ((1 - q) + (nlat - 1 - lat) == 0, (b, slice(None), AP + 1)),
        ):
            def clear(place=place):
                xe[place[0]][place[1:]] = jnp.zeros((10, 16, NX), F32)

            pl.when(condition)(clear)

    @pl.when(lat == 0)
    def _():
        lat_in[0] = jnp.zeros(lat_in.shape[1:], F32)

    @pl.when(lat == nlat - 1)
    def _():
        lat_in[1] = jnp.zeros(lat_in.shape[1:], F32)

    @pl.when(jnp.logical_and(me > 0, xl == 0))
    def _():
        pbuf[...] = jnp.zeros(pbuf.shape, F32)

    kap[pl.ds(0, NA), :] = jnp.zeros((NA, NX), F32)
    kap[pl.ds((levels + 1) * NA, NA), :] = jnp.zeros((NA, NX), F32)
    take_table.wait()
    table = [table_ref[c] for c in range(8)]
    take_reg.wait()
    take_u.wait()

    for group in range((levels + 31) // 32):
        def conduct(g, packs):
            gathered = [zero, zero]
            for j in range(16):
                at = pl.multiple_of((group * 4 + g) * 128, 8) + j * 8
                reg = reg_ref[pl.ds(at, 8), :]
                k = jnp.full((8, NX), table[0], F32)
                for c in range(1, 8):
                    k = jnp.where(reg == c, table[c], k)
                kap[pl.ds(at + NA, 8), :] = k
                u = u_ref[pl.ds(at, 8), :]
                for f, tile in ((0, u), (1, k)):
                    gathered[f] = jnp.where(lane_pair == j, pltpu.roll(tile, 2 * j + 1, 1), gathered[f])
            mask = lax.div(lane, 32) == g
            return tuple(jnp.where(mask, pltpu.roll(gathered[f], g * 32, 1), packs[f]) for f in range(2))

        packs = lax.fori_loop(0, min(4, levels // 8 - 4 * group), conduct, (zero, zero))
        for f in range(2):
            lon_out[group, f] = packs[f]
    for g in range(zs):
        e = lax.rem(g + zs - z, zs) - zs // 2
        at = pl.multiple_of(jnp.where(e < 0, -2 * e - 1, 2 * e) * 16, 8)
        for side, row in ((0, 0), (1, NA - 1)):
            lat_out[side, pl.ds(at, 8), :] = u_ref[pl.ds(g * 128 + row, 8, stride=NA), :]
            lat_out[side, pl.ds(at + 8, 8), :] = kap[pl.ds(NA + g * 128 + row, 8, stride=NA), :]

    lat_count = jnp.where(lat > 0, 1, 0) + jnp.where(lat < nlat - 1, 1, 0)
    pl.semaphore_wait(barrier, steps - 1 + 2 + lat_count)

    def lat_rows(d):
        return pl.ds(0, 16) if d < 2 else pl.ds(16, 2 * levels - 16)

    def side_copy(d):
        if d in (2, 3):
            return remote(lon_out, lon_in.at[3 - d], side_s.at[d], side_r.at[5 - d], sides[d][1])
        e = d % 2
        return remote(
            lat_out.at[e, lat_rows(d)], lat_in.at[1 - e, lat_rows(d)], side_s.at[d], side_r.at[d + 1 - 2 * e], sides[e][1]
        )

    def side_arrival(d):
        if d in (2, 3):
            return remote(lon_out, lon_in.at[d - 2], side_s.at[d], side_r.at[d], sides[d][1])
        e = d % 2
        return remote(lat_out.at[e, lat_rows(d)], lat_in.at[e, lat_rows(d)], side_s.at[d], side_r.at[d], sides[e][1])

    def side_there(d):
        return None if d in (2, 3) else sides[d % 2][0]

    for d in (2, 3, 0, 1, 4, 5):
        guarded(side_there(d), lambda d=d: side_copy(d).start())

    def order(i, at):
        odd = lax.rem(i, 2)
        away = zs // 2 + (1 - odd) * lax.div(i, 2) - odd * lax.div(i + 1, 2)
        return lax.rem(at + away, zs)

    rows = LP * NA

    def shift_copy(i):
        part = pl.ds(pl.multiple_of(order(i, z) * rows, 8), rows)
        return remote(u_hbm.at[part, :], pbuf.at[part, :], shift_s.at[i], shift_r.at[i], {"tm": me + 1 - 2 * xl})

    @pl.when(xl == 0)
    def _():
        for i in range(zs):
            shift_copy(i).start()

    sends_state = z < zs - 1
    relayed = min(4, zs // 2 + 0)

    def state_parts(i, x):
        return u_parts.at[pl.ds(order(i, z) * LP, LP), lax.rem(x + lat, 2)]

    def relay_copy(i):
        return remote(state_parts(i, 0), relay.at[i], relay_s.at[i], relay_r.at[i], {"tm": me + 1 - 2 * xl})

    def state_copy(i):
        to = order(i, z) * 2 + 1
        return remote(state_parts(i, 1), ur.at[z], state_s.at[i], state_r.at[z], {"tm": to})

    def direct_copy(i):
        return remote(state_parts(i, 0), ur.at[z], relay_s.at[i], state_r.at[z], {"tm": order(i, z) * 2})

    def forward_copy(i):
        return remote(relay.at[i], ur.at[z], state_s.at[i], state_r.at[z], {"tm": order(i, z) * 2})

    @pl.when(jnp.logical_and(xl == 1, sends_state))
    def _():
        for i in range(zs):
            if i < relayed:
                relay_copy(i).start()
            if i < zs - 1:
                state_copy(i).start()
            if i >= relayed:
                direct_copy(i).start()
        for l in range(LP):
            row = pl.multiple_of((z * LP + l) * NA + q * 8, 8)
            ur[z, l] = u_ref[pl.ds(row, 8), :]

    forwards = jnp.logical_and(xl == 0, sends_state)

    @pl.when(forwards)
    def _():
        for i in range(relayed):
            relay_copy(i).wait_recv()
            forward_copy(i).start()

    take_h.wait()

    @pl.when(me == 0)
    def _():
        take_init.wait()

    for d in range(4):
        guarded(side_there(d), lambda d=d: side_arrival(d).wait_recv())
    for group in range((levels + 31) // 32):
        for f in range(2):
            lon_mix[group, f] = jnp.where(odd_lane, lon_in[1, group, f], lon_in[0, group, f])

    gamma = [CORNER ** (n / steps) for n in range(steps)]
    scale = pick(me, gamma)

    def fwd_copy(part, zd, to):
        return remote(
            rs.at[part, pl.ds(pl.multiple_of(zd * 64, 8), 64), :], rr.at[me], fwd_s.at[to], fwd_r.at[me], {"tm": to}
        )

    def chunk(i, carry):
        zd = order(i, z)

        @pl.when(i == 1)
        def _():
            for d in (4, 5):
                guarded(side_there(d), lambda d=d: side_arrival(d).wait_recv())

        @pl.when(xl == 1)
        def _():
            shift_copy(i).wait_recv()

        def level(l):
            lev = zd * LP + l
            base = pl.multiple_of(lev * NA, 8)
            under = pl.multiple_of(jnp.maximum(lev - 1, 0) * NA, 8)
            over = pl.multiple_of(jnp.minimum(lev + 1, levels - 1) * NA, 8)
            group = lax.div(lev, 32)
            fields = []
            for f, ref, low, mid, high in (
                (0, u_ref, under, base, over),
                (1, kap, base, base + NA, base + 2 * NA),
            ):
                tile = [ref[pl.ds(mid + 8 * t, 8), :] for t in range(2)]
                down = [ref[pl.ds(low + 8 * t, 8), :] for t in range(2)]
                up = [ref[pl.ds(high + 8 * t, 8), :] for t in range(2)]
                row = [
                    jnp.broadcast_to(lat_in[s, pl.ds(i * 16 + f * 8 + l, 1), :], (8, NX)) for s in range(2)
                ]
                one = [pltpu.roll(tile[t], 1, 0) for t in range(2)]
                seven = [pltpu.roll(tile[t], 7, 0) for t in range(2)]
                before = [jnp.where(sub == 0, row[0], one[0]), jnp.where(sub == 0, one[0], one[1])]
                after = [jnp.where(sub == 7, seven[1], seven[0]), jnp.where(sub == 7, row[1], seven[1])]
                ends = lon_mix[group, f]
                west, east = [], []
                for t in range(2):
                    halo = pltpu.roll(ends, NX - 1 - 2 * (lax.rem(lev, 32) * 2 + t), 1)
                    west.append(pltpu.roll(jnp.where(last_lane, halo, tile[t]), 1, 1))
                    east.append(pltpu.roll(jnp.where(first_lane, halo, tile[t]), NX - 1, 1))
                fields.append((tile, (down, up, before, after, west, east)))
            (u, u_near), (k, k_near) = fields
            for t in range(2):
                at = pl.multiple_of(l * NA, 8) + 8 * t
                total = None
                for f in range(6):
                    w = harmonic(k[t], k_near[f][t])
                    wts[f, pl.ds(at, 8), :] = w
                    term = w * (u_near[f][t] - u[t])
                    total = term if total is None else total + term
                r = (h_ref[pl.ds(base + 8 * t, 8), :] + pbuf[pl.ds(base + 8 * t, 8), :]) - (u[t] - total)
                rs[t, pl.ds(pl.multiple_of(lev * 8, 8), 8), :] = r * scale

        def some_levels(m, carry):
            for l in range(4):
                level(m * 4 + l)
            return carry

        lax.fori_loop(0, LP // 4, some_levels, 0)
        for part in range(2):
            to = zd * 2 + lax.rem(part + lat, 2)

            @pl.when(to != me)
            def _():
                fwd_copy(part, zd, to).start()

            @pl.when(to == me)
            def _():
                rr[me] = rs[part, pl.ds(pl.multiple_of(zd * 64, 8), 64), :]

        return carry

    lax.fori_loop(0, zs, chunk, 0)

    beta = CORNER ** (1.0 / steps)
    shift_re = [1.0 - beta * math.cos(2 * math.pi * k / steps) for k in range(half + 1)]
    shift_im = [beta * math.sin(2 * math.pi * k / steps) for k in range(half + 1)]

    def invert(l, carry):
        at = pl.multiple_of(l * NA + q * 8, 8)
        total = None
        for f in range(6):
            w = wts[f, pl.ds(at, 8), :]
            own[f, l] = w
            total = w if total is None else total + w
        for k in range(half + 1):
            re = total + shift_re[k]
            if k in (0, half):
                value = 1.0 / re
                row = 0 if k == 0 else 8
                coef[pl.ds(l * 192 + row, 8, stride=24), :] = value
                if k == 0:
                    coef[pl.ds(l * 192 + 16, 8, stride=24), :] = zero
            else:
                share = 1.0 / (re * re + shift_im[k] * shift_im[k])
                real = re * share
                coef[pl.ds(l * 192 + k, 8, stride=24), :] = real
                coef[pl.ds(l * 192 + 8 + k, 8, stride=24), :] = real
                coef[pl.ds(l * 192 + 16 + k, 8, stride=24), :] = share * (-shift_im[k])
        return carry

    lax.fori_loop(0, LP, invert, 0)

    def await_fwd(d, carry):
        src = lax.rem(me + d, steps)
        remote(rs.at[0, pl.ds(0, 64), :], rr.at[src], fwd_s.at[src], fwd_r.at[src], {"tm": src}).wait_recv()
        return carry

    lax.fori_loop(1, steps, await_fwd, 0)
    for i in range(zs - 1):

        @pl.when(jnp.logical_or(z != i, xl == 0))
        def _():
            remote(relay.at[0], ur.at[i], state_s.at[i], state_r.at[i], {"tm": 2 * i + xl}).wait_recv()

    def sent_index(m, s):
        return 2 + 2 * m + s

    def inner_index(m, s):
        return jnp.where(m == LP // 2 - 1, LP + 1 - s, 4 + 2 * m + s)

    def level_of(m, s):
        return m + s * (LP - 1 - 2 * m)

    def divide(l, a, re, im):
        at = pl.multiple_of((l * 8 + a) * 24, 8)
        c_re, c_im, cross = (coef[pl.ds(at + 8 * i, 8), :] for i in range(3))
        return re * c_re - im * cross, im * c_im + re * cross

    def turn(tile, by):
        return tile if by % NX == 0 else pltpu.roll(tile, by % NX, 1)

    class Packed:
        def __init__(self):
            self.parts = [zero, zero]

        def add(self, p, a, f, tile):
            j = (p * AP + a) * 2 + f
            turned = pltpu.roll(tile, 2 * j + 1, 1)
            self.parts[f] = jnp.where(lane_pair == j, turned, self.parts[f])
            return turned

        def value(self):
            return jnp.where(lax.rem(lane_pair, 2) == 0, self.parts[0], self.parts[1])

    inner = pl.ds(1, AP)

    def lev_copy(b, d):
        return remote(
            xe[b].at[2 + d, inner], xe[b].at[1 - d, inner], lev_s.at[b, d], lev_r.at[b, 1 - d], lev_sides[d][1]
        )

    def lev_arrival(b, d):
        return remote(xe[b].at[2 + d, inner], xe[b].at[d, inner], lev_s.at[b, d], lev_r.at[b, d], lev_sides[d][1])

    def lat_copy(b, m, d):
        pair = pl.ds(2 + 4 * m, 4)
        return remote(
            xe[b].at[pair, 1 + d * (AP - 1)], xe[b].at[pair, (1 - d) * (AP + 1)],
            lat_s.at[b, m, d], lat_r.at[b, m, 1 - d], lat_sides[d][1],
        )

    def lat_arrival(b, m, d):
        pair = pl.ds(2 + 4 * m, 4)
        return remote(
            xe[b].at[pair, 1 + d * (AP - 1)], xe[b].at[pair, d * (AP + 1)],
            lat_s.at[b, m, d], lat_r.at[b, m, d], lat_sides[d][1],
        )

    def lon_copy(b, m, d):
        return remote(
            edge_out.at[b, m], edge_in.at[b, m, 1 - d], lon_s.at[b, m, d], lon_r.at[b, m, 1 - d], lon_sides[d][1]
        )

    def lon_arrival(b, m, d):
        return remote(edge_out.at[b, m], edge_in.at[b, m, d], lon_s.at[b, m, d], lon_r.at[b, m, d], lon_sides[d][1])

    def send_edges(b, m, packed):
        edge_out[b, m] = packed.value()

        for d in range(2):
            lon_copy(b, m, d).start()
        for d in range(2):
            guarded(lat_sides[d][0], lambda d=d: lat_copy(b, m, d).start())

    def send_levels(b, m):
        @pl.when(m == 0)
        def _():
            for d in range(2):
                guarded(lev_sides[d][0], lambda d=d: lev_copy(b, d).start())

    def await_edges(b, m):
        @pl.when(m == 0)
        def _():
            for d in range(2):
                guarded(lev_sides[d][0], lambda d=d: lev_arrival(b, d).wait_recv())

        for d in range(2):
            guarded(lat_sides[d][0], lambda d=d: lat_arrival(b, m, d).wait_recv())
        for d in range(2):
            lon_arrival(b, m, d).wait_recv()

    members = ((0, 0), (0, 1), (1, 0), (1, 1))

    def to_spectrum(g, carry):
        packed = Packed()
        for mm, s in members:
            l = level_of(2 * g + mm, s)
            at = pl.multiple_of(l * 8, 8)
            r = [rr[n, pl.ds(at, 8), :] for n in range(steps)]
            for n in range(2, steps, 2):
                r[n] = r[n] + ur[n // 2 - 1, l] * gamma[n]
            e = [r[0]] + [r[n] + r[steps - n] for n in range(1, half)] + [r[half]]
            o = [r[n] - r[steps - n] for n in range(1, half)]
            real = cosine_sums(e, steps)
            imag = sine_sums(o, steps)
            for k in range(half):
                spec[pl.ds(l * 128 + k, 8, stride=16), :] = real[k]
            spec[pl.ds(l * 128 + 8, 8, stride=16), :] = real[half]
            for k in range(1, half):
                spec[pl.ds(l * 128 + 8 + k, 8, stride=16), :] = -imag[k - 1]
        for p, (mm, s) in enumerate(members):
            m = 2 * g + mm
            l = level_of(m, s)
            for a in range(AP):
                row = pl.multiple_of((l * 8 + a) * 16, 8)
                x = divide(l, a, spec[pl.ds(row, 8), :], spec[pl.ds(row + 8, 8), :])
                for f in range(2):
                    xe[0][sent_index(m, s), a + 1, pl.ds(8 * f, 8), :] = x[f]
                    rot[0][sent_index(m, s), a, pl.ds(8 * f, 8), :] = packed.add(p, a, f, x[f])
            if p == 1:
                send_levels(0, g)
        send_edges(0, g, packed)
        return carry

    lax.fori_loop(0, GROUPS, to_spectrum, 0)

    def back_copy(to, first, count):
        part = pl.ds(pl.multiple_of(first, 8), count)
        return remote(ws.at[to, part], wb.at[me, part], back_s.at[to], back_r.at[me], {"tm": to})

    def from_spectrum(g, p):
        base = p * 128
        x = [xf[pl.ds(base + k, 8, stride=16), :] for k in range(half)]
        x_half = xf[pl.ds(base + 8, 8, stride=16), :]
        y = [xf[pl.ds(base + 8 + k, 8, stride=16), :] for k in range(1, half)]
        even = cosine_sums([x[0] * 0.5] + x[1:] + [x_half * 0.5], steps)
        odd = sine_sums(y, steps)
        at = pl.ds(pl.multiple_of(g * 32, 8) + p * 8, 8)
        ws[0, at, :] = even[0]
        ws[half, at, :] = even[half]
        for n in range(1, half):
            ws[n, at, :] = even[n] - odd[n - 1]
            ws[steps - n, at, :] = even[n] + odd[n - 1]

    def sweep(b, last):
        def some_pairs(g, carry):
            await_edges(b, g)
            ends = jnp.where(odd_lane, edge_in[b, g, 1], edge_in[b, g, 0])
            packed = Packed()
            for p, (mm, s) in enumerate(members):
                m = 2 * g + mm
                l = level_of(m, s)
                i = sent_index(m, s)
                beyond = (i - 2, inner_index(m, s))
                under, over = beyond if s == 0 else beyond[::-1]
                for a in range(AP):
                    w = [
                        jnp.broadcast_to(own[f, l, pl.ds(a, 1), :], (8, NX)) for f in range(6)
                    ]
                    row = pl.multiple_of((l * 8 + a) * 16, 8)
                    rhs = []
                    for f in range(2):
                        part = pl.ds(8 * f, 8)
                        j = (p * AP + a) * 2 + f
                        turned = rot[b][i, a, part, :]
                        west = jnp.where(lane == 2 * j, ends, turned)
                        east = jnp.where(lane == 2 * j + 1, ends, turned)
                        total = spec[pl.ds(row + 8 * f, 8), :]
                        total = total + w[0] * xe[b][under, a + 1, part, :] + w[1] * xe[b][over, a + 1, part, :]
                        total = total + w[2] * xe[b][i, a, part, :] + w[3] * xe[b][i, a + 2, part, :]
                        total = total + w[4] * turn(west, NX - 2 * j) + w[5] * turn(east, NX - 2 * j - 2)
                        rhs.append(total)
                    x = divide(l, a, rhs[0], rhs[1])
                    for f in range(2):
                        if last:
                            xf[pl.ds((p * AP + a) * 16 + 8 * f, 8), :] = x[f]
                        else:
                            xe[b + 1][i, a + 1, pl.ds(8 * f, 8), :] = x[f]
                            rot[b + 1][i, a, pl.ds(8 * f, 8), :] = packed.add(p, a, f, x[f])
                if p == 1 and not last:
                    send_levels(b + 1, g)
            if not last:
                send_edges(b + 1, g, packed)
            else:
                for p in range(4):
                    from_spectrum(g, p)

                def send(i, carry):
                    odd = lax.rem(i, 2)
                    d = half + (1 - odd) * lax.div(i, 2) - odd * lax.div(i + 1, 2)
                    back_copy(lax.rem(me + d, steps), g * 32, 32).start()
                    return carry

                lax.fori_loop(0, steps - 1, send, 0)
            return carry

        lax.fori_loop(0, GROUPS, some_pairs, 0)

    for b in range(SWEEPS):
        sweep(b, b == SWEEPS - 1)

    wb[me] = ws[me]
    share = pick(me, [2.0 / (steps * g) for g in gamma])

    def finish(i, carry):
        odd = lax.rem(i, 2)
        away = lax.div(i + 1, 2)
        src = lax.rem(me + steps + odd * away - (1 - odd) * away, steps)
        zz = lax.div(src, 2)
        part = lax.rem(lax.rem(src, 2) + lat, 2)

        @pl.when(i > 0)
        def _():
            remote(ws.at[src], wb.at[src], back_s.at[src], back_r.at[src], {"tm": src}).wait_recv()

        for m in range(LP // 2):
            for s in range(2):
                at = pl.multiple_of((zz * LP + level_of(m, s)) * NA + part * 8, 8)
                out_ref[pl.ds(at, 8), :] = u_ref[pl.ds(at, 8), :] + wb[src, pl.ds(m * 16 + s * 8, 8), :] * share
        return carry

    lax.fori_loop(0, steps, finish, 0)

    @pl.when(xl == 0)
    def _():
        for i in range(zs):
            shift_copy(i).wait_send()

    for d in range(6):
        guarded(side_there(d), lambda d=d: side_copy(d).wait_send())

    def sent(d, carry):
        to = lax.rem(me + d, steps)
        fwd_copy(0, 0, to).wait_send()
        back_copy(to, 0, 64).wait_send()
        return carry

    lax.fori_loop(1, steps, sent, 0)

    @pl.when(forwards)
    def _():
        for i in range(relayed):
            forward_copy(i).wait_send()

    @pl.when(jnp.logical_and(xl == 1, sends_state))
    def _():
        for i in range(zs):
            relay_copy(i).wait_send()
            if i < zs - 1:
                state_copy(i).wait_send()

    for b in range(SWEEPS):
        for d in range(2):
            guarded(lev_sides[d][0], lambda b=b, d=d: lev_copy(b, d).wait_send())

        def edges_sent(m, carry, b=b):
            for d in range(2):
                guarded(lat_sides[d][0], lambda d=d: lat_copy(b, m, d).wait_send())
                lon_copy(b, m, d).wait_send()
            return carry

        lax.fori_loop(0, GROUPS, edges_sent, 0)


def on_device(steps, nlat, nlon, iterate, heating, initial, region, cond_table):
    levels = initial.shape[0]
    rows = levels * NA
    zs = steps // 2
    groups = (levels + 31) // 32
    vmem = pl.BlockSpec(memory_space=pltpu.VMEM)
    anywhere = pl.BlockSpec(memory_space=pl.ANY)
    flat = lambda value: value.reshape(rows, NX)
    dma = pltpu.SemaphoreType.DMA
    out = pl.pallas_call(
        functools.partial(kernel, steps, nlat, nlon),
        out_shape=jax.ShapeDtypeStruct((rows, NX), F32),
        in_specs=[anywhere] * 6,
        out_specs=vmem,
        scratch_shapes=[
            pltpu.SMEM(cond_table.shape, F32),
            pltpu.VMEM((rows, NX), F32),
            pltpu.VMEM((rows, NX), F32),
            pltpu.VMEM((rows, NX), jnp.int32),
            pltpu.VMEM((rows + 2 * NA, NX), F32),
            pltpu.VMEM((6, LP * NA, NX), F32),
            pltpu.VMEM((6, LP, AP, NX), F32),
            pltpu.VMEM((rows, NX), F32),
            pltpu.VMEM((2, 2 * levels, NX), F32),
            pltpu.VMEM((2, 2 * levels, NX), F32),
            pltpu.VMEM((groups, 2, 8, NX), F32),
            pltpu.VMEM((2, groups, 2, 8, NX), F32),
            pltpu.VMEM((groups, 2, 8, NX), F32),
            pltpu.VMEM((2, levels * 8, NX), F32),
            pltpu.VMEM((steps, 64, NX), F32),
            pltpu.VMEM((zs, LP, 8, NX), F32),
            pltpu.VMEM((zs, LP, 8, NX), F32),
            pltpu.VMEM((64 * 16, NX), F32),
            pltpu.VMEM((64 * 24, NX), F32),
            *[pltpu.VMEM((LP + 2, AP + 2, 16, NX), F32) for _ in range(SWEEPS)],
            *[pltpu.VMEM((LP + 2, AP, 16, NX), F32) for _ in range(SWEEPS)],
            pltpu.VMEM((32 * 16, NX), F32),
            pltpu.VMEM((SWEEPS, GROUPS, 8, NX), F32),
            pltpu.VMEM((SWEEPS, GROUPS, 2, 8, NX), F32),
            pltpu.VMEM((steps, 64, NX), F32),
            pltpu.VMEM((steps, 64, NX), F32),
            dma((5,)),
            dma((zs,)),
            dma((zs,)),
            dma((6,)),
            dma((6,)),
            dma((zs,)),
            dma((zs,)),
            dma((zs,)),
            dma((zs,)),
            dma((steps,)),
            dma((steps,)),
            dma((SWEEPS, 2)),
            dma((SWEEPS, 2)),
            dma((SWEEPS, GROUPS, 2)),
            dma((SWEEPS, GROUPS, 2)),
            dma((SWEEPS, GROUPS, 2)),
            dma((SWEEPS, GROUPS, 2)),
            dma((steps,)),
            dma((steps,)),
        ],
        compiler_params=pltpu.CompilerParams(
            collective_id=0, has_side_effects=True, vmem_limit_bytes=VMEM_LIMIT
        ),
    )(*(
        pltpu.with_memory_space_constraint(value, pltpu.HBM)
        for value in (
            flat(iterate), iterate.reshape(levels, 2, AP, NX), flat(heating), flat(region), flat(initial), cond_table
        )
    ))
    return out.reshape(iterate.shape)


def solution(mesh):
    sizes = mesh.shape
    return jax.shard_map(
        functools.partial(on_device, sizes["tm"], sizes["lat"], sizes["lon"]),
        mesh=mesh,
        in_specs=(
            P("tm", None, "lat", "lon"),
            P("tm", None, "lat", "lon"),
            P(None, "lat", "lon"),
            P(None, "lat", "lon"),
            P(),
        ),
        out_specs=P("tm", None, "lat", "lon"),
        check_vma=False,
    )
```

```python
import functools
import math

import jax
import jax.numpy as jnp
from jax import lax
from jax.experimental import pallas as pl
from jax.experimental.pallas import tpu as pltpu
from jax.sharding import PartitionSpec as P

MESH = pl.DeviceIdType.MESH
F32 = jnp.float32
CORNER = 0.1
SWEEPS = 3
LP = 8
GROUPS = 2
AP = 8
NA = 16
NX = 128
VMEM_LIMIT = 40 * 1024 * 1024


def harmonic(first, second):
    return 2.0 * first * second / (first + second)


def weighted(pairs):
    total = None
    for coefficient, value in pairs:
        if abs(coefficient) < 1e-12:
            continue
        if abs(coefficient - 1.0) < 1e-12:
            term = value
        elif abs(coefficient + 1.0) < 1e-12:
            total = -value if total is None else total - value
            continue
        else:
            term = value * coefficient
        total = term if total is None else total + term
    return total


def cosine_sums(e, n):
    half, quarter = n // 2, n // 4
    even = [e[m] + e[half - m] for m in range(quarter)]
    odd = [e[m] - e[half - m] for m in range(quarter)]
    out = []
    for k in range(half + 1):
        parts = even if k % 2 == 0 else odd
        pairs = [(math.cos(2 * math.pi * k * m / n), parts[m]) for m in range(quarter)]
        pairs.append((math.cos(2 * math.pi * k * quarter / n), e[quarter]))
        out.append(weighted(pairs))
    return out


def sine_sums(o, n):
    half, quarter = n // 2, n // 4
    plus = [o[m - 1] + o[half - m - 1] for m in range(1, quarter)]
    minus = [o[m - 1] - o[half - m - 1] for m in range(1, quarter)]
    out = []
    for k in range(1, half):
        parts = plus if k % 2 == 1 else minus
        pairs = [(math.sin(2 * math.pi * k * m / n), parts[m - 1]) for m in range(1, quarter)]
        pairs.append((math.sin(2 * math.pi * k * quarter / n), o[quarter - 1]))
        total = weighted(pairs)
        out.append(total if total is not None else jnp.zeros_like(o[0]))
    return out


def pick(index, values):
    chosen = jnp.float32(values[0])
    for i, value in enumerate(values):
        if i > 0:
            chosen = jnp.where(index == i, jnp.float32(value), chosen)
    return chosen


def kernel(
    steps, nlat, nlon,
    u_hbm, u_parts, h_hbm, reg_hbm, init_hbm, table_hbm, out_ref,
    table_ref, u_ref, h_ref, reg_ref, kap, wts, own, pbuf, lat_out, lat_in, lon_out, lon_in, lon_mix,
    rs, rr, ur, relay, spec, coef, xe0, xe1, xe2, rot0, rot1, rot2, xf, edge_out, edge_in, ws, wb,
    local, shift_s, shift_r, side_s, side_r, relay_s, relay_r, state_s, state_r, fwd_s, fwd_r,
    lev_s, lev_r, lat_s, lat_r, lon_s, lon_r, back_s, back_r,
):
    levels = u_ref.shape[0] // NA
    xe = (xe0, xe1, xe2)
    rot = (rot0, rot1, rot2)
    zs = steps // 2
    half = steps // 2
    me = lax.axis_index("tm")
    lat = lax.axis_index("lat")
    lon = lax.axis_index("lon")
    z = lax.div(me, 2)
    xl = lax.rem(me, 2)
    q = lax.rem(xl + lat, 2)
    left = lax.rem(lon + nlon - 1, nlon)
    right = lax.rem(lon + 1, nlon)
    sub = lax.broadcasted_iota(jnp.int32, (8, NX), 0)
    lane = lax.broadcasted_iota(jnp.int32, (8, NX), 1)
    lane_pair = lax.div(lane, 2)
    odd_lane = lax.rem(lane, 2) == 1
    first_lane = lane == 0
    last_lane = lane == NX - 1
    zero = jnp.zeros((8, NX), F32)

    def remote(src, dst, send, recv, device):
        return pltpu.make_async_remote_copy(
            src_ref=src, dst_ref=dst, send_sem=send, recv_sem=recv, device_id=device, device_id_type=MESH
        )

    def guarded(condition, act):
        if condition is None:
            act()
        else:
            pl.when(condition)(act)

    sides = (
        (lat > 0, {"lat": lat - 1}),
        (lat < nlat - 1, {"lat": lat + 1}),
        (None, {"lon": left}),
        (None, {"lon": right}),
    )
    x_low = xl * (1 - q) + (1 - xl) * q
    x_high = xl * q + (1 - xl) * (1 - q)
    lev_sides = ((z > 0, {"tm": me - 2}), (z < zs - 1, {"tm": me + 2}))
    lat_sides = (
        (q + lat > 0, {"tm": z * 2 + x_low, "lat": lat - (1 - q)}),
        ((1 - q) + (nlat - 1 - lat) > 0, {"tm": z * 2 + x_high, "lat": lat + q}),
    )
    lon_sides = ((None, {"lon": left}), (None, {"lon": right}))

    barrier = pltpu.get_barrier_semaphore()
    for d in range(1, steps):
        pl.semaphore_signal(barrier, inc=1, device_id={"tm": lax.rem(me + d, steps)}, device_id_type=MESH)
    for condition, device in sides:
        guarded(
            condition,
            functools.partial(pl.semaphore_signal, barrier, inc=1, device_id=device, device_id_type=MESH),
        )

    take_reg = pltpu.make_async_copy(reg_hbm, reg_ref, local.at[0])
    take_u = pltpu.make_async_copy(u_hbm, u_ref, local.at[1])
    take_h = pltpu.make_async_copy(h_hbm, h_ref, local.at[2])
    take_init = pltpu.make_async_copy(init_hbm, pbuf, local.at[3])
    take_table = pltpu.make_async_copy(table_hbm, table_ref, local.at[4])
    take_table.start()
    take_reg.start()
    take_u.start()
    take_h.start()

    @pl.when(me == 0)
    def _():
        take_init.start()

    for b in range(SWEEPS):
        for condition, place in (
            (z == 0, (b, 0, slice(None))),
            (z == zs - 1, (b, 1, slice(None))),
            (q + lat == 0, (b, slice(None), 0)),
            ((1 - q) + (nlat - 1 - lat) == 0, (b, slice(None), AP + 1)),
        ):
            def clear(place=place):
                xe[place[0]][place[1:]] = jnp.zeros((10, 16, NX), F32)

            pl.when(condition)(clear)

    @pl.when(lat == 0)
    def _():
        lat_in[0] = jnp.zeros(lat_in.shape[1:], F32)

    @pl.when(lat == nlat - 1)
    def _():
        lat_in[1] = jnp.zeros(lat_in.shape[1:], F32)

    @pl.when(jnp.logical_and(me > 0, xl == 0))
    def _():
        pbuf[...] = jnp.zeros(pbuf.shape, F32)

    kap[pl.ds(0, NA), :] = jnp.zeros((NA, NX), F32)
    kap[pl.ds((levels + 1) * NA, NA), :] = jnp.zeros((NA, NX), F32)
    take_table.wait()
    table = [table_ref[c] for c in range(8)]
    take_reg.wait()
    take_u.wait()

    for group in range((levels + 31) // 32):
        def conduct(g, packs):
            gathered = [zero, zero]
            for j in range(16):
                at = pl.multiple_of((group * 4 + g) * 128, 8) + j * 8
                reg = reg_ref[pl.ds(at, 8), :]
                k = jnp.full((8, NX), table[0], F32)
                for c in range(1, 8):
                    k = jnp.where(reg == c, table[c], k)
                kap[pl.ds(at + NA, 8), :] = k
                u = u_ref[pl.ds(at, 8), :]
                for f, tile in ((0, u), (1, k)):
                    gathered[f] = jnp.where(lane_pair == j, pltpu.roll(tile, 2 * j + 1, 1), gathered[f])
            mask = lax.div(lane, 32) == g
            return tuple(jnp.where(mask, pltpu.roll(gathered[f], g * 32, 1), packs[f]) for f in range(2))

        packs = lax.fori_loop(0, min(4, levels // 8 - 4 * group), conduct, (zero, zero))
        for f in range(2):
            lon_out[group, f] = packs[f]
    for g in range(zs):
        e = lax.rem(g + zs - z, zs) - zs // 2
        at = pl.multiple_of(jnp.where(e < 0, -2 * e - 1, 2 * e) * 16, 8)
        for side, row in ((0, 0), (1, NA - 1)):
            lat_out[side, pl.ds(at, 8), :] = u_ref[pl.ds(g * 128 + row, 8, stride=NA), :]
            lat_out[side, pl.ds(at + 8, 8), :] = kap[pl.ds(NA + g * 128 + row, 8, stride=NA), :]

    lat_count = jnp.where(lat > 0, 1, 0) + jnp.where(lat < nlat - 1, 1, 0)
    pl.semaphore_wait(barrier, steps - 1 + 2 + lat_count)

    def lat_rows(d):
        return pl.ds(0, 16) if d < 2 else pl.ds(16, 2 * levels - 16)

    def side_copy(d):
        if d in (2, 3):
            return remote(lon_out, lon_in.at[3 - d], side_s.at[d], side_r.at[5 - d], sides[d][1])
        e = d % 2
        return remote(
            lat_out.at[e, lat_rows(d)], lat_in.at[1 - e, lat_rows(d)], side_s.at[d], side_r.at[d + 1 - 2 * e], sides[e][1]
        )

    def side_arrival(d):
        if d in (2, 3):
            return remote(lon_out, lon_in.at[d - 2], side_s.at[d], side_r.at[d], sides[d][1])
        e = d % 2
        return remote(lat_out.at[e, lat_rows(d)], lat_in.at[e, lat_rows(d)], side_s.at[d], side_r.at[d], sides[e][1])

    def side_there(d):
        return None if d in (2, 3) else sides[d % 2][0]

    for d in (2, 3, 0, 1, 4, 5):
        guarded(side_there(d), lambda d=d: side_copy(d).start())

    def order(i, at):
        odd = lax.rem(i, 2)
        away = zs // 2 + (1 - odd) * lax.div(i, 2) - odd * lax.div(i + 1, 2)
        return lax.rem(at + away, zs)

    rows = LP * NA

    def shift_copy(i):
        part = pl.ds(pl.multiple_of(order(i, z) * rows, 8), rows)
        return remote(u_hbm.at[part, :], pbuf.at[part, :], shift_s.at[i], shift_r.at[i], {"tm": me + 1 - 2 * xl})

    @pl.when(xl == 0)
    def _():
        for i in range(zs):
            shift_copy(i).start()

    sends_state = z < zs - 1
    relayed = min(5, zs // 2 + 1)

    def state_parts(i, x):
        return u_parts.at[pl.ds(order(i, z) * LP, LP), lax.rem(x + lat, 2)]

    def relay_copy(i):
        return remote(state_parts(i, 0), relay.at[i], relay_s.at[i], relay_r.at[i], {"tm": me + 1 - 2 * xl})

    def state_copy(i):
        to = order(i, z) * 2 + 1
        return remote(state_parts(i, 1), ur.at[z], state_s.at[i], state_r.at[z], {"tm": to})

    def direct_copy(i):
        return remote(state_parts(i, 0), ur.at[z], relay_s.at[i], state_r.at[z], {"tm": order(i, z) * 2})

    def forward_copy(i):
        return remote(relay.at[i], ur.at[z], state_s.at[i], state_r.at[z], {"tm": order(i, z) * 2})

    @pl.when(jnp.logical_and(xl == 1, sends_state))
    def _():
        for i in range(zs):
            if i < relayed:
                relay_copy(i).start()
            if i < zs - 1:
                state_copy(i).start()
            if i >= relayed:
                direct_copy(i).start()
        for l in range(LP):
            row = pl.multiple_of((z * LP + l) * NA + q * 8, 8)
            ur[z, l] = u_ref[pl.ds(row, 8), :]

    forwards = jnp.logical_and(xl == 0, sends_state)

    @pl.when(forwards)
    def _():
        for i in range(relayed):
            relay_copy(i).wait_recv()
            forward_copy(i).start()

    take_h.wait()

    @pl.when(me == 0)
    def _():
        take_init.wait()

    for d in range(4):
        guarded(side_there(d), lambda d=d: side_arrival(d).wait_recv())
    for group in range((levels + 31) // 32):
        for f in range(2):
            lon_mix[group, f] = jnp.where(odd_lane, lon_in[1, group, f], lon_in[0, group, f])

    gamma = [CORNER ** (n / steps) for n in range(steps)]
    scale = pick(me, gamma)

    def fwd_copy(part, zd, to):
        return remote(
            rs.at[part, pl.ds(pl.multiple_of(zd * 64, 8), 64), :], rr.at[me], fwd_s.at[to], fwd_r.at[me], {"tm": to}
        )

    def chunk(i, carry):
        zd = order(i, z)

        @pl.when(i == 1)
        def _():
            for d in (4, 5):
                guarded(side_there(d), lambda d=d: side_arrival(d).wait_recv())

        @pl.when(xl == 1)
        def _():
            shift_copy(i).wait_recv()

        def level(l):
            lev = zd * LP + l
            base = pl.multiple_of(lev * NA, 8)
            under = pl.multiple_of(jnp.maximum(lev - 1, 0) * NA, 8)
            over = pl.multiple_of(jnp.minimum(lev + 1, levels - 1) * NA, 8)
            group = lax.div(lev, 32)
            fields = []
            for f, ref, low, mid, high in (
                (0, u_ref, under, base, over),
                (1, kap, base, base + NA, base + 2 * NA),
            ):
                tile = [ref[pl.ds(mid + 8 * t, 8), :] for t in range(2)]
                down = [ref[pl.ds(low + 8 * t, 8), :] for t in range(2)]
                up = [ref[pl.ds(high + 8 * t, 8), :] for t in range(2)]
                row = [
                    jnp.broadcast_to(lat_in[s, pl.ds(i * 16 + f * 8 + l, 1), :], (8, NX)) for s in range(2)
                ]
                one = [pltpu.roll(tile[t], 1, 0) for t in range(2)]
                seven = [pltpu.roll(tile[t], 7, 0) for t in range(2)]
                before = [jnp.where(sub == 0, row[0], one[0]), jnp.where(sub == 0, one[0], one[1])]
                after = [jnp.where(sub == 7, seven[1], seven[0]), jnp.where(sub == 7, row[1], seven[1])]
                ends = lon_mix[group, f]
                west, east = [], []
                for t in range(2):
                    halo = pltpu.roll(ends, NX - 1 - 2 * (lax.rem(lev, 32) * 2 + t), 1)
                    west.append(pltpu.roll(jnp.where(last_lane, halo, tile[t]), 1, 1))
                    east.append(pltpu.roll(jnp.where(first_lane, halo, tile[t]), NX - 1, 1))
                fields.append((tile, (down, up, before, after, west, east)))
            (u, u_near), (k, k_near) = fields
            for t in range(2):
                at = pl.multiple_of(l * NA, 8) + 8 * t
                total = None
                for f in range(6):
                    w = harmonic(k[t], k_near[f][t])
                    wts[f, pl.ds(at, 8), :] = w
                    term = w * (u_near[f][t] - u[t])
                    total = term if total is None else total + term
                r = (h_ref[pl.ds(base + 8 * t, 8), :] + pbuf[pl.ds(base + 8 * t, 8), :]) - (u[t] - total)
                rs[t, pl.ds(pl.multiple_of(lev * 8, 8), 8), :] = r * scale

        def some_levels(m, carry):
            for l in range(4):
                level(m * 4 + l)
            return carry

        lax.fori_loop(0, LP // 4, some_levels, 0)
        for part in range(2):
            to = zd * 2 + lax.rem(part + lat, 2)

            @pl.when(to != me)
            def _():
                fwd_copy(part, zd, to).start()

            @pl.when(to == me)
            def _():
                rr[me] = rs[part, pl.ds(pl.multiple_of(zd * 64, 8), 64), :]

        return carry

    lax.fori_loop(0, zs, chunk, 0)

    beta = CORNER ** (1.0 / steps)
    shift_re = [1.0 - beta * math.cos(2 * math.pi * k / steps) for k in range(half + 1)]
    shift_im = [beta * math.sin(2 * math.pi * k / steps) for k in range(half + 1)]

    def invert(l, carry):
        at = pl.multiple_of(l * NA + q * 8, 8)
        total = None
        for f in range(6):
            w = wts[f, pl.ds(at, 8), :]
            own[f, l] = w
            total = w if total is None else total + w
        for k in range(half + 1):
            re = total + shift_re[k]
            if k in (0, half):
                value = 1.0 / re
                row = 0 if k == 0 else 8
                coef[pl.ds(l * 192 + row, 8, stride=24), :] = value
                if k == 0:
                    coef[pl.ds(l * 192 + 16, 8, stride=24), :] = zero
            else:
                share = 1.0 / (re * re + shift_im[k] * shift_im[k])
                real = re * share
                coef[pl.ds(l * 192 + k, 8, stride=24), :] = real
                coef[pl.ds(l * 192 + 8 + k, 8, stride=24), :] = real
                coef[pl.ds(l * 192 + 16 + k, 8, stride=24), :] = share * (-shift_im[k])
        return carry

    lax.fori_loop(0, LP, invert, 0)

    def await_fwd(d, carry):
        src = lax.rem(me + d, steps)
        remote(rs.at[0, pl.ds(0, 64), :], rr.at[src], fwd_s.at[src], fwd_r.at[src], {"tm": src}).wait_recv()
        return carry

    lax.fori_loop(1, steps, await_fwd, 0)
    for i in range(zs - 1):

        @pl.when(jnp.logical_or(z != i, xl == 0))
        def _():
            remote(relay.at[0], ur.at[i], state_s.at[i], state_r.at[i], {"tm": 2 * i + xl}).wait_recv()

    def sent_index(m, s):
        return 2 + 2 * m + s

    def inner_index(m, s):
        return jnp.where(m == LP // 2 - 1, LP + 1 - s, 4 + 2 * m + s)

    def level_of(m, s):
        return m + s * (LP - 1 - 2 * m)

    def divide(l, a, re, im):
        at = pl.multiple_of((l * 8 + a) * 24, 8)
        c_re, c_im, cross = (coef[pl.ds(at + 8 * i, 8), :] for i in range(3))
        return re * c_re - im * cross, im * c_im + re * cross

    def turn(tile, by):
        return tile if by % NX == 0 else pltpu.roll(tile, by % NX, 1)

    class Packed:
        def __init__(self):
            self.parts = [zero, zero]

        def add(self, p, a, f, tile):
            j = (p * AP + a) * 2 + f
            turned = pltpu.roll(tile, 2 * j + 1, 1)
            self.parts[f] = jnp.where(lane_pair == j, turned, self.parts[f])
            return turned

        def value(self):
            return jnp.where(lax.rem(lane_pair, 2) == 0, self.parts[0], self.parts[1])

    inner = pl.ds(1, AP)

    def lev_copy(b, d):
        return remote(
            xe[b].at[2 + d, inner], xe[b].at[1 - d, inner], lev_s.at[b, d], lev_r.at[b, 1 - d], lev_sides[d][1]
        )

    def lev_arrival(b, d):
        return remote(xe[b].at[2 + d, inner], xe[b].at[d, inner], lev_s.at[b, d], lev_r.at[b, d], lev_sides[d][1])

    def lat_copy(b, m, d, at=0, count=4):
        pair = pl.ds(2 + 4 * m + at, count)
        return remote(
            xe[b].at[pair, 1 + d * (AP - 1)], xe[b].at[pair, (1 - d) * (AP + 1)],
            lat_s.at[b, m, d], lat_r.at[b, m, 1 - d], lat_sides[d][1],
        )

    def lat_arrival(b, m, d):
        pair = pl.ds(2 + 4 * m, 4)
        return remote(
            xe[b].at[pair, 1 + d * (AP - 1)], xe[b].at[pair, d * (AP + 1)],
            lat_s.at[b, m, d], lat_r.at[b, m, d], lat_sides[d][1],
        )

    def lon_copy(b, m, d):
        return remote(
            edge_out.at[b, m], edge_in.at[b, m, 1 - d], lon_s.at[b, m, d], lon_r.at[b, m, 1 - d], lon_sides[d][1]
        )

    def lon_arrival(b, m, d):
        return remote(edge_out.at[b, m], edge_in.at[b, m, d], lon_s.at[b, m, d], lon_r.at[b, m, d], lon_sides[d][1])

    def send_edges(b, m, packed):
        edge_out[b, m] = packed.value()

        for d in range(2):
            lon_copy(b, m, d).start()
        for d in range(2):
            guarded(lat_sides[d][0], lambda d=d: lat_copy(b, m, d, 2, 2).start())

    def send_levels(b, m):
        for d in range(2):
            guarded(lat_sides[d][0], lambda d=d: lat_copy(b, m, d, 0, 2).start())

        @pl.when(m == 0)
        def _():
            for d in range(2):
                guarded(lev_sides[d][0], lambda d=d: lev_copy(b, d).start())

    def await_edges(b, m):
        @pl.when(m == 0)
        def _():
            for d in range(2):
                guarded(lev_sides[d][0], lambda d=d: lev_arrival(b, d).wait_recv())

        for d in range(2):
            guarded(lat_sides[d][0], lambda d=d: lat_arrival(b, m, d).wait_recv())
        for d in range(2):
            lon_arrival(b, m, d).wait_recv()

    members = ((0, 0), (0, 1), (1, 0), (1, 1))

    def to_spectrum(g, carry):
        packed = Packed()
        for mm, s in members:
            l = level_of(2 * g + mm, s)
            at = pl.multiple_of(l * 8, 8)
            r = [rr[n, pl.ds(at, 8), :] for n in range(steps)]
            for n in range(2, steps, 2):
                r[n] = r[n] + ur[n // 2 - 1, l] * gamma[n]
            e = [r[0]] + [r[n] + r[steps - n] for n in range(1, half)] + [r[half]]
            o = [r[n] - r[steps - n] for n in range(1, half)]
            real = cosine_sums(e, steps)
            imag = sine_sums(o, steps)
            for k in range(half):
                spec[pl.ds(l * 128 + k, 8, stride=16), :] = real[k]
            spec[pl.ds(l * 128 + 8, 8, stride=16), :] = real[half]
            for k in range(1, half):
                spec[pl.ds(l * 128 + 8 + k, 8, stride=16), :] = -imag[k - 1]
        for p, (mm, s) in enumerate(members):
            m = 2 * g + mm
            l = level_of(m, s)
            for a in range(AP):
                row = pl.multiple_of((l * 8 + a) * 16, 8)
                x = divide(l, a, spec[pl.ds(row, 8), :], spec[pl.ds(row + 8, 8), :])
                for f in range(2):
                    xe[0][sent_index(m, s), a + 1, pl.ds(8 * f, 8), :] = x[f]
                    rot[0][sent_index(m, s), a, pl.ds(8 * f, 8), :] = packed.add(p, a, f, x[f])
            if p == 1:
                send_levels(0, g)
        send_edges(0, g, packed)
        return carry

    lax.fori_loop(0, GROUPS, to_spectrum, 0)

    def back_copy(to, first, count):
        part = pl.ds(pl.multiple_of(first, 8), count)
        return remote(ws.at[to, part], wb.at[me, part], back_s.at[to], back_r.at[me], {"tm": to})

    def from_spectrum(g, p):
        base = p * 128
        x = [xf[pl.ds(base + k, 8, stride=16), :] for k in range(half)]
        x_half = xf[pl.ds(base + 8, 8, stride=16), :]
        y = [xf[pl.ds(base + 8 + k, 8, stride=16), :] for k in range(1, half)]
        even = cosine_sums([x[0] * 0.5] + x[1:] + [x_half * 0.5], steps)
        odd = sine_sums(y, steps)
        at = pl.ds(pl.multiple_of(g * 32, 8) + p * 8, 8)
        ws[0, at, :] = even[0]
        ws[half, at, :] = even[half]
        for n in range(1, half):
            ws[n, at, :] = even[n] - odd[n - 1]
            ws[steps - n, at, :] = even[n] + odd[n - 1]

    def sweep(b, last):
        def some_pairs(g, carry):
            await_edges(b, g)
            ends = jnp.where(odd_lane, edge_in[b, g, 1], edge_in[b, g, 0])
            packed = Packed()
            for p, (mm, s) in enumerate(members):
                m = 2 * g + mm
                l = level_of(m, s)
                i = sent_index(m, s)
                beyond = (i - 2, inner_index(m, s))
                under, over = beyond if s == 0 else beyond[::-1]
                for a in range(AP):
                    w = [
                        jnp.broadcast_to(own[f, l, pl.ds(a, 1), :], (8, NX)) for f in range(6)
                    ]
                    row = pl.multiple_of((l * 8 + a) * 16, 8)
                    rhs = []
                    for f in range(2):
                        part = pl.ds(8 * f, 8)
                        j = (p * AP + a) * 2 + f
                        turned = rot[b][i, a, part, :]
                        west = jnp.where(lane == 2 * j, ends, turned)
                        east = jnp.where(lane == 2 * j + 1, ends, turned)
                        total = spec[pl.ds(row + 8 * f, 8), :]
                        total = total + w[0] * xe[b][under, a + 1, part, :] + w[1] * xe[b][over, a + 1, part, :]
                        total = total + w[2] * xe[b][i, a, part, :] + w[3] * xe[b][i, a + 2, part, :]
                        total = total + w[4] * turn(west, NX - 2 * j) + w[5] * turn(east, NX - 2 * j - 2)
                        rhs.append(total)
                    x = divide(l, a, rhs[0], rhs[1])
                    for f in range(2):
                        if last:
                            xf[pl.ds((p * AP + a) * 16 + 8 * f, 8), :] = x[f]
                        else:
                            xe[b + 1][i, a + 1, pl.ds(8 * f, 8), :] = x[f]
                            rot[b + 1][i, a, pl.ds(8 * f, 8), :] = packed.add(p, a, f, x[f])
                if p == 1 and not last:
                    send_levels(b + 1, g)
            if not last:
                send_edges(b + 1, g, packed)
            else:
                for p in range(4):
                    from_spectrum(g, p)

                def send(i, carry):
                    odd = lax.rem(i, 2)
                    d = half + (1 - odd) * lax.div(i, 2) - odd * lax.div(i + 1, 2)
                    back_copy(lax.rem(me + d, steps), g * 32, 32).start()
                    return carry

                lax.fori_loop(0, steps - 1, send, 0)
            return carry

        lax.fori_loop(0, GROUPS, some_pairs, 0)

    for b in range(SWEEPS):
        sweep(b, b == SWEEPS - 1)

    wb[me] = ws[me]
    share = pick(me, [2.0 / (steps * g) for g in gamma])

    def finish(i, carry):
        odd = lax.rem(i, 2)
        away = lax.div(i + 1, 2)
        src = lax.rem(me + steps + odd * away - (1 - odd) * away, steps)
        zz = lax.div(src, 2)
        part = lax.rem(lax.rem(src, 2) + lat, 2)

        @pl.when(i > 0)
        def _():
            remote(ws.at[src], wb.at[src], back_s.at[src], back_r.at[src], {"tm": src}).wait_recv()

        for m in range(LP // 2):
            for s in range(2):
                at = pl.multiple_of((zz * LP + level_of(m, s)) * NA + part * 8, 8)
                out_ref[pl.ds(at, 8), :] = u_ref[pl.ds(at, 8), :] + wb[src, pl.ds(m * 16 + s * 8, 8), :] * share
        return carry

    lax.fori_loop(0, steps, finish, 0)

    @pl.when(xl == 0)
    def _():
        for i in range(zs):
            shift_copy(i).wait_send()

    for d in range(6):
        guarded(side_there(d), lambda d=d: side_copy(d).wait_send())

    def sent(d, carry):
        to = lax.rem(me + d, steps)
        fwd_copy(0, 0, to).wait_send()
        back_copy(to, 0, 64).wait_send()
        return carry

    lax.fori_loop(1, steps, sent, 0)

    @pl.when(forwards)
    def _():
        for i in range(relayed):
            forward_copy(i).wait_send()

    @pl.when(jnp.logical_and(xl == 1, sends_state))
    def _():
        for i in range(zs):
            relay_copy(i).wait_send()
            if i < zs - 1:
                state_copy(i).wait_send()

    for b in range(SWEEPS):
        for d in range(2):
            guarded(lev_sides[d][0], lambda b=b, d=d: lev_copy(b, d).wait_send())

        def edges_sent(m, carry, b=b):
            for d in range(2):
                guarded(lat_sides[d][0], lambda d=d: lat_copy(b, m, d).wait_send())
                lon_copy(b, m, d).wait_send()
            return carry

        lax.fori_loop(0, GROUPS, edges_sent, 0)


def on_device(steps, nlat, nlon, iterate, heating, initial, region, cond_table):
    levels = initial.shape[0]
    rows = levels * NA
    zs = steps // 2
    groups = (levels + 31) // 32
    vmem = pl.BlockSpec(memory_space=pltpu.VMEM)
    anywhere = pl.BlockSpec(memory_space=pl.ANY)
    flat = lambda value: value.reshape(rows, NX)
    dma = pltpu.SemaphoreType.DMA
    out = pl.pallas_call(
        functools.partial(kernel, steps, nlat, nlon),
        out_shape=jax.ShapeDtypeStruct((rows, NX), F32),
        in_specs=[anywhere] * 6,
        out_specs=vmem,
        scratch_shapes=[
            pltpu.SMEM(cond_table.shape, F32),
            pltpu.VMEM((rows, NX), F32),
            pltpu.VMEM((rows, NX), F32),
            pltpu.VMEM((rows, NX), jnp.int32),
            pltpu.VMEM((rows + 2 * NA, NX), F32),
            pltpu.VMEM((6, LP * NA, NX), F32),
            pltpu.VMEM((6, LP, AP, NX), F32),
            pltpu.VMEM((rows, NX), F32),
            pltpu.VMEM((2, 2 * levels, NX), F32),
            pltpu.VMEM((2, 2 * levels, NX), F32),
            pltpu.VMEM((groups, 2, 8, NX), F32),
            pltpu.VMEM((2, groups, 2, 8, NX), F32),
            pltpu.VMEM((groups, 2, 8, NX), F32),
            pltpu.VMEM((2, levels * 8, NX), F32),
            pltpu.VMEM((steps, 64, NX), F32),
            pltpu.VMEM((zs, LP, 8, NX), F32),
            pltpu.VMEM((zs, LP, 8, NX), F32),
            pltpu.VMEM((64 * 16, NX), F32),
            pltpu.VMEM((64 * 24, NX), F32),
            *[pltpu.VMEM((LP + 2, AP + 2, 16, NX), F32) for _ in range(SWEEPS)],
            *[pltpu.VMEM((LP + 2, AP, 16, NX), F32) for _ in range(SWEEPS)],
            pltpu.VMEM((32 * 16, NX), F32),
            pltpu.VMEM((SWEEPS, GROUPS, 8, NX), F32),
            pltpu.VMEM((SWEEPS, GROUPS, 2, 8, NX), F32),
            pltpu.VMEM((steps, 64, NX), F32),
            pltpu.VMEM((steps, 64, NX), F32),
            dma((5,)),
            dma((zs,)),
            dma((zs,)),
            dma((6,)),
            dma((6,)),
            dma((zs,)),
            dma((zs,)),
            dma((zs,)),
            dma((zs,)),
            dma((steps,)),
            dma((steps,)),
            dma((SWEEPS, 2)),
            dma((SWEEPS, 2)),
            dma((SWEEPS, GROUPS, 2)),
            dma((SWEEPS, GROUPS, 2)),
            dma((SWEEPS, GROUPS, 2)),
            dma((SWEEPS, GROUPS, 2)),
            dma((steps,)),
            dma((steps,)),
        ],
        compiler_params=pltpu.CompilerParams(
            collective_id=0, has_side_effects=True, vmem_limit_bytes=VMEM_LIMIT
        ),
    )(*(
        pltpu.with_memory_space_constraint(value, pltpu.HBM)
        for value in (
            flat(iterate), iterate.reshape(levels, 2, AP, NX), flat(heating), flat(region), flat(initial), cond_table
        )
    ))
    return out.reshape(iterate.shape)


def solution(mesh):
    sizes = mesh.shape
    return jax.shard_map(
        functools.partial(on_device, sizes["tm"], sizes["lat"], sizes["lon"]),
        mesh=mesh,
        in_specs=(
            P("tm", None, "lat", "lon"),
            P("tm", None, "lat", "lon"),
            P(None, "lat", "lon"),
            P(None, "lat", "lon"),
            P(),
        ),
        out_specs=P("tm", None, "lat", "lon"),
        check_vma=False,
    )
```

```python
import functools
import math

import jax
import jax.numpy as jnp
from jax import lax
from jax.experimental import pallas as pl
from jax.experimental.pallas import tpu as pltpu
from jax.sharding import PartitionSpec as P

MESH = pl.DeviceIdType.MESH
F32 = jnp.float32
CORNER = 0.1
SWEEPS = 3
LP = 8
GROUPS = 2
AP = 8
NA = 16
NX = 128
VMEM_LIMIT = 40 * 1024 * 1024


def harmonic(first, second):
    return 2.0 * first * second / (first + second)


def weighted(pairs):
    total = None
    for coefficient, value in pairs:
        if abs(coefficient) < 1e-12:
            continue
        if abs(coefficient - 1.0) < 1e-12:
            term = value
        elif abs(coefficient + 1.0) < 1e-12:
            total = -value if total is None else total - value
            continue
        else:
            term = value * coefficient
        total = term if total is None else total + term
    return total


def cosine_sums(e, n):
    half, quarter = n // 2, n // 4
    even = [e[m] + e[half - m] for m in range(quarter)]
    odd = [e[m] - e[half - m] for m in range(quarter)]
    out = []
    for k in range(half + 1):
        parts = even if k % 2 == 0 else odd
        pairs = [(math.cos(2 * math.pi * k * m / n), parts[m]) for m in range(quarter)]
        pairs.append((math.cos(2 * math.pi * k * quarter / n), e[quarter]))
        out.append(weighted(pairs))
    return out


def sine_sums(o, n):
    half, quarter = n // 2, n // 4
    plus = [o[m - 1] + o[half - m - 1] for m in range(1, quarter)]
    minus = [o[m - 1] - o[half - m - 1] for m in range(1, quarter)]
    out = []
    for k in range(1, half):
        parts = plus if k % 2 == 1 else minus
        pairs = [(math.sin(2 * math.pi * k * m / n), parts[m - 1]) for m in range(1, quarter)]
        pairs.append((math.sin(2 * math.pi * k * quarter / n), o[quarter - 1]))
        total = weighted(pairs)
        out.append(total if total is not None else jnp.zeros_like(o[0]))
    return out


def pick(index, values):
    chosen = jnp.float32(values[0])
    for i, value in enumerate(values):
        if i > 0:
            chosen = jnp.where(index == i, jnp.float32(value), chosen)
    return chosen


def kernel(
    steps, nlat, nlon,
    u_hbm, u_parts, h_hbm, reg_hbm, init_hbm, table_hbm, out_ref,
    table_ref, u_ref, h_ref, reg_ref, kap, wts, own, pbuf, lat_out, lat_in, lon_out, lon_in, lon_mix,
    rs, rr, ur, relay, spec, coef, xe0, xe1, xe2, rot0, rot1, rot2, xf, edge_out, edge_in, ws, wb,
    local, shift_s, shift_r, side_s, side_r, relay_s, relay_r, state_s, state_r, fwd_s, fwd_r,
    lev_s, lev_r, lat_s, lat_r, lon_s, lon_r, back_s, back_r,
):
    levels = u_ref.shape[0] // NA
    xe = (xe0, xe1, xe2)
    rot = (rot0, rot1, rot2)
    zs = steps // 2
    half = steps // 2
    me = lax.axis_index("tm")
    lat = lax.axis_index("lat")
    lon = lax.axis_index("lon")
    z = lax.div(me, 2)
    xl = lax.rem(me, 2)
    q = lax.rem(xl + lat, 2)
    left = lax.rem(lon + nlon - 1, nlon)
    right = lax.rem(lon + 1, nlon)
    sub = lax.broadcasted_iota(jnp.int32, (8, NX), 0)
    lane = lax.broadcasted_iota(jnp.int32, (8, NX), 1)
    lane_pair = lax.div(lane, 2)
    odd_lane = lax.rem(lane, 2) == 1
    first_lane = lane == 0
    last_lane = lane == NX - 1
    zero = jnp.zeros((8, NX), F32)

    def remote(src, dst, send, recv, device):
        return pltpu.make_async_remote_copy(
            src_ref=src, dst_ref=dst, send_sem=send, recv_sem=recv, device_id=device, device_id_type=MESH
        )

    def guarded(condition, act):
        if condition is None:
            act()
        else:
            pl.when(condition)(act)

    sides = (
        (lat > 0, {"lat": lat - 1}),
        (lat < nlat - 1, {"lat": lat + 1}),
        (None, {"lon": left}),
        (None, {"lon": right}),
    )
    x_low = xl * (1 - q) + (1 - xl) * q
    x_high = xl * q + (1 - xl) * (1 - q)
    lev_sides = ((z > 0, {"tm": me - 2}), (z < zs - 1, {"tm": me + 2}))
    lat_sides = (
        (q + lat > 0, {"tm": z * 2 + x_low, "lat": lat - (1 - q)}),
        ((1 - q) + (nlat - 1 - lat) > 0, {"tm": z * 2 + x_high, "lat": lat + q}),
    )
    lon_sides = ((None, {"lon": left}), (None, {"lon": right}))

    barrier = pltpu.get_barrier_semaphore()
    for d in range(1, steps):
        pl.semaphore_signal(barrier, inc=1, device_id={"tm": lax.rem(me + d, steps)}, device_id_type=MESH)
    for condition, device in sides:
        guarded(
            condition,
            functools.partial(pl.semaphore_signal, barrier, inc=1, device_id=device, device_id_type=MESH),
        )

    take_reg = pltpu.make_async_copy(reg_hbm, reg_ref, local.at[0])
    take_u = pltpu.make_async_copy(u_hbm, u_ref, local.at[1])
    take_h = pltpu.make_async_copy(h_hbm, h_ref, local.at[2])
    take_init = pltpu.make_async_copy(init_hbm, pbuf, local.at[3])
    take_table = pltpu.make_async_copy(table_hbm, table_ref, local.at[4])
    take_table.start()
    take_reg.start()
    take_u.start()
    take_h.start()

    @pl.when(me == 0)
    def _():
        take_init.start()

    for b in range(SWEEPS):
        for condition, place in (
            (z == 0, (b, 0, slice(None))),
            (z == zs - 1, (b, 1, slice(None))),
            (q + lat == 0, (b, slice(None), 0)),
            ((1 - q) + (nlat - 1 - lat) == 0, (b, slice(None), AP + 1)),
        ):
            def clear(place=place):
                xe[place[0]][place[1:]] = jnp.zeros((10, 16, NX), F32)

            pl.when(condition)(clear)

    @pl.when(lat == 0)
    def _():
        lat_in[0] = jnp.zeros(lat_in.shape[1:], F32)

    @pl.when(lat == nlat - 1)
    def _():
        lat_in[1] = jnp.zeros(lat_in.shape[1:], F32)

    @pl.when(jnp.logical_and(me > 0, xl == 0))
    def _():
        pbuf[...] = jnp.zeros(pbuf.shape, F32)

    kap[pl.ds(0, NA), :] = jnp.zeros((NA, NX), F32)
    kap[pl.ds((levels + 1) * NA, NA), :] = jnp.zeros((NA, NX), F32)
    take_table.wait()
    table = [table_ref[c] for c in range(8)]
    take_reg.wait()
    take_u.wait()

    for group in range((levels + 31) // 32):
        def conduct(g, packs):
            gathered = [zero, zero]
            for j in range(16):
                at = pl.multiple_of((group * 4 + g) * 128, 8) + j * 8
                reg = reg_ref[pl.ds(at, 8), :]
                k = jnp.full((8, NX), table[0], F32)
                for c in range(1, 8):
                    k = jnp.where(reg == c, table[c], k)
                kap[pl.ds(at + NA, 8), :] = k
                u = u_ref[pl.ds(at, 8), :]
                for f, tile in ((0, u), (1, k)):
                    gathered[f] = jnp.where(lane_pair == j, pltpu.roll(tile, 2 * j + 1, 1), gathered[f])
            mask = lax.div(lane, 32) == g
            return tuple(jnp.where(mask, pltpu.roll(gathered[f], g * 32, 1), packs[f]) for f in range(2))

        packs = lax.fori_loop(0, min(4, levels // 8 - 4 * group), conduct, (zero, zero))
        for f in range(2):
            lon_out[group, f] = packs[f]
    for g in range(zs):
        e = lax.rem(g + zs - z, zs) - zs // 2
        at = pl.multiple_of(jnp.where(e < 0, -2 * e - 1, 2 * e) * 16, 8)
        for side, row in ((0, 0), (1, NA - 1)):
            lat_out[side, pl.ds(at, 8), :] = u_ref[pl.ds(g * 128 + row, 8, stride=NA), :]
            lat_out[side, pl.ds(at + 8, 8), :] = kap[pl.ds(NA + g * 128 + row, 8, stride=NA), :]

    lat_count = jnp.where(lat > 0, 1, 0) + jnp.where(lat < nlat - 1, 1, 0)
    pl.semaphore_wait(barrier, steps - 1 + 2 + lat_count)

    def lat_rows(d):
        return pl.ds(0, 16) if d < 2 else pl.ds(16, 2 * levels - 16)

    def side_copy(d):
        if d in (2, 3):
            return remote(lon_out, lon_in.at[3 - d], side_s.at[d], side_r.at[5 - d], sides[d][1])
        e = d % 2
        return remote(
            lat_out.at[e, lat_rows(d)], lat_in.at[1 - e, lat_rows(d)], side_s.at[d], side_r.at[d + 1 - 2 * e], sides[e][1]
        )

    def side_arrival(d):
        if d in (2, 3):
            return remote(lon_out, lon_in.at[d - 2], side_s.at[d], side_r.at[d], sides[d][1])
        e = d % 2
        return remote(lat_out.at[e, lat_rows(d)], lat_in.at[e, lat_rows(d)], side_s.at[d], side_r.at[d], sides[e][1])

    def side_there(d):
        return None if d in (2, 3) else sides[d % 2][0]

    for d in (2, 3, 0, 1, 4, 5):
        guarded(side_there(d), lambda d=d: side_copy(d).start())

    def order(i, at):
        odd = lax.rem(i, 2)
        away = zs // 2 + (1 - odd) * lax.div(i, 2) - odd * lax.div(i + 1, 2)
        return lax.rem(at + away, zs)

    rows = LP * NA

    def shift_copy(i):
        part = pl.ds(pl.multiple_of(order(i, z) * rows, 8), rows)
        return remote(u_hbm.at[part, :], pbuf.at[part, :], shift_s.at[i], shift_r.at[i], {"tm": me + 1 - 2 * xl})

    @pl.when(xl == 0)
    def _():
        for i in range(zs):
            shift_copy(i).start()

    sends_state = z < zs - 1
    relayed = min(5, zs // 2 + 1)

    def state_parts(i, x):
        return u_parts.at[pl.ds(order(i, z) * LP, LP), lax.rem(x + lat, 2)]

    def relay_copy(i):
        return remote(state_parts(i, 0), relay.at[i], relay_s.at[i], relay_r.at[i], {"tm": me + 1 - 2 * xl})

    def state_copy(i):
        to = order(i, z) * 2 + 1
        return remote(state_parts(i, 1), ur.at[z], state_s.at[i], state_r.at[z], {"tm": to})

    def direct_copy(i):
        return remote(state_parts(i, 0), ur.at[z], relay_s.at[i], state_r.at[z], {"tm": order(i, z) * 2})

    def forward_copy(i):
        return remote(relay.at[i], ur.at[z], state_s.at[i], state_r.at[z], {"tm": order(i, z) * 2})

    @pl.when(jnp.logical_and(xl == 1, sends_state))
    def _():
        for i in range(zs):
            if i < relayed:
                relay_copy(i).start()
            if i < zs - 1:
                state_copy(i).start()
            if i >= relayed:
                direct_copy(i).start()
        for l in range(LP):
            row = pl.multiple_of((z * LP + l) * NA + q * 8, 8)
            ur[z, l] = u_ref[pl.ds(row, 8), :]

    forwards = jnp.logical_and(xl == 0, sends_state)

    @pl.when(forwards)
    def _():
        for i in range(relayed):
            relay_copy(i).wait_recv()
            forward_copy(i).start()

    take_h.wait()

    @pl.when(me == 0)
    def _():
        take_init.wait()

    for d in range(4):
        guarded(side_there(d), lambda d=d: side_arrival(d).wait_recv())
    for group in range((levels + 31) // 32):
        for f in range(2):
            lon_mix[group, f] = jnp.where(odd_lane, lon_in[1, group, f], lon_in[0, group, f])

    gamma = [CORNER ** (n / steps) for n in range(steps)]
    scale = pick(me, gamma)

    def fwd_copy(part, zd, to):
        return remote(
            rs.at[part, pl.ds(pl.multiple_of(zd * 64, 8), 64), :], rr.at[me], fwd_s.at[to], fwd_r.at[me], {"tm": to}
        )

    def chunk(i, carry):
        zd = order(i, z)

        @pl.when(i == 1)
        def _():
            for d in (4, 5):
                guarded(side_there(d), lambda d=d: side_arrival(d).wait_recv())

        @pl.when(xl == 1)
        def _():
            shift_copy(i).wait_recv()

        def level(l):
            lev = zd * LP + l
            base = pl.multiple_of(lev * NA, 8)
            under = pl.multiple_of(jnp.maximum(lev - 1, 0) * NA, 8)
            over = pl.multiple_of(jnp.minimum(lev + 1, levels - 1) * NA, 8)
            group = lax.div(lev, 32)
            fields = []
            for f, ref, low, mid, high in (
                (0, u_ref, under, base, over),
                (1, kap, base, base + NA, base + 2 * NA),
            ):
                tile = [ref[pl.ds(mid + 8 * t, 8), :] for t in range(2)]
                down = [ref[pl.ds(low + 8 * t, 8), :] for t in range(2)]
                up = [ref[pl.ds(high + 8 * t, 8), :] for t in range(2)]
                row = [
                    jnp.broadcast_to(lat_in[s, pl.ds(i * 16 + f * 8 + l, 1), :], (8, NX)) for s in range(2)
                ]
                one = [pltpu.roll(tile[t], 1, 0) for t in range(2)]
                seven = [pltpu.roll(tile[t], 7, 0) for t in range(2)]
                before = [jnp.where(sub == 0, row[0], one[0]), jnp.where(sub == 0, one[0], one[1])]
                after = [jnp.where(sub == 7, seven[1], seven[0]), jnp.where(sub == 7, row[1], seven[1])]
                ends = lon_mix[group, f]
                west, east = [], []
                for t in range(2):
                    halo = pltpu.roll(ends, NX - 1 - 2 * (lax.rem(lev, 32) * 2 + t), 1)
                    west.append(pltpu.roll(jnp.where(last_lane, halo, tile[t]), 1, 1))
                    east.append(pltpu.roll(jnp.where(first_lane, halo, tile[t]), NX - 1, 1))
                fields.append((tile, (down, up, before, after, west, east)))
            (u, u_near), (k, k_near) = fields
            for t in range(2):
                at = pl.multiple_of(l * NA, 8) + 8 * t
                total = None
                for f in range(6):
                    w = harmonic(k[t], k_near[f][t])
                    wts[f, pl.ds(at, 8), :] = w
                    term = w * (u_near[f][t] - u[t])
                    total = term if total is None else total + term
                r = (h_ref[pl.ds(base + 8 * t, 8), :] + pbuf[pl.ds(base + 8 * t, 8), :]) - (u[t] - total)
                rs[t, pl.ds(pl.multiple_of(lev * 8, 8), 8), :] = r * scale

        def some_levels(m, carry):
            for l in range(4):
                level(m * 4 + l)
            return carry

        lax.fori_loop(0, LP // 4, some_levels, 0)
        for part in range(2):
            to = zd * 2 + lax.rem(part + lat, 2)

            @pl.when(to != me)
            def _():
                fwd_copy(part, zd, to).start()

            @pl.when(to == me)
            def _():
                rr[me] = rs[part, pl.ds(pl.multiple_of(zd * 64, 8), 64), :]

        return carry

    lax.fori_loop(0, zs, chunk, 0)

    beta = CORNER ** (1.0 / steps)
    shift_re = [1.0 - beta * math.cos(2 * math.pi * k / steps) for k in range(half + 1)]
    shift_im = [beta * math.sin(2 * math.pi * k / steps) for k in range(half + 1)]

    def invert(l, carry):
        at = pl.multiple_of(l * NA + q * 8, 8)
        total = None
        for f in range(6):
            w = wts[f, pl.ds(at, 8), :]
            own[f, l] = w
            total = w if total is None else total + w
        for k in range(half + 1):
            re = total + shift_re[k]
            if k in (0, half):
                value = 1.0 / re
                row = 0 if k == 0 else 8
                coef[pl.ds(l * 192 + row, 8, stride=24), :] = value
                if k == 0:
                    coef[pl.ds(l * 192 + 16, 8, stride=24), :] = zero
            else:
                share = 1.0 / (re * re + shift_im[k] * shift_im[k])
                real = re * share
                coef[pl.ds(l * 192 + k, 8, stride=24), :] = real
                coef[pl.ds(l * 192 + 8 + k, 8, stride=24), :] = real
                coef[pl.ds(l * 192 + 16 + k, 8, stride=24), :] = share * (-shift_im[k])
        return carry

    lax.fori_loop(0, LP, invert, 0)

    def await_fwd(d, carry):
        src = lax.rem(me + d, steps)
        remote(rs.at[0, pl.ds(0, 64), :], rr.at[src], fwd_s.at[src], fwd_r.at[src], {"tm": src}).wait_recv()
        return carry

    lax.fori_loop(1, steps, await_fwd, 0)
    for i in range(zs - 1):

        @pl.when(jnp.logical_or(z != i, xl == 0))
        def _():
            remote(relay.at[0], ur.at[i], state_s.at[i], state_r.at[i], {"tm": 2 * i + xl}).wait_recv()

    def sent_index(m, s):
        return 2 + 2 * m + s

    def inner_index(m, s):
        return jnp.where(m == LP // 2 - 1, LP + 1 - s, 4 + 2 * m + s)

    def level_of(m, s):
        return m + s * (LP - 1 - 2 * m)

    def divide(l, a, re, im):
        at = pl.multiple_of((l * 8 + a) * 24, 8)
        c_re, c_im, cross = (coef[pl.ds(at + 8 * i, 8), :] for i in range(3))
        return re * c_re - im * cross, im * c_im + re * cross

    def turn(tile, by):
        return tile if by % NX == 0 else pltpu.roll(tile, by % NX, 1)

    class Packed:
        def __init__(self):
            self.parts = [zero, zero]

        def add(self, p, a, f, tile):
            j = (p * AP + a) * 2 + f
            turned = pltpu.roll(tile, 2 * j + 1, 1)
            self.parts[f] = jnp.where(lane_pair == j, turned, self.parts[f])
            return turned

        def value(self):
            return jnp.where(lax.rem(lane_pair, 2) == 0, self.parts[0], self.parts[1])

    inner = pl.ds(1, AP)

    def lev_copy(b, d):
        return remote(
            xe[b].at[2 + d, inner], xe[b].at[1 - d, inner], lev_s.at[b, d], lev_r.at[b, 1 - d], lev_sides[d][1]
        )

    def lev_arrival(b, d):
        return remote(xe[b].at[2 + d, inner], xe[b].at[d, inner], lev_s.at[b, d], lev_r.at[b, d], lev_sides[d][1])

    def lat_copy(b, m, d, at=0, count=4):
        pair = pl.ds(2 + 4 * m + at, count)
        return remote(
            xe[b].at[pair, 1 + d * (AP - 1)], xe[b].at[pair, (1 - d) * (AP + 1)],
            lat_s.at[b, m, d], lat_r.at[b, m, 1 - d], lat_sides[d][1],
        )

    def lat_arrival(b, m, d):
        pair = pl.ds(2 + 4 * m, 4)
        return remote(
            xe[b].at[pair, 1 + d * (AP - 1)], xe[b].at[pair, d * (AP + 1)],
            lat_s.at[b, m, d], lat_r.at[b, m, d], lat_sides[d][1],
        )

    def lon_copy(b, m, d):
        return remote(
            edge_out.at[b, m], edge_in.at[b, m, 1 - d], lon_s.at[b, m, d], lon_r.at[b, m, 1 - d], lon_sides[d][1]
        )

    def lon_arrival(b, m, d):
        return remote(edge_out.at[b, m], edge_in.at[b, m, d], lon_s.at[b, m, d], lon_r.at[b, m, d], lon_sides[d][1])

    def send_edges(b, m, packed):
        edge_out[b, m] = packed.value()

        for d in range(2):
            lon_copy(b, m, d).start()
        for d in range(2):
            guarded(lat_sides[d][0], lambda d=d: lat_copy(b, m, d, 2, 2).start())

    def send_levels(b, m):
        for d in range(2):
            guarded(lat_sides[d][0], lambda d=d: lat_copy(b, m, d, 0, 2).start())

        @pl.when(m == 0)
        def _():
            for d in range(2):
                guarded(lev_sides[d][0], lambda d=d: lev_copy(b, d).start())

    def await_edges(b, m):
        @pl.when(m == 0)
        def _():
            for d in range(2):
                guarded(lev_sides[d][0], lambda d=d: lev_arrival(b, d).wait_recv())

        for d in range(2):
            guarded(lat_sides[d][0], lambda d=d: lat_arrival(b, m, d).wait_recv())
        for d in range(2):
            lon_arrival(b, m, d).wait_recv()

    members = ((0, 0), (0, 1), (1, 0), (1, 1))

    def to_spectrum(g, carry):
        packed = Packed()
        for mm, s in members:
            l = level_of(2 * g + mm, s)
            at = pl.multiple_of(l * 8, 8)
            r = [rr[n, pl.ds(at, 8), :] for n in range(steps)]
            for n in range(2, steps, 2):
                r[n] = r[n] + ur[n // 2 - 1, l] * gamma[n]
            e = [r[0]] + [r[n] + r[steps - n] for n in range(1, half)] + [r[half]]
            o = [r[n] - r[steps - n] for n in range(1, half)]
            real = cosine_sums(e, steps)
            imag = sine_sums(o, steps)
            for k in range(half):
                spec[pl.ds(l * 128 + k, 8, stride=16), :] = real[k]
            spec[pl.ds(l * 128 + 8, 8, stride=16), :] = real[half]
            for k in range(1, half):
                spec[pl.ds(l * 128 + 8 + k, 8, stride=16), :] = -imag[k - 1]
        for p, (mm, s) in enumerate(members):
            m = 2 * g + mm
            l = level_of(m, s)
            for a in range(AP):
                row = pl.multiple_of((l * 8 + a) * 16, 8)
                x = divide(l, a, spec[pl.ds(row, 8), :], spec[pl.ds(row + 8, 8), :])
                for f in range(2):
                    xe[0][sent_index(m, s), a + 1, pl.ds(8 * f, 8), :] = x[f]
                    rot[0][sent_index(m, s), a, pl.ds(8 * f, 8), :] = packed.add(p, a, f, x[f])
            if p == 1:
                send_levels(0, g)
        send_edges(0, g, packed)
        return carry

    lax.fori_loop(0, GROUPS, to_spectrum, 0)

    def back_copy(to, first, count):
        part = pl.ds(pl.multiple_of(first, 8), count)
        return remote(ws.at[to, part], wb.at[me, part], back_s.at[to], back_r.at[me], {"tm": to})

    def from_spectrum(g, p):
        base = p * 128
        x = [xf[pl.ds(base + k, 8, stride=16), :] for k in range(half)]
        x_half = xf[pl.ds(base + 8, 8, stride=16), :]
        y = [xf[pl.ds(base + 8 + k, 8, stride=16), :] for k in range(1, half)]
        even = cosine_sums([x[0] * 0.5] + x[1:] + [x_half * 0.5], steps)
        odd = sine_sums(y, steps)
        at = pl.ds(pl.multiple_of(g * 32, 8) + p * 8, 8)
        ws[0, at, :] = even[0]
        ws[half, at, :] = even[half]
        for n in range(1, half):
            ws[n, at, :] = even[n] - odd[n - 1]
            ws[steps - n, at, :] = even[n] + odd[n - 1]

    def sweep(b, last):
        def some_pairs(g, carry):
            await_edges(b, g)
            ends = jnp.where(odd_lane, edge_in[b, g, 1], edge_in[b, g, 0])
            packed = Packed()
            for p, (mm, s) in enumerate(members):
                m = 2 * g + mm
                l = level_of(m, s)
                i = sent_index(m, s)
                beyond = (i - 2, inner_index(m, s))
                under, over = beyond if s == 0 else beyond[::-1]
                for a in range(AP):
                    w = [
                        jnp.broadcast_to(own[f, l, pl.ds(a, 1), :], (8, NX)) for f in range(6)
                    ]
                    row = pl.multiple_of((l * 8 + a) * 16, 8)
                    rhs = []
                    for f in range(2):
                        part = pl.ds(8 * f, 8)
                        j = (p * AP + a) * 2 + f
                        turned = rot[b][i, a, part, :]
                        west = jnp.where(lane == 2 * j, ends, turned)
                        east = jnp.where(lane == 2 * j + 1, ends, turned)
                        total = spec[pl.ds(row + 8 * f, 8), :]
                        total = total + w[0] * xe[b][under, a + 1, part, :] + w[1] * xe[b][over, a + 1, part, :]
                        total = total + w[2] * xe[b][i, a, part, :] + w[3] * xe[b][i, a + 2, part, :]
                        total = total + w[4] * turn(west, NX - 2 * j) + w[5] * turn(east, NX - 2 * j - 2)
                        rhs.append(total)
                    x = divide(l, a, rhs[0], rhs[1])
                    for f in range(2):
                        if last:
                            xf[pl.ds((p * AP + a) * 16 + 8 * f, 8), :] = x[f]
                        else:
                            xe[b + 1][i, a + 1, pl.ds(8 * f, 8), :] = x[f]
                            rot[b + 1][i, a, pl.ds(8 * f, 8), :] = packed.add(p, a, f, x[f])
                if p == 1 and not last:
                    send_levels(b + 1, g)
            if not last:
                send_edges(b + 1, g, packed)
            else:
                for p in range(4):
                    from_spectrum(g, p)

                def send(i, carry):
                    odd = lax.rem(i, 2)
                    d = half + (1 - odd) * lax.div(i, 2) - odd * lax.div(i + 1, 2)
                    back_copy(lax.rem(me + d, steps), g * 32, 32).start()
                    return carry

                lax.fori_loop(0, steps - 1, send, 0)
            return carry

        lax.fori_loop(0, GROUPS, some_pairs, 0)

    for b in range(SWEEPS):
        sweep(b, b == SWEEPS - 1)

    @pl.when(xl == 0)
    def _():
        for i in range(zs):
            shift_copy(i).wait_send()

    for d in range(6):
        guarded(side_there(d), lambda d=d: side_copy(d).wait_send())

    def sent(d, carry):
        to = lax.rem(me + d, steps)
        fwd_copy(0, 0, to).wait_send()
        return carry

    lax.fori_loop(1, steps, sent, 0)

    @pl.when(forwards)
    def _():
        for i in range(relayed):
            forward_copy(i).wait_send()

    @pl.when(jnp.logical_and(xl == 1, sends_state))
    def _():
        for i in range(zs):
            relay_copy(i).wait_send()
            if i < zs - 1:
                state_copy(i).wait_send()

    for b in range(SWEEPS):
        for d in range(2):
            guarded(lev_sides[d][0], lambda b=b, d=d: lev_copy(b, d).wait_send())

        def edges_sent(m, carry, b=b):
            for d in range(2):
                guarded(lat_sides[d][0], lambda d=d: lat_copy(b, m, d).wait_send())
                lon_copy(b, m, d).wait_send()
            return carry

        lax.fori_loop(0, GROUPS, edges_sent, 0)

    wb[me] = ws[me]
    share = pick(me, [2.0 / (steps * g) for g in gamma])

    def finish(i, carry):
        odd = lax.rem(i, 2)
        away = lax.div(i + 1, 2)
        src = lax.rem(me + steps + odd * away - (1 - odd) * away, steps)
        zz = lax.div(src, 2)
        part = lax.rem(lax.rem(src, 2) + lat, 2)

        @pl.when(i > 0)
        def _():
            remote(ws.at[src], wb.at[src], back_s.at[src], back_r.at[src], {"tm": src}).wait_recv()

        for m in range(LP // 2):
            for s in range(2):
                at = pl.multiple_of((zz * LP + level_of(m, s)) * NA + part * 8, 8)
                out_ref[pl.ds(at, 8), :] = u_ref[pl.ds(at, 8), :] + wb[src, pl.ds(m * 16 + s * 8, 8), :] * share
        return carry

    lax.fori_loop(0, steps, finish, 0)

    def returned(d, carry):
        back_copy(lax.rem(me + d, steps), 0, 64).wait_send()
        return carry

    lax.fori_loop(1, steps, returned, 0)


def on_device(steps, nlat, nlon, iterate, heating, initial, region, cond_table):
    levels = initial.shape[0]
    rows = levels * NA
    zs = steps // 2
    groups = (levels + 31) // 32
    vmem = pl.BlockSpec(memory_space=pltpu.VMEM)
    anywhere = pl.BlockSpec(memory_space=pl.ANY)
    flat = lambda value: value.reshape(rows, NX)
    dma = pltpu.SemaphoreType.DMA
    out = pl.pallas_call(
        functools.partial(kernel, steps, nlat, nlon),
        out_shape=jax.ShapeDtypeStruct((rows, NX), F32),
        in_specs=[anywhere] * 6,
        out_specs=vmem,
        scratch_shapes=[
            pltpu.SMEM(cond_table.shape, F32),
            pltpu.VMEM((rows, NX), F32),
            pltpu.VMEM((rows, NX), F32),
            pltpu.VMEM((rows, NX), jnp.int32),
            pltpu.VMEM((rows + 2 * NA, NX), F32),
            pltpu.VMEM((6, LP * NA, NX), F32),
            pltpu.VMEM((6, LP, AP, NX), F32),
            pltpu.VMEM((rows, NX), F32),
            pltpu.VMEM((2, 2 * levels, NX), F32),
            pltpu.VMEM((2, 2 * levels, NX), F32),
            pltpu.VMEM((groups, 2, 8, NX), F32),
            pltpu.VMEM((2, groups, 2, 8, NX), F32),
            pltpu.VMEM((groups, 2, 8, NX), F32),
            pltpu.VMEM((2, levels * 8, NX), F32),
            pltpu.VMEM((steps, 64, NX), F32),
            pltpu.VMEM((zs, LP, 8, NX), F32),
            pltpu.VMEM((zs, LP, 8, NX), F32),
            pltpu.VMEM((64 * 16, NX), F32),
            pltpu.VMEM((64 * 24, NX), F32),
            *[pltpu.VMEM((LP + 2, AP + 2, 16, NX), F32) for _ in range(SWEEPS)],
            *[pltpu.VMEM((LP + 2, AP, 16, NX), F32) for _ in range(SWEEPS)],
            pltpu.VMEM((32 * 16, NX), F32),
            pltpu.VMEM((SWEEPS, GROUPS, 8, NX), F32),
            pltpu.VMEM((SWEEPS, GROUPS, 2, 8, NX), F32),
            pltpu.VMEM((steps, 64, NX), F32),
            pltpu.VMEM((steps, 64, NX), F32),
            dma((5,)),
            dma((zs,)),
            dma((zs,)),
            dma((6,)),
            dma((6,)),
            dma((zs,)),
            dma((zs,)),
            dma((zs,)),
            dma((zs,)),
            dma((steps,)),
            dma((steps,)),
            dma((SWEEPS, 2)),
            dma((SWEEPS, 2)),
            dma((SWEEPS, GROUPS, 2)),
            dma((SWEEPS, GROUPS, 2)),
            dma((SWEEPS, GROUPS, 2)),
            dma((SWEEPS, GROUPS, 2)),
            dma((steps,)),
            dma((steps,)),
        ],
        compiler_params=pltpu.CompilerParams(
            collective_id=0, has_side_effects=True, vmem_limit_bytes=VMEM_LIMIT
        ),
    )(*(
        pltpu.with_memory_space_constraint(value, pltpu.HBM)
        for value in (
            flat(iterate), iterate.reshape(levels, 2, AP, NX), flat(heating), flat(region), flat(initial), cond_table
        )
    ))
    return out.reshape(iterate.shape)


def solution(mesh):
    sizes = mesh.shape
    return jax.shard_map(
        functools.partial(on_device, sizes["tm"], sizes["lat"], sizes["lon"]),
        mesh=mesh,
        in_specs=(
            P("tm", None, "lat", "lon"),
            P("tm", None, "lat", "lon"),
            P(None, "lat", "lon"),
            P(None, "lat", "lon"),
            P(),
        ),
        out_specs=P("tm", None, "lat", "lon"),
        check_vma=False,
    )
```
